32 devices in a mesh: groups: 2 (over x), pool: 8 (over z, y), head: 2 (over core).
Axes of the slice: x: 2, y: 2, z: 4, core: 2. Of those that a mesh axis runs over, the one named last changes fastest.
Arguments:
- queries: bfloat16 [2048, 32, 128], P(('groups', 'pool'), 'head'), parts along dimension 0, may hold values from -400 to 400
- new_kv: bfloat16 [2048, 2, 4, 128], P(('groups', 'pool'), None, 'head'), parts along dimension 0, may hold values from -4 to 4
- pool: bfloat16 [528, 2, 4, 128, 128], P(('groups', 'pool'), None, 'head'), parts along dimension 0, may hold values from -6 to 6
- block_table: int32 [8, 64], P('groups'), parts along dimension 0, may hold values from -1 to 263, as said below
- prefix_len: int32 [8], P('groups'), parts along dimension 0, may hold values from 2048 to 8192, as said below
- new_slots: int32 [16], P('groups'), parts along dimension 0, may hold values from 0 to 263, as said below
Outputs:
- attended: bfloat16 [2048, 32, 128], P(('groups', 'pool'), 'head'), parts along dimension 0
- updated_pool: bfloat16 [528, 2, 4, 128, 128], P(('groups', 'pool'), None, 'head'), parts along dimension 0
The draws below stay inside these ranges and needn't reach their ends.
There are 2 independent parts, one for each index of `groups`. The reference program is written for one: setup_inputs(seed, part) draws one part's arguments, and reference() takes and returns one part's arrays. A program takes and returns all parts, laid end to end along the dimension named above; each array names one. Nothing has to cross between parts.
Inputs may be any that keep to these rules, and one draw needn't show every extreme that they name: `block_table`: entry [r, j] is the slot (owner times 33 plus local slot) of page j of request r for j < ceil(prefix_len[r] / 128), and -1 after. All named slots differ. No owner holds more than 8 pages of one request, and the request with the longest prefix has exactly 8 on every owner. `prefix_len`: the longest prefix is exactly 8192 tokens. `new_slots`: entry d is a slot of owner d (d * 33 to (d + 1) * 33 - 1) that block_table does not name.
All inputs are finite; a program needn't handle non-finite values.
Results may differ from the reference program's by a relative error of at most 0.012.
Values may be sent and summed in bfloat16 or wider, within the bound.
No kernel may reach another device: no remote copies, remote signals or barrier semaphores. Data moves between devices by JAX's collectives and lax.ppermute only.
A program may use at most 128 MiB of HBM per device.

```python
import jax
import jax.numpy as jnp
from jax import lax

HD = 128
KVH = 4
GQ = 8
PAGE = 128
PMAX = 64
QH = 32
NEWTOK = 256
OWNERS = 8
REQS = 4
TOKENS = 1024
SLOTS = 33


def layout(key):
    folded = jax.random.fold_in(key, 7)
    subkeys = jax.random.split(folded, 5)
    lengths = jax.random.randint(subkeys[0], (REQS,), PMAX * PAGE // 4, PMAX * PAGE + 1)
    longest = jax.random.randint(subkeys[1], (), 0, REQS)
    request = jnp.arange(REQS)
    lengths = jnp.where(request == longest, PMAX * PAGE, lengths).astype(jnp.int32)
    page_count = (lengths + PAGE - 1) // PAGE
    starts = jnp.cumsum(page_count) - page_count
    used_total = jnp.sum(page_count)
    column = jnp.arange(PMAX)
    page_order = starts[:, None] + column[None, :]
    offset_owner = jax.random.randint(subkeys[2], (), 0, OWNERS)
    owner_perm = jax.random.permutation(subkeys[3], OWNERS)
    slot_perm = jax.random.permutation(subkeys[4], SLOTS)

    def placed(index):
        return owner_perm[(index + offset_owner) % OWNERS] * SLOTS + slot_perm[jnp.minimum(index // OWNERS, SLOTS - 1)]
    block_rows = jnp.where(column[None, :] < page_count[:, None], placed(page_order), -1).astype(jnp.int32)
    owner_ids = jnp.arange(OWNERS)
    inverse = jnp.argsort(owner_perm)
    rank = (inverse[owner_ids] - offset_owner) % OWNERS
    used_here = used_total // OWNERS + (rank < used_total % OWNERS).astype(jnp.int32)
    fresh = owner_ids * SLOTS + slot_perm[jnp.minimum(used_here, SLOTS - 1)]
    return (block_rows, lengths, fresh.astype(jnp.int32))


def token_draw(key):
    folded = jax.random.fold_in(key, 11)
    subkeys = jax.random.split(folded, 2)
    query_vals = jax.random.truncated_normal(subkeys[0], -4.0, 4.0, (TOKENS, QH, HD), jnp.float32)
    pair_vals = jax.random.truncated_normal(subkeys[1], -4.0, 4.0, (TOKENS, 2, KVH, HD), jnp.float32)
    return (query_vals, pair_vals)


def draw_queries(key, part):
    return token_draw(key)[0].astype(jnp.bfloat16)


def draw_new_kv(key, part):
    return token_draw(key)[1].astype(jnp.bfloat16)


def draw_block_table(key, part):
    return layout(key)[0]


def draw_prefix_len(key, part):
    return layout(key)[1]


def draw_new_slots(key, part):
    return layout(key)[2]


def block_scale(key, extent, pieces, least, top_value):
    loudness = 1.0
    for axis_at, blocks in pieces:
        steps = jax.random.uniform(jax.random.fold_in(jax.random.fold_in(key, 6), axis_at), (blocks,), jnp.float32, least / len(pieces), top_value / len(pieces))
        loudness = loudness * jnp.repeat(jnp.exp(steps), extent[axis_at] // blocks).reshape((-1,) + (1,) * (len(extent) - 1 - axis_at))
    return loudness


def normal_values(stream_key, dims, width, reach, shards=(), held_as=jnp.bfloat16):
    gain = block_scale(stream_key, dims, shards, -0.22, 0.18) if shards else 1.0
    drawn = jax.random.normal(stream_key, dims, jnp.float32) * width * gain
    return jnp.minimum(jnp.maximum(drawn, -reach), reach).astype(held_as)


def setup_inputs(seed: int = 0, part: int = 0) -> dict:
    arg_keys = jax.random.split(jax.random.key(seed), 7)
    own_keys = jax.random.split(jax.random.fold_in(arg_keys[6], part), 7)
    queries = draw_queries(jax.random.fold_in(jax.random.fold_in(arg_keys[6], part), 71), part)
    new_kv = draw_new_kv(jax.random.fold_in(jax.random.fold_in(arg_keys[6], part), 71), part)
    pool = normal_values(own_keys[2], (OWNERS * SLOTS, 2, KVH, PAGE, HD), 1.0, 6.0, ((0, 8), (2, 2)))
    block_table = draw_block_table(jax.random.fold_in(jax.random.fold_in(arg_keys[6], part), 71), part)
    prefix_len = draw_prefix_len(jax.random.fold_in(jax.random.fold_in(arg_keys[6], part), 71), part)
    new_slots = draw_new_slots(jax.random.fold_in(jax.random.fold_in(arg_keys[6], part), 71), part)
    return {"queries": queries, "new_kv": new_kv, "pool": pool, "block_table": block_table, "prefix_len": prefix_len, "new_slots": new_slots}


neg_big = -1e30


def one_request(request_id, queries, new_kv, pool, block_table, prefix_len):
    slot_ids = jnp.maximum(block_table[request_id], 0)
    pages = pool[slot_ids]
    prefix_keys = pages[:, 0].transpose(1, 0, 2, 3).reshape(KVH, PMAX * PAGE, HD)
    prefix_vals = pages[:, 1].transpose(1, 0, 2, 3).reshape(KVH, PMAX * PAGE, HD)
    start = (request_id * NEWTOK).astype(jnp.int32)
    swapped = ((1 - request_id % 2) * PAGE).astype(jnp.int32)
    recent = jnp.roll(lax.dynamic_slice_in_dim(new_kv, start, NEWTOK, 0), swapped, axis=0)
    all_keys = jnp.concatenate([prefix_keys, recent[:, 0].transpose(1, 0, 2)], axis=1)
    all_vals = jnp.concatenate([prefix_vals, recent[:, 1].transpose(1, 0, 2)], axis=1)
    query_block = jnp.roll(lax.dynamic_slice_in_dim(queries, start, NEWTOK, 0), swapped, axis=0).reshape(NEWTOK, KVH, GQ, HD)
    scores = jnp.einsum("tkgd,knd->kgtn", query_block.astype(jnp.float32), all_keys.astype(jnp.float32)) * HD ** -0.5
    position = jnp.arange(PMAX * PAGE, dtype=jnp.int32)
    prefix_mask = jnp.broadcast_to(position[None, :] < prefix_len[request_id], (NEWTOK, PMAX * PAGE))
    token_pos = jnp.arange(NEWTOK, dtype=jnp.int32)
    causal = token_pos[None, :] <= token_pos[:, None]
    allowed = jnp.concatenate([prefix_mask, causal], axis=1)[None, None]
    scores = jnp.where(allowed, scores, neg_big)
    row_max = jnp.max(scores, axis=-1, keepdims=True)
    weights = jnp.where(allowed, jnp.exp(scores - row_max), 0.0)
    row_total = jnp.sum(weights, axis=-1)
    rounded = weights.astype(jnp.bfloat16).astype(jnp.float32)
    mixed = jnp.einsum("kgtn,knd->kgtd", rounded, all_vals.astype(jnp.float32)) / row_total[..., None]
    logical = mixed.transpose(2, 0, 1, 3).reshape(NEWTOK, QH, HD).astype(jnp.bfloat16)
    return jnp.roll(logical, swapped, axis=0)


def reference(queries, new_kv, pool, block_table, prefix_len, new_slots):
    outputs = lax.map(lambda request_id: one_request(request_id, queries, new_kv, pool, block_table, prefix_len), jnp.arange(REQS, dtype=jnp.int32))
    attended = outputs.reshape(TOKENS, QH, HD)
    new_pages = new_kv.reshape(2 * REQS, PAGE, 2, KVH, HD).transpose(0, 2, 3, 1, 4)
    updated_pool = pool.at[new_slots].set(new_pages)
    return attended, updated_pool
```

```python
import functools

import jax
import jax.numpy as jnp
from jax import lax
from jax.experimental import pallas as pl
from jax.experimental.pallas import tpu as pltpu
from jax.sharding import PartitionSpec as P

log2_e = 1.4426950408889634
hidden_score = -2e30
lowest_top = -1e30
lanes = 128
block_rows = 128


def moved(array, apart):
    count = lax.axis_size("pool")
    return lax.ppermute(array, "pool", [(i, i ^ apart) for i in range(count)])


def whole(array):
    return pl.BlockSpec(array.shape, lambda i, *_: (0,) * len(array.shape))


def diagonal():
    shape = (lanes, lanes)
    return lax.broadcasted_iota(jnp.int32, shape, 0) == lax.broadcasted_iota(jnp.int32, shape, 1)


def as_row(column, eye):
    spread = jnp.where(eye, jnp.broadcast_to(column, (lanes, lanes)), 0.0)
    return jnp.sum(spread, axis=0, keepdims=True)


def as_column(row, eye):
    spread = jnp.where(eye, jnp.broadcast_to(row, (lanes, lanes)), 0.0)
    return jnp.sum(spread, axis=1, keepdims=True)


def in_three(values):
    high = values.astype(jnp.bfloat16)
    rest = values - high.astype(jnp.float32)
    middle = rest.astype(jnp.bfloat16)
    low = (rest - middle.astype(jnp.float32)).astype(jnp.bfloat16)
    return (high, middle, low)


def from_three(ref, begin, count):
    parts = [
        ref[begin + i * count : begin + (i + 1) * count].astype(jnp.float32) for i in range(3)
    ]
    return parts[0] + parts[1] + parts[2]


def gather_body(owner_ref, table_ref, pool_ref, *refs, lists, kv_heads, cap):
    outs = refs[:-2]
    slots, sem = refs[-2:]
    owner = owner_ref[0]
    pair = owner // 2
    slot_count = pool_ref.shape[0]
    base = owner * slot_count
    width = table_ref.shape[1]
    copies = []
    for at, which in enumerate(lists):
        request = pair ^ which
        begin = at * (cap + 1)

        def look(j, found):
            slot = table_ref[request, j] - base
            slots[begin + jnp.minimum(found, cap)] = slot
            held = (slot >= 0) & (slot < slot_count)
            return found + held.astype(jnp.int32)

        found = lax.fori_loop(0, width, look, jnp.int32(0), unroll=8)
        for i in range(cap):
            slot = jnp.where(i < found, slots[begin + i], 0)
            for k in range(kv_heads):
                copy = pltpu.make_async_copy(
                    pool_ref.at[slot, :, k], outs[at * kv_heads + k].at[i], sem.at[at, k, i]
                )
                copy.start()
                copies.append(copy)
    for copy in copies:
        copy.wait()


def gather_pages(owner, table, pool, lists, cap):
    slot_count, pair_of, kv_heads, page_len, head_dim = pool.shape
    shape = jax.ShapeDtypeStruct((cap, pair_of, page_len, head_dim), pool.dtype)
    count = len(lists) * kv_heads
    outs = pl.pallas_call(
        functools.partial(gather_body, lists=lists, kv_heads=kv_heads, cap=cap),
        out_shape=[shape] * count,
        grid_spec=pltpu.PrefetchScalarGridSpec(
            num_scalar_prefetch=2,
            grid=(1,),
            in_specs=[pl.BlockSpec(memory_space=pl.ANY)],
            out_specs=[pl.BlockSpec(memory_space=pl.ANY)] * count,
            scratch_shapes=[
                pltpu.SMEM((len(lists) * (cap + 1),), jnp.int32),
                pltpu.SemaphoreType.DMA((len(lists), kv_heads, cap)),
            ],
        ),
        name="gather_pages",
    )(owner, table, pool)
    return [outs[i * kv_heads : (i + 1) * kv_heads] for i in range(len(lists))]


def attend_body(info_ref, *refs, halves, source_count, has_page, has_prev, packed, step_rows, group, scale, copies_pool):
    refs = list(refs)
    q_refs = [refs.pop(0) for _ in range(halves)]
    kv_refs = [refs.pop(0) for _ in range(source_count)]
    page_ref = refs.pop(0) if has_page else None
    prev_refs = [(refs.pop(0), refs.pop(0)) for _ in range(halves)] if has_prev else None
    pool_refs = [refs.pop(0) for _ in range(2)] if copies_pool else None
    out_refs = []
    for h in range(halves):
        out_refs.append((refs.pop(0),) if packed[h] else (refs.pop(0), refs.pop(0)))
    new_pool = refs.pop(0) if copies_pool else None
    wide_values = refs.pop(0)
    tables = [refs.pop(0) if packed[h] else out_refs[h][1] for h in range(halves)]
    sem = refs.pop(0) if copies_pool else None
    step = pl.program_id(0)
    steps = pl.num_programs(0)
    keys = [ref.shape[0] * ref.shape[2] for ref in kv_refs]
    page_len = kv_refs[0].shape[2]

    def pool_copy(slot, source):
        return pltpu.make_async_copy(source, new_pool.at[slot], sem)

    if copies_pool:

        @pl.when(step == 0)
        def _():
            fresh = info_ref[source_count + 1]

            def start(slot, carry):
                @pl.when(slot == fresh)
                def _():
                    pool_copy(slot, pool_refs[1]).start()

                @pl.when(slot != fresh)
                def _():
                    pool_copy(slot, pool_refs[0].at[slot]).start()

                return carry

            lax.fori_loop(0, new_pool.shape[0], start, 0)

    @pl.when(step == 0)
    def _():
        ones = jnp.ones((page_len, lanes), jnp.bfloat16)
        begin = 0
        for ref in kv_refs:
            for p in range(ref.shape[0]):
                wide_values[begin : begin + page_len, :lanes] = ref[p, 1]
                wide_values[begin : begin + page_len, lanes:] = ones
                begin += page_len
        if has_page:
            wide_values[begin : begin + page_len, :lanes] = page_ref[1]
            wide_values[begin : begin + page_len, lanes:] = ones

    eye = diagonal()
    limits = []
    for s in range(source_count):
        position = lax.broadcasted_iota(jnp.int32, (1, keys[s]), 1)
        limit = jnp.where(position < info_ref[s], jnp.inf, hidden_score)
        limits.append(limit.astype(jnp.float32))
    for h in range(halves):
        for t in range(step_rows // block_rows):
            rows = slice(t * block_rows, (t + 1) * block_rows)
            query = q_refs[h][rows]
            scores = []
            for s in range(source_count):
                key_rows = kv_refs[s][:, 0].reshape(keys[s], lanes)
                product = lax.dot_general(
                    query, key_rows, (((1,), (1,)), ((), ())), preferred_element_type=jnp.float32
                )
                scores.append(jnp.minimum(product, limits[s]))
            if has_page:
                product = lax.dot_general(
                    query, page_ref[0], (((1,), (1,)), ((), ())), preferred_element_type=jnp.float32
                )
                key_at = lax.broadcasted_iota(jnp.int32, product.shape, 1)
                if h == 0:
                    row_at = lax.broadcasted_iota(jnp.int32, product.shape, 0)
                    token = (step * step_rows + t * block_rows + row_at) // group
                    seen = key_at <= token
                else:
                    seen = key_at < info_ref[source_count]
                scores.append(jnp.where(seen, product, hidden_score))
            top = jnp.full((block_rows, 1), lowest_top, jnp.float32)
            for part in scores:
                top = jnp.maximum(top, jnp.max(part, axis=1, keepdims=True))
            scaled_top = top * scale
            mixed = None
            begin = 0
            for part in scores:
                weights = jnp.exp2(part * scale - scaled_top).astype(jnp.bfloat16)
                values = wide_values[begin : begin + part.shape[1]]
                begin += part.shape[1]
                product = jnp.dot(weights, values, preferred_element_type=jnp.float32)
                mixed = product if mixed is None else mixed + product
            total = mixed[:, lanes : lanes + 1]
            mixed = mixed[:, :lanes]
            row = step * (step_rows // block_rows) + t
            count = tables[h].shape[0] // 2
            if has_prev:
                prev_mixed, prev_table = prev_refs[h]
                prev_top = as_column(prev_table[pl.ds(row, 1)], eye)
                prev_total = as_column(prev_table[pl.ds(count + row, 1)], eye)
                joint = jnp.maximum(top, prev_top)
                keep = jnp.exp2((top - joint) * scale)
                keep_prev = jnp.exp2((prev_top - joint) * scale)
                mixed = mixed * keep + prev_mixed[rows] * keep_prev
                total = total * keep + prev_total * keep_prev
                top = joint
            tables[h][pl.ds(row, 1)] = as_row(top, eye)
            tables[h][pl.ds(count + row, 1)] = as_row(total, eye)
            if packed[h]:
                at = pl.multiple_of(row * block_rows, block_rows)
                out_refs[h][0][pl.ds(at, block_rows)] = mixed.astype(jnp.bfloat16)
            else:
                out_refs[h][0][rows] = mixed

    @pl.when(step == steps - 1)
    def _():
        for h in range(halves):
            if packed[h]:
                size = tables[h].shape[0]
                begin = out_refs[h][0].shape[0] - 3 * size
                for i, part in enumerate(in_three(tables[h][...])):
                    out_refs[h][0][begin + i * size : begin + (i + 1) * size] = part
        if copies_pool:
            pltpu.make_async_copy(pool_refs[0], new_pool, sem).wait()


def attend(info, queries, sources, packed, scale, group, page=None, prev=None, pool=None):
    halves = len(queries)
    rows = queries[0].shape[0]
    size = 2 * (rows // block_rows)
    step_rows = min(rows, 512 // halves)
    key_count = sum(s.shape[0] * s.shape[2] for s in sources)
    by_rows = pl.BlockSpec((step_rows, lanes), lambda i, *_: (i, 0))
    anywhere = pl.BlockSpec(memory_space=pl.ANY)
    args = list(queries) + list(sources)
    in_specs = [by_rows] * halves + [whole(s) for s in sources]
    if page is not None:
        args.append(page)
        in_specs.append(whole(page))
        key_count += page.shape[1]
    if prev is not None:
        for mixed, table in prev:
            args += [mixed, table]
            in_specs += [by_rows, whole(table)]
    if pool is not None:
        args += list(pool)
        in_specs += [anywhere, anywhere]
    out_shape = []
    out_specs = []
    scratch = [pltpu.VMEM((key_count, 2 * lanes), jnp.bfloat16)]
    table_spec = pl.BlockSpec((size, lanes), lambda i, *_: (0, 0))
    for h in range(halves):
        if packed[h]:
            full_rows = rows + 3 * size
            out_shape.append(jax.ShapeDtypeStruct((full_rows, lanes), jnp.bfloat16))
            out_specs.append(pl.BlockSpec((full_rows, lanes), lambda i, *_: (0, 0)))
            scratch.append(pltpu.VMEM((size, lanes), jnp.float32))
        else:
            out_shape.append(jax.ShapeDtypeStruct((rows, lanes), jnp.float32))
            out_shape.append(jax.ShapeDtypeStruct((size, lanes), jnp.float32))
            out_specs += [by_rows, table_spec]
    if pool is not None:
        out_shape.append(jax.ShapeDtypeStruct(pool[0].shape, pool[0].dtype))
        out_specs.append(anywhere)
        scratch.append(pltpu.SemaphoreType.DMA)
    flops = 4 * halves * rows * key_count * lanes
    return pl.pallas_call(
        functools.partial(
            attend_body,
            halves=halves,
            source_count=len(sources),
            has_page=page is not None,
            has_prev=prev is not None,
            packed=packed,
            step_rows=step_rows,
            group=group,
            scale=scale,
            copies_pool=pool is not None,
        ),
        out_shape=out_shape,
        grid_spec=pltpu.PrefetchScalarGridSpec(
            num_scalar_prefetch=1,
            grid=(rows // step_rows,),
            in_specs=in_specs,
            out_specs=out_specs,
            scratch_shapes=scratch,
        ),
        cost_estimate=pl.CostEstimate(
            flops=flops, transcendentals=halves * rows * key_count, bytes_accessed=4 * key_count * lanes
        ),
        name="attend",
    )(info, *args)


def join_body(own_mixed, own_table, *refs, scale, packs, aliased):
    refs = list(refs)
    out_ref = refs.pop()
    if aliased:
        refs.pop()
    size = own_table.shape[0]
    count = size // 2
    rows = count * block_rows
    eye = diagonal()
    tops = [own_table[:count]]
    totals = [own_table[count:]]
    for ref in refs:
        table = from_three(ref, rows, size)
        tops.append(table[:count])
        totals.append(table[count:])
    top = functools.reduce(jnp.maximum, tops)
    keeps = [jnp.exp2((t - top) * scale) for t in tops]
    total = sum(t * keep for t, keep in zip(totals, keeps))
    if not packs:
        keeps = [keep / total for keep in keeps]
    for t in range(count):
        at = slice(t * block_rows, (t + 1) * block_rows)
        mixed = own_mixed[at] * as_column(keeps[0][t : t + 1], eye)
        for ref, keep in zip(refs, keeps[1:]):
            mixed = mixed + ref[at].astype(jnp.float32) * as_column(keep[t : t + 1], eye)
        if packs:
            out_ref[at] = mixed.astype(jnp.bfloat16)
        else:
            heads = out_ref.shape[1]
            tokens = block_rows // heads
            shaped = mixed.reshape(tokens, heads, lanes)
            out_ref[t * tokens : (t + 1) * tokens] = shaped.astype(jnp.bfloat16)
    if packs:
        table = jnp.concatenate([top, total], axis=0)
        for i, part in enumerate(in_three(table)):
            out_ref[rows + i * size : rows + (i + 1) * size] = part


def join_packed(own, received, scale):
    mixed, table = own
    return pl.pallas_call(
        functools.partial(join_body, scale=scale, packs=True, aliased=False),
        out_shape=jax.ShapeDtypeStruct(received.shape, received.dtype),
        grid=(1,),
        in_specs=[whole(mixed), whole(table), whole(received)],
        out_specs=whole(received),
        name="join_packed",
    )(mixed, table, received)


def join_out(own, received, target, shape, index, group, scale):
    mixed, table = own
    args = [mixed, table, *received]
    in_specs = [whole(a) for a in args]
    aliases = {}
    if target is not None:
        aliases = {len(args): 0}
        args.append(target)
        in_specs.append(pl.BlockSpec(memory_space=pl.ANY))
    return pl.pallas_call(
        functools.partial(join_body, scale=scale, packs=False, aliased=target is not None),
        out_shape=jax.ShapeDtypeStruct(shape, jnp.bfloat16),
        grid=(1,),
        in_specs=in_specs,
        out_specs=pl.BlockSpec((shape[0], group, shape[2]), lambda i: (0, index, 0)),
        input_output_aliases=aliases,
        name="join_out",
    )(*args)


def visible_counts(table, lengths, owner, steps, slot_count, page_len):
    requests, width = table.shape
    pair = owner // 2
    holders = owner ^ (2 * jnp.arange(steps, dtype=jnp.int32))
    chosen = pair ^ (jnp.arange(2, dtype=jnp.int32) * steps)
    column = jnp.arange(width, dtype=jnp.int32)
    count = jnp.clip(lengths[:, None] - column[None, :] * page_len, 0, page_len)
    first = holders[None, :, None, None] * slot_count
    entry = table[None, None]
    held = (entry >= first) & (entry < first + slot_count)
    asked = jnp.arange(requests, dtype=jnp.int32)[None, :] == chosen[:, None]
    picked = held & asked[:, None, :, None]
    return jnp.sum(jnp.where(picked, count[None, None], 0), axis=(2, 3))


def on_device(queries, new_kv, pool, block_table, prefix_len, new_slots):
    owner_count = lax.axis_size("pool")
    owner = lax.axis_index("pool").astype(jnp.int32)
    half = 1 - ((owner % 2) ^ (owner // 2 % 2))
    slot_count, _, kv_heads, page_len, head_dim = pool.shape
    tokens, q_heads, _ = queries.shape
    group = q_heads // kv_heads
    rows = tokens * group
    pairs = owner_count // 2
    near = pairs // 2
    cap = block_table.shape[1] // owner_count
    scale = head_dim**-0.5 * log2_e

    split = [
        queries[:, k * group : (k + 1) * group].reshape(rows, head_dim) for k in range(kv_heads)
    ]
    far_own = [moved(q, pairs) for q in split]
    other = [moved(q, 1) for q in split]
    owner_list = jnp.full((1,), owner, jnp.int32)
    sent_far = gather_pages(owner_list, block_table, pool, [near + k for k in range(1, near)], cap)
    got_far = [
        [moved(sent_far[i][k], 2 * (i + 1)) for i in range(near - 1)] for k in range(kv_heads)
    ]
    kept = gather_pages(owner_list, block_table, pool, [0, near] + list(range(1, near)), cap)
    local, local_far, sent_near = kept[0], kept[1], kept[2:]
    got_near = [
        [moved(sent_near[i][k], 2 * (i + 1)) for i in range(near - 1)] for k in range(kv_heads)
    ]
    seen = visible_counts(block_table, prefix_len, owner, near, slot_count, page_len)
    own_slot = lax.dynamic_index_in_dim(new_slots, owner, 0, keepdims=False) - owner * slot_count
    page_seen = jnp.where(half == 0, page_len, 0)
    new_page = new_kv.transpose(1, 2, 0, 3)
    local_info = jnp.concatenate([seen[0, :1], jnp.stack([page_seen, own_slot])]).astype(jnp.int32)

    started = []
    updated = None
    for k in range(kv_heads):
        results = attend(
            local_info,
            [split[k], other[k]],
            [local[k]],
            (False, False),
            scale,
            group,
            page=new_page[:, k],
            pool=(pool, new_page) if k == 0 else None,
        )
        if k == 0:
            updated = results[4]
        started.append(((results[0], results[1]), (results[2], results[3])))

    far_other = [moved(q, 1) for q in far_own]
    back = []
    for k in range(kv_heads):
        keys = [local_far[k]] + got_far[k]
        own_far = attend(seen[1], [far_own[k]], keys, (False,), scale, group)
        (other_far,) = attend(seen[1], [far_other[k]], keys, (True,), scale, group)
        joined = join_packed(own_far, moved(other_far, 1), scale)
        back.append(moved(joined, pairs))
    attended = None
    for k in range(kv_heads):
        mine, theirs = started[k]
        (other_part,) = attend(seen[0, 1:], [other[k]], got_near[k], (True,), scale, group, prev=[theirs])
        own_part = attend(seen[0, 1:], [split[k]], got_near[k], (False,), scale, group, prev=[mine])
        attended = join_out(
            own_part, [moved(other_part, 1), back[k]], attended, queries.shape, k, group, scale
        )
    return (attended, updated)


def solution(mesh):
    placed = (
        P(("groups", "pool"), "head", None),
        P(("groups", "pool"), None, "head", None),
        P(("groups", "pool"), None, "head", None, None),
        P("groups", None),
        P("groups"),
        P("groups"),
    )
    return jax.shard_map(
        on_device,
        mesh=mesh,
        in_specs=placed,
        out_specs=(
            P(("groups", "pool"), "head", None),
            P(("groups", "pool"), None, "head", None, None),
        ),
        check_vma=False,
    )
```

```python
import functools

import jax
import jax.numpy as jnp
from jax import lax
from jax.experimental import pallas as pl
from jax.experimental.pallas import tpu as pltpu
from jax.sharding import PartitionSpec as P

log2_e = 1.4426950408889634
hidden_score = -2e30
lowest_top = -1e30
lanes = 128
block_rows = 128


def moved(array, apart):
    count = lax.axis_size("pool")
    return lax.ppermute(array, "pool", [(i, i ^ apart) for i in range(count)])


def whole(array):
    return pl.BlockSpec(array.shape, lambda i, *_: (0,) * len(array.shape))


def diagonal():
    shape = (lanes, lanes)
    return lax.broadcasted_iota(jnp.int32, shape, 0) == lax.broadcasted_iota(jnp.int32, shape, 1)


def as_row(column, eye):
    spread = jnp.where(eye, jnp.broadcast_to(column, (lanes, lanes)), 0.0)
    return jnp.sum(spread, axis=0, keepdims=True)


def as_column(row, eye):
    spread = jnp.where(eye, jnp.broadcast_to(row, (lanes, lanes)), 0.0)
    return jnp.sum(spread, axis=1, keepdims=True)


def in_three(values):
    high = values.astype(jnp.bfloat16)
    rest = values - high.astype(jnp.float32)
    middle = rest.astype(jnp.bfloat16)
    low = (rest - middle.astype(jnp.float32)).astype(jnp.bfloat16)
    return (high, middle, low)


def from_three(ref, begin, count):
    parts = [
        ref[0, begin + i * count : begin + (i + 1) * count].astype(jnp.float32) for i in range(3)
    ]
    return parts[0] + parts[1] + parts[2]


def gather_body(owner_ref, table_ref, pool_ref, *refs, lists, kv_heads, cap):
    outs = refs[:-2]
    slots, sem = refs[-2:]
    owner = owner_ref[0]
    pair = owner >> 1
    slot_count = pool_ref.shape[0]
    base = owner * slot_count
    width = table_ref.shape[1]
    copies = []
    for at, which in enumerate(lists):
        request = pair ^ which
        begin = at * (cap + 1)

        def look(j, found):
            slot = table_ref[request, j] - base
            slots[begin + jnp.minimum(found, cap)] = slot
            held = (slot >= 0) & (slot < slot_count)
            return found + held.astype(jnp.int32)

        found = lax.fori_loop(0, width, look, jnp.int32(0), unroll=8)
        for i in range(cap):
            slot = jnp.where(i < found, slots[begin + i], 0)
            for k in range(kv_heads):
                copy = pltpu.make_async_copy(
                    pool_ref.at[slot, :, k], outs[at * kv_heads + k].at[0, i], sem.at[at, k, i]
                )
                copy.start()
                copies.append(copy)
    for copy in copies:
        copy.wait()


def gather_pages(owner, table, pool, lists, cap):
    slot_count, pair_of, kv_heads, page_len, head_dim = pool.shape
    shape = jax.ShapeDtypeStruct((1, cap, pair_of, page_len, head_dim), pool.dtype)
    count = len(lists) * kv_heads
    outs = pl.pallas_call(
        functools.partial(gather_body, lists=lists, kv_heads=kv_heads, cap=cap),
        out_shape=[shape] * count,
        grid_spec=pltpu.PrefetchScalarGridSpec(
            num_scalar_prefetch=2,
            grid=(1,),
            in_specs=[pl.BlockSpec(memory_space=pl.ANY)],
            out_specs=[whole(shape)] * count,
            scratch_shapes=[
                pltpu.SMEM((len(lists) * (cap + 1),), jnp.int32),
                pltpu.SemaphoreType.DMA((len(lists), kv_heads, cap)),
            ],
        ),
        name="gather_pages",
    )(owner, table, pool)
    return [outs[i * kv_heads : (i + 1) * kv_heads] for i in range(len(lists))]


def attend_body(
    owner_ref,
    seen_ref,
    fresh_ref,
    *refs,
    halves,
    seen_at,
    has_page,
    has_prev,
    packed,
    step_rows,
    tile_rows,
    group,
    scale,
    copies_pool,
    waits,
    page_at,
):
    refs = list(refs)
    q_refs = [refs.pop(0) for _ in range(halves)]
    kv_refs = [refs.pop(0) for _ in seen_at]
    page_ref = refs.pop(0) if has_page else None
    prev_refs = [(refs.pop(0), refs.pop(0)) for _ in range(halves)] if has_prev else None
    pool_ref = refs.pop(0) if copies_pool else None
    del refs[:waits]
    out_refs = []
    for h in range(halves):
        out_refs.append((refs.pop(0),) if packed[h] else (refs.pop(0), refs.pop(0)))
    new_pool = refs.pop(0) if copies_pool else None
    wide_values = refs.pop(0)
    tables = [refs.pop(0) if packed[h] else out_refs[h][1].at[0] for h in range(halves)]
    if copies_pool:
        staged, sem_in, sem_out = refs
    head = pl.program_id(0)
    step = pl.program_id(1)
    heads = pl.num_programs(0)
    steps = pl.num_programs(1)
    owner = owner_ref[0]
    half = 1 - ((owner & 1) ^ ((owner >> 1) & 1))
    page_len = kv_refs[0].shape[3]
    keys = [ref.shape[1] * page_len for ref in kv_refs]

    if copies_pool:

        @pl.when((head == 0) & (step == 0))
        def _():
            pltpu.make_async_copy(pool_ref, staged, sem_in).start()

        @pl.when((head == 0) & (step == jnp.minimum(1, steps - 1)))
        def _():
            pltpu.make_async_copy(pool_ref, staged, sem_in).wait()
            staged[fresh_ref[owner] - owner * staged.shape[0]] = page_ref[...]
            pltpu.make_async_copy(staged, new_pool, sem_out).start()

    @pl.when(step == 0)
    def _():
        ones = jnp.ones((page_len, lanes), jnp.bfloat16)
        begin = 0
        for ref in kv_refs:
            for p in range(ref.shape[1]):
                wide_values[begin : begin + page_len, :lanes] = ref[0, p, 1]
                wide_values[begin : begin + page_len, lanes:] = ones
                begin += page_len
        if has_page:
            wide_values[begin : begin + page_len, :lanes] = page_ref[1, page_at]
            wide_values[begin : begin + page_len, lanes:] = ones

    eye = diagonal()
    limits = []
    for s, at in enumerate(seen_at):
        position = lax.broadcasted_iota(jnp.int32, (1, keys[s]), 1)
        limit = jnp.where(position < seen_ref[at[0], at[1]], jnp.inf, hidden_score)
        limits.append(limit.astype(jnp.float32))

    def score(h, t):
        query = q_refs[h][0, t * tile_rows : (t + 1) * tile_rows]
        scores = []
        for s, ref in enumerate(kv_refs):
            key_rows = ref[0, :, 0].reshape(keys[s], lanes)
            product = lax.dot_general(
                query, key_rows, (((1,), (1,)), ((), ())), preferred_element_type=jnp.float32
            )
            scores.append(jnp.minimum(product, limits[s]))
        if has_page:
            product = lax.dot_general(
                query, page_ref[0, page_at], (((1,), (1,)), ((), ())), preferred_element_type=jnp.float32
            )
            key_at = lax.broadcasted_iota(jnp.int32, product.shape, 1)
            if h == 0:
                row_at = lax.broadcasted_iota(jnp.int32, product.shape, 0)
                token = (step * step_rows + t * tile_rows + row_at) // group
                shown = key_at <= token
            else:
                shown = key_at < jnp.where(half == 0, page_len, 0)
            scores.append(jnp.where(shown, product, hidden_score))
        return scores

    def finish(h, t, scores):
        rows = slice(t * tile_rows, (t + 1) * tile_rows)
        top = jnp.full((tile_rows, 1), lowest_top, jnp.float32)
        for part in scores:
            top = jnp.maximum(top, jnp.max(part, axis=1, keepdims=True))
        scaled_top = top * scale
        weights = [jnp.exp2(part * scale - scaled_top).astype(jnp.bfloat16) for part in scores]
        mixed = jnp.dot(
            jnp.concatenate(weights, axis=1), wide_values[...], preferred_element_type=jnp.float32
        )
        total = mixed[:, lanes:]
        mixed = mixed[:, :lanes]
        first = step * (step_rows // block_rows) + t * (tile_rows // block_rows)
        count = tables[h].shape[0] // 2
        for u in range(tile_rows // block_rows):
            inner = slice(u * block_rows, (u + 1) * block_rows)
            outer = slice(t * tile_rows + u * block_rows, t * tile_rows + (u + 1) * block_rows)
            part_top, part_total, part_mixed = top[inner], total[inner], mixed[inner]
            row = first + u
            if has_prev:
                prev_mixed, prev_table = prev_refs[h]
                prev_top = as_column(prev_table[0, pl.ds(row, 1)], eye)
                prev_total = as_column(prev_table[0, pl.ds(count + row, 1)], eye)
                joint = jnp.maximum(part_top, prev_top)
                keep = jnp.exp2((part_top - joint) * scale)
                keep_prev = jnp.exp2((prev_top - joint) * scale)
                part_mixed = part_mixed * keep + prev_mixed[0, outer] * keep_prev
                part_total = part_total * keep + prev_total * keep_prev
                part_top = joint
            tables[h][pl.ds(row, 1)] = as_row(part_top, eye)
            tables[h][pl.ds(count + row, 1)] = as_row(part_total, eye)
            if packed[h]:
                at = pl.multiple_of(row * block_rows, block_rows)
                out_refs[h][0][0, pl.ds(at, block_rows)] = part_mixed.astype(jnp.bfloat16)
            else:
                out_refs[h][0][0, outer] = part_mixed

    chains = [(h, t) for t in range(step_rows // tile_rows) for h in range(halves)]
    scores = score(*chains[0])
    for i, chain in enumerate(chains):
        following = score(*chains[i + 1]) if i + 1 < len(chains) else None
        finish(*chain, scores)
        scores = following

    @pl.when(step == steps - 1)
    def _():
        for h in range(halves):
            if packed[h]:
                size = tables[h].shape[0]
                begin = out_refs[h][0].shape[1] - 3 * size
                for i, part in enumerate(in_three(tables[h][...])):
                    out_refs[h][0][0, begin + i * size : begin + (i + 1) * size] = part

    if copies_pool:

        @pl.when((head == heads - 1) & (step == steps - 1))
        def _():
            pltpu.make_async_copy(staged, new_pool, sem_out).wait()


def attend(
    scalars, queries, sources, seen_at, packed, scale, group, heads, page=None, prev=None, pool=None, after=()
):
    halves = len(queries)
    rows = queries[0][0].shape[1]
    size = 2 * (rows // block_rows)
    step_rows = min(rows, 1024 // halves)
    tile_rows = min(step_rows, 256)
    key_count = sum(s.shape[1] * s.shape[3] for s, _ in sources)

    def per_rows(offset):
        return pl.BlockSpec((1, step_rows, lanes), lambda k, i, *_: (k + offset, i, 0))

    def per_head(array, offset):
        tail = array.shape[1:]
        return pl.BlockSpec((1, *tail), lambda k, i, *_: (k + offset,) + (0,) * len(tail))

    anywhere = pl.BlockSpec(memory_space=pl.ANY)
    args = [q for q, _ in queries] + [s for s, _ in sources]
    in_specs = [per_rows(at) for _, at in queries] + [per_head(s, at) for s, at in sources]
    page_at = 0
    if page is not None:
        page, page_at = page
        args.append(page)
        in_specs.append(whole(page))
        key_count += page.shape[2]
    if prev is not None:
        for mixed, table, at in prev:
            args += [mixed, table]
            in_specs += [per_rows(at), per_head(table, at)]
    if pool is not None:
        args.append(pool)
        in_specs.append(anywhere)
    args += list(after)
    in_specs += [anywhere] * len(after)
    out_shape = []
    out_specs = []
    scratch = [pltpu.VMEM((key_count, 2 * lanes), jnp.bfloat16)]
    for h in range(halves):
        if packed[h]:
            shape = jax.ShapeDtypeStruct((heads, rows + 3 * size, lanes), jnp.bfloat16)
            out_shape.append(shape)
            out_specs.append(per_head(shape, 0))
            scratch.append(pltpu.VMEM((size, lanes), jnp.float32))
        else:
            table = jax.ShapeDtypeStruct((heads, size, lanes), jnp.float32)
            out_shape += [jax.ShapeDtypeStruct((heads, rows, lanes), jnp.float32), table]
            out_specs += [per_rows(0), per_head(table, 0)]
    if pool is not None:
        out_shape.append(jax.ShapeDtypeStruct(pool.shape, pool.dtype))
        out_specs.append(anywhere)
        scratch.append(pltpu.VMEM(pool.shape, pool.dtype))
        scratch += [pltpu.SemaphoreType.DMA, pltpu.SemaphoreType.DMA]
    work = halves * heads * rows * key_count
    return pl.pallas_call(
        functools.partial(
            attend_body,
            halves=halves,
            seen_at=seen_at,
            has_page=page is not None,
            has_prev=prev is not None,
            packed=packed,
            step_rows=step_rows,
            tile_rows=tile_rows,
            group=group,
            scale=scale,
            copies_pool=pool is not None,
            waits=len(after),
            page_at=page_at,
        ),
        out_shape=out_shape,
        grid_spec=pltpu.PrefetchScalarGridSpec(
            num_scalar_prefetch=3,
            grid=(heads, rows // step_rows),
            in_specs=in_specs,
            out_specs=out_specs,
            scratch_shapes=scratch,
        ),
        cost_estimate=pl.CostEstimate(
            flops=4 * work * lanes,
            transcendentals=work,
            bytes_accessed=4 * heads * key_count * lanes,
        ),
        name="attend",
    )(*scalars, *args)


def join_body(own_mixed, own_table, *refs, scale, packs, waits):
    refs = list(refs)
    out_ref = refs.pop()
    if waits:
        del refs[-waits:]
    size = own_table.shape[1]
    count = size // 2
    rows = count * block_rows
    eye = diagonal()
    tops = [own_table[0, :count]]
    totals = [own_table[0, count:]]
    for ref in refs:
        table = from_three(ref, rows, size)
        tops.append(table[:count])
        totals.append(table[count:])
    top = functools.reduce(jnp.maximum, tops)
    keeps = [jnp.exp2((t - top) * scale) for t in tops]
    total = sum(t * keep for t, keep in zip(totals, keeps))
    if not packs:
        keeps = [keep / total for keep in keeps]
    for t in range(count):
        at = slice(t * block_rows, (t + 1) * block_rows)
        mixed = own_mixed[0, at] * as_column(keeps[0][t : t + 1], eye)
        for ref, keep in zip(refs, keeps[1:]):
            mixed = mixed + ref[0, at].astype(jnp.float32) * as_column(keep[t : t + 1], eye)
        if packs:
            out_ref[0, at] = mixed.astype(jnp.bfloat16)
        else:
            heads = out_ref.shape[1]
            tokens = block_rows // heads
            shaped = mixed.reshape(tokens, heads, lanes)
            out_ref[t * tokens : (t + 1) * tokens] = shaped.astype(jnp.bfloat16)
    if packs:
        table = jnp.concatenate([top, total], axis=0)
        for i, part in enumerate(in_three(table)):
            out_ref[0, rows + i * size : rows + (i + 1) * size] = part


def join_packed(own, received, scale, after=()):
    mixed, table = own
    args = [mixed, table, received]
    return pl.pallas_call(
        functools.partial(join_body, scale=scale, packs=True, waits=len(after)),
        out_shape=jax.ShapeDtypeStruct(received.shape, received.dtype),
        grid=(1,),
        in_specs=[whole(a) for a in args] + [pl.BlockSpec(memory_space=pl.ANY)] * len(after),
        out_specs=whole(received),
        name="join_packed",
    )(*args, *after)


def join_out(own, received, target, shape, index, group, scale):
    mixed, table = own
    args = [mixed, table, *received]
    in_specs = [whole(a) for a in args]
    aliases = {}
    if target is not None:
        aliases = {len(args): 0}
        args.append(target)
        in_specs.append(pl.BlockSpec(memory_space=pl.ANY))
    return pl.pallas_call(
        functools.partial(join_body, scale=scale, packs=False, waits=len(aliases)),
        out_shape=jax.ShapeDtypeStruct(shape, jnp.bfloat16),
        grid=(1,),
        in_specs=in_specs,
        out_specs=pl.BlockSpec((shape[0], group, shape[2]), lambda i: (0, index, 0)),
        input_output_aliases=aliases,
        name="join_out",
    )(*args)


def visible_counts(table, lengths, owner, steps, slot_count, page_len):
    requests, width = table.shape
    holders = owner ^ (2 * jnp.arange(steps, dtype=jnp.int32))
    chosen = (owner >> 1) ^ (jnp.arange(2, dtype=jnp.int32) * steps)
    column = jnp.arange(width, dtype=jnp.int32)
    count = jnp.clip(lengths[:, None] - column[None, :] * page_len, 0, page_len)
    first = holders[None, :, None, None] * slot_count
    entry = table[None, None]
    held = (entry >= first) & (entry < first + slot_count)
    asked = jnp.arange(requests, dtype=jnp.int32)[None, :] == chosen[:, None]
    picked = held & asked[:, None, :, None]
    return jnp.sum(jnp.where(picked, count[None, None], 0), axis=(2, 3))


def on_device(queries, new_kv, pool, block_table, prefix_len, new_slots):
    owner_count = lax.axis_size("pool")
    owner = lax.axis_index("pool").astype(jnp.int32)
    slot_count, _, kv_heads, page_len, head_dim = pool.shape
    tokens, q_heads, _ = queries.shape
    group = q_heads // kv_heads
    rows = tokens * group
    pairs = owner_count // 2
    near = pairs // 2
    cap = block_table.shape[1] // owner_count
    scale = head_dim**-0.5 * log2_e
    each = range(kv_heads)

    split = [
        queries[:, k * group : (k + 1) * group].reshape(1, rows, head_dim) for k in each
    ]
    stacked = jnp.concatenate(split, axis=0)
    far_own = [moved(q, pairs) for q in split]
    other = moved(stacked, 1)
    owner_list = jnp.full((1,), owner, jnp.int32)
    sent_far = gather_pages(owner_list, block_table, pool, [near + k for k in range(1, near)], cap)
    got_far = [[moved(sent_far[i][k], 2 * (i + 1)) for i in range(near - 1)] for k in each]
    sent_near = gather_pages(owner_list, block_table, pool, list(range(1, near)), cap)
    got_near = [[moved(sent_near[i][k], 2 * (i + 1)) for i in range(near - 1)] for k in each]
    local, local_far = gather_pages(owner_list, block_table, pool, [0, near], cap)
    seen = visible_counts(block_table, prefix_len, owner, near, slot_count, page_len)
    scalars = (owner_list, seen, new_slots)
    new_page = new_kv.transpose(1, 2, 0, 3)

    started = []
    updated = None
    for k in each:
        results = attend(
            scalars,
            [(stacked, k), (other, k)],
            [(local[k], 0)],
            [(0, 0)],
            (False, False),
            scale,
            group,
            1,
            page=(new_page, k),
            pool=pool if k == 0 else None,
            after=[started[-1][1]] if started else [],
        )
        if k == 0:
            updated = results[4]
        started.append(results[:4])
    far_other = [moved(q, 1) for q in far_own]
    far = []
    last = started[-1][1]
    for k in each:
        far.append(
            attend(
                scalars,
                [(far_own[k], 0), (far_other[k], 0)],
                [(local_far[k], 0)] + [(a, 0) for a in got_far[k]],
                [(1, i) for i in range(near)],
                (False, True),
                scale,
                group,
                1,
                after=[last],
            )
        )
        last = far[-1][1]
    back = []
    ready = []
    for k in each:
        own_far, own_far_table, other_far = far[k]
        joined = join_packed((own_far, own_far_table), moved(other_far, 1), scale, after=[last])
        back.append(moved(joined, pairs))
        mine, mine_table, theirs, theirs_table = started[k]
        ready.append(
            attend(
                scalars,
                [(stacked, k), (other, k)],
                [(a, 0) for a in got_near[k]],
                [(0, i) for i in range(1, near)],
                (False, True),
                scale,
                group,
                1,
                prev=[(mine, mine_table, 0), (theirs, theirs_table, 0)],
                after=[joined],
            )
        )
        last = ready[-1][1]
    attended = None
    for k in each:
        own_part, own_table, other_part = ready[k]
        attended = join_out(
            (own_part, own_table), [moved(other_part, 1), back[k]], attended, queries.shape, k, group, scale
        )
    return (attended, updated)


def solution(mesh):
    placed = (
        P(("groups", "pool"), "head", None),
        P(("groups", "pool"), None, "head", None),
        P(("groups", "pool"), None, "head", None, None),
        P("groups", None),
        P("groups"),
        P("groups"),
    )
    return jax.shard_map(
        on_device,
        mesh=mesh,
        in_specs=placed,
        out_specs=(
            P(("groups", "pool"), "head", None),
            P(("groups", "pool"), None, "head", None, None),
        ),
        check_vma=False,
    )
```

```python
import functools

import jax
import jax.numpy as jnp
from jax import lax
from jax.experimental import pallas as pl
from jax.experimental.pallas import tpu as pltpu
from jax.sharding import PartitionSpec as P


log2_e = 1.4426950408889634
hidden_score = -2e30
lowest_top = -1e30
lanes = 128
block_rows = 128
kernel_bytes = 24 << 20


def moved(array, apart):
    count = lax.axis_size("pool")
    return lax.ppermute(array, "pool", [(i, i ^ apart) for i in range(count)])


def whole(array):
    return pl.BlockSpec(array.shape, lambda i, *_: (0,) * len(array.shape))


def diagonal():
    shape = (lanes, lanes)
    return lax.broadcasted_iota(jnp.int32, shape, 0) == lax.broadcasted_iota(jnp.int32, shape, 1)


def as_row(column, eye):
    spread = jnp.where(eye, jnp.broadcast_to(column, (lanes, lanes)), 0.0)
    return jnp.sum(spread, axis=0, keepdims=True)


def as_column(row, eye):
    spread = jnp.where(eye, jnp.broadcast_to(row, (lanes, lanes)), 0.0)
    return jnp.sum(spread, axis=1, keepdims=True)


def in_three(values):
    high = values.astype(jnp.bfloat16)
    rest = values - high.astype(jnp.float32)
    middle = rest.astype(jnp.bfloat16)
    low = (rest - middle.astype(jnp.float32)).astype(jnp.bfloat16)
    return (high, middle, low)


def from_three(ref, begin, count):
    parts = [
        ref[0, begin + i * count : begin + (i + 1) * count].astype(jnp.float32) for i in range(3)
    ]
    return parts[0] + parts[1] + parts[2]


def gather_body(owner_ref, table_ref, pool_ref, *refs, lists, kv_heads, cap):
    outs = refs[:-4]
    staged, slots, sem_in, sem_out = refs[-4:]
    owner = owner_ref[0]
    pair = owner >> 1
    slot_count = pool_ref.shape[0]
    base = owner * slot_count
    width = table_ref.shape[1]

    def look(j, found):
        following = []
        for at, which in enumerate(lists):
            slot = table_ref[pair ^ which, j] - base
            slots[at * (cap + 1) + jnp.minimum(found[at], cap)] = slot
            held = (slot >= 0) & (slot < slot_count)
            following.append(found[at] + held.astype(jnp.int32))
        return tuple(following)

    found = lax.fori_loop(0, width, look, (jnp.int32(0),) * len(lists), unroll=4)
    arriving = []
    for at in range(len(lists)):
        for k in range(kv_heads):
            for i in range(cap):
                slot = jnp.where(i < found[at], slots[at * (cap + 1) + i], 0)
                copy = pltpu.make_async_copy(
                    pool_ref.at[slot, :, k], staged.at[at, k, i], sem_in.at[at, k, i]
                )
                copy.start()
                arriving.append(copy)
    leaving = []
    for at in range(len(lists)):
        for k in range(kv_heads):
            for i in range(cap):
                arriving[(at * kv_heads + k) * cap + i].wait()
            copy = pltpu.make_async_copy(
                staged.at[at, k], outs[at * kv_heads + k].at[0], sem_out.at[at, k]
            )
            copy.start()
            leaving.append(copy)
    for copy in leaving:
        copy.wait()


def gather_pages(owner, table, pool, lists, cap):
    _, pair_of, kv_heads, page_len, head_dim = pool.shape
    shape = pltpu.HBM((1, cap, pair_of, page_len, head_dim), pool.dtype)
    count = len(lists) * kv_heads
    outs = pl.pallas_call(
        functools.partial(gather_body, lists=lists, kv_heads=kv_heads, cap=cap),
        out_shape=[shape] * count,
        grid_spec=pltpu.PrefetchScalarGridSpec(
            num_scalar_prefetch=2,
            grid=(1,),
            in_specs=[pl.BlockSpec(memory_space=pltpu.HBM)],
            out_specs=[pl.BlockSpec(memory_space=pltpu.HBM)] * count,
            scratch_shapes=[
                pltpu.VMEM((len(lists), kv_heads, cap, pair_of, page_len, head_dim), pool.dtype),
                pltpu.SMEM((len(lists) * (cap + 1),), jnp.int32),
                pltpu.SemaphoreType.DMA((len(lists), kv_heads, cap)),
                pltpu.SemaphoreType.DMA((len(lists), kv_heads)),
            ],
        ),
        compiler_params=pltpu.CompilerParams(vmem_limit_bytes=kernel_bytes),
        name="gather_pages",
    )(owner, table, pltpu.with_memory_space_constraint(pool, pltpu.HBM))
    return [outs[i * kv_heads : (i + 1) * kv_heads] for i in range(len(lists))]


def attend_body(
    owner_ref,
    seen_ref,
    fresh_ref,
    *refs,
    halves,
    seen_at,
    has_page,
    has_prev,
    packed,
    step_rows,
    tile_rows,
    group,
    scale,
    copies_pool,
    waits,
    page_at,
):
    refs = list(refs)
    q_refs = [refs.pop(0) for _ in range(halves)]
    kv_refs = [refs.pop(0) for _ in seen_at]
    page_ref = refs.pop(0) if has_page else None
    prev_refs = [(refs.pop(0), refs.pop(0)) for _ in range(halves)] if has_prev else None
    pool_ref = refs.pop(0) if copies_pool else None
    del refs[:waits]
    out_refs = []
    for h in range(halves):
        out_refs.append((refs.pop(0),) if packed[h] else (refs.pop(0), refs.pop(0)))
    new_pool = refs.pop(0) if copies_pool else None
    wide_values = refs.pop(0)
    tables = [refs.pop(0) if packed[h] else out_refs[h][1].at[0] for h in range(halves)]
    if copies_pool:
        staged, sem_in, sem_out = refs
    head = pl.program_id(0)
    step = pl.program_id(1)
    heads = pl.num_programs(0)
    steps = pl.num_programs(1)
    owner = owner_ref[0]
    half = 1 - ((owner & 1) ^ ((owner >> 1) & 1))
    page_len = kv_refs[0].shape[3]
    keys = [ref.shape[1] * page_len for ref in kv_refs]

    if copies_pool:

        @pl.when((head == 0) & (step == 0))
        def _():
            pltpu.make_async_copy(pool_ref, staged, sem_in).start()

        @pl.when((head == 0) & (step == jnp.minimum(1, steps - 1)))
        def _():
            pltpu.make_async_copy(pool_ref, staged, sem_in).wait()
            staged[fresh_ref[owner] - owner * staged.shape[0]] = page_ref[...]
            pltpu.make_async_copy(staged, new_pool, sem_out).start()

    @pl.when(step == 0)
    def _():
        ones = jnp.ones((page_len, lanes), jnp.bfloat16)
        begin = 0
        for ref in kv_refs:
            for p in range(ref.shape[1]):
                wide_values[begin : begin + page_len, :lanes] = ref[0, p, 1]
                wide_values[begin : begin + page_len, lanes:] = ones
                begin += page_len
        if has_page:
            wide_values[begin : begin + page_len, :lanes] = page_ref[1, page_at]
            wide_values[begin : begin + page_len, lanes:] = ones

    eye = diagonal()
    limits = []
    for s, at in enumerate(seen_at):
        position = lax.broadcasted_iota(jnp.int32, (1, keys[s]), 1)
        limit = jnp.where(position < seen_ref[at[0], at[1]], jnp.inf, hidden_score)
        limits.append(limit.astype(jnp.float32))

    def score(h, t):
        query = q_refs[h][0, t * tile_rows : (t + 1) * tile_rows]
        scores = []
        for s, ref in enumerate(kv_refs):
            key_rows = ref[0, :, 0].reshape(keys[s], lanes)
            product = lax.dot_general(
                query, key_rows, (((1,), (1,)), ((), ())), preferred_element_type=jnp.float32
            )
            scores.append(jnp.minimum(product, limits[s]))
        if has_page:
            product = lax.dot_general(
                query, page_ref[0, page_at], (((1,), (1,)), ((), ())), preferred_element_type=jnp.float32
            )
            key_at = lax.broadcasted_iota(jnp.int32, product.shape, 1)
            if h == 0:
                row_at = lax.broadcasted_iota(jnp.int32, product.shape, 0)
                token = (step * step_rows + t * tile_rows + row_at) // group
                shown = key_at <= token
            else:
                shown = key_at < jnp.where(half == 0, page_len, 0)
            scores.append(jnp.where(shown, product, hidden_score))
        return scores

    def finish(h, t, scores):
        top = jnp.full((tile_rows, 1), lowest_top, jnp.float32)
        for part in scores:
            top = jnp.maximum(top, jnp.max(part, axis=1, keepdims=True))
        scaled_top = top * scale
        weights = [jnp.exp2(part * scale - scaled_top).astype(jnp.bfloat16) for part in scores]
        mixed = jnp.dot(
            jnp.concatenate(weights, axis=1), wide_values[...], preferred_element_type=jnp.float32
        )
        total = mixed[:, lanes:]
        mixed = mixed[:, :lanes]
        first = step * (step_rows // block_rows) + t * (tile_rows // block_rows)
        count = tables[h].shape[0] // 2
        for u in range(tile_rows // block_rows):
            inner = slice(u * block_rows, (u + 1) * block_rows)
            outer = slice(t * tile_rows + u * block_rows, t * tile_rows + (u + 1) * block_rows)
            part_top, part_total, part_mixed = top[inner], total[inner], mixed[inner]
            row = first + u
            if has_prev:
                prev_mixed, prev_table = prev_refs[h]
                prev_top = as_column(prev_table[0, pl.ds(row, 1)], eye)
                prev_total = as_column(prev_table[0, pl.ds(count + row, 1)], eye)
                joint = jnp.maximum(part_top, prev_top)
                keep = jnp.exp2((part_top - joint) * scale)
                keep_prev = jnp.exp2((prev_top - joint) * scale)
                part_mixed = part_mixed * keep + prev_mixed[0, outer] * keep_prev
                part_total = part_total * keep + prev_total * keep_prev
                part_top = joint
            tables[h][pl.ds(row, 1)] = as_row(part_top, eye)
            tables[h][pl.ds(count + row, 1)] = as_row(part_total, eye)
            if packed[h]:
                at = pl.multiple_of(row * block_rows, block_rows)
                out_refs[h][0][0, pl.ds(at, block_rows)] = part_mixed.astype(jnp.bfloat16)
            else:
                out_refs[h][0][0, outer] = part_mixed

    chains = [(h, t) for t in range(step_rows // tile_rows) for h in range(halves)]
    scores = score(*chains[0])
    for i, chain in enumerate(chains):
        following = score(*chains[i + 1]) if i + 1 < len(chains) else None
        finish(*chain, scores)
        scores = following

    @pl.when(step == steps - 1)
    def _():
        for h in range(halves):
            if packed[h]:
                size = tables[h].shape[0]
                begin = out_refs[h][0].shape[1] - 3 * size
                for i, part in enumerate(in_three(tables[h][...])):
                    out_refs[h][0][0, begin + i * size : begin + (i + 1) * size] = part

    if copies_pool:

        @pl.when((head == heads - 1) & (step == steps - 1))
        def _():
            pltpu.make_async_copy(staged, new_pool, sem_out).wait()


def attend(
    scalars, queries, sources, seen_at, packed, scale, group, heads, page=None, prev=None, pool=None, after=()
):
    halves = len(queries)
    rows = queries[0][0].shape[1]
    size = 2 * (rows // block_rows)
    step_rows = min(rows, 1024 // halves)
    tile_rows = min(step_rows, 256)
    key_count = sum(s.shape[1] * s.shape[3] for s, _ in sources)

    def per_rows(offset):
        return pl.BlockSpec((1, step_rows, lanes), lambda k, i, *_: (k + offset, i, 0))

    def per_head(array, offset):
        tail = array.shape[1:]
        return pl.BlockSpec((1, *tail), lambda k, i, *_: (k + offset,) + (0,) * len(tail))

    anywhere = pl.BlockSpec(memory_space=pl.ANY)
    args = [q for q, _ in queries] + [s for s, _ in sources]
    in_specs = [per_rows(at) for _, at in queries] + [per_head(s, at) for s, at in sources]
    page_at = 0
    if page is not None:
        page, page_at = page
        args.append(page)
        in_specs.append(whole(page))
        key_count += page.shape[2]
    if prev is not None:
        for mixed, table, at in prev:
            args += [mixed, table]
            in_specs += [per_rows(at), per_head(table, at)]
    if pool is not None:
        args.append(pltpu.with_memory_space_constraint(pool, pltpu.HBM))
        in_specs.append(pl.BlockSpec(memory_space=pltpu.HBM))
    args += list(after)
    in_specs += [anywhere] * len(after)
    out_shape = []
    out_specs = []
    scratch = [pltpu.VMEM((key_count, 2 * lanes), jnp.bfloat16)]
    for h in range(halves):
        if packed[h]:
            shape = jax.ShapeDtypeStruct((heads, rows + 3 * size, lanes), jnp.bfloat16)
            out_shape.append(shape)
            out_specs.append(per_head(shape, 0))
            scratch.append(pltpu.VMEM((size, lanes), jnp.float32))
        else:
            table = jax.ShapeDtypeStruct((heads, size, lanes), jnp.float32)
            out_shape += [jax.ShapeDtypeStruct((heads, rows, lanes), jnp.float32), table]
            out_specs += [per_rows(0), per_head(table, 0)]
    if pool is not None:
        out_shape.append(jax.ShapeDtypeStruct(pool.shape, pool.dtype))
        out_specs.append(pl.BlockSpec(memory_space=pltpu.HBM))
        scratch.append(pltpu.VMEM(pool.shape, pool.dtype))
        scratch += [pltpu.SemaphoreType.DMA, pltpu.SemaphoreType.DMA]
    work = halves * heads * rows * key_count
    return pl.pallas_call(
        functools.partial(
            attend_body,
            halves=halves,
            seen_at=seen_at,
            has_page=page is not None,
            has_prev=prev is not None,
            packed=packed,
            step_rows=step_rows,
            tile_rows=tile_rows,
            group=group,
            scale=scale,
            copies_pool=pool is not None,
            waits=len(after),
            page_at=page_at,
        ),
        out_shape=out_shape,
        grid_spec=pltpu.PrefetchScalarGridSpec(
            num_scalar_prefetch=3,
            grid=(heads, rows // step_rows),
            in_specs=in_specs,
            out_specs=out_specs,
            scratch_shapes=scratch,
        ),
        cost_estimate=pl.CostEstimate(
            flops=4 * work * lanes,
            transcendentals=work,
            bytes_accessed=4 * heads * key_count * lanes,
        ),
        compiler_params=pltpu.CompilerParams(vmem_limit_bytes=kernel_bytes),
        name="attend",
    )(*scalars, *args)


def join_body(own_mixed, own_table, *refs, scale, packs, waits):
    refs = list(refs)
    out_ref = refs.pop()
    if waits:
        del refs[-waits:]
    size = own_table.shape[1]
    count = size // 2
    rows = count * block_rows
    eye = diagonal()
    tops = [own_table[0, :count]]
    totals = [own_table[0, count:]]
    for ref in refs:
        table = from_three(ref, rows, size)
        tops.append(table[:count])
        totals.append(table[count:])
    top = functools.reduce(jnp.maximum, tops)
    keeps = [jnp.exp2((t - top) * scale) for t in tops]
    total = sum(t * keep for t, keep in zip(totals, keeps))
    if not packs:
        keeps = [keep / total for keep in keeps]
    for t in range(count):
        at = slice(t * block_rows, (t + 1) * block_rows)
        mixed = own_mixed[0, at] * as_column(keeps[0][t : t + 1], eye)
        for ref, keep in zip(refs, keeps[1:]):
            mixed = mixed + ref[0, at].astype(jnp.float32) * as_column(keep[t : t + 1], eye)
        if packs:
            out_ref[0, at] = mixed.astype(jnp.bfloat16)
        else:
            heads = out_ref.shape[1]
            tokens = block_rows // heads
            shaped = mixed.reshape(tokens, heads, lanes)
            out_ref[t * tokens : (t + 1) * tokens] = shaped.astype(jnp.bfloat16)
    if packs:
        table = jnp.concatenate([top, total], axis=0)
        for i, part in enumerate(in_three(table)):
            out_ref[0, rows + i * size : rows + (i + 1) * size] = part


def join_packed(own, received, scale, after=()):
    mixed, table = own
    args = [mixed, table, received]
    return pl.pallas_call(
        functools.partial(join_body, scale=scale, packs=True, waits=len(after)),
        out_shape=jax.ShapeDtypeStruct(received.shape, received.dtype),
        grid=(1,),
        in_specs=[whole(a) for a in args] + [pl.BlockSpec(memory_space=pl.ANY)] * len(after),
        out_specs=whole(received),
        compiler_params=pltpu.CompilerParams(vmem_limit_bytes=kernel_bytes),
        name="join_packed",
    )(*args, *after)


def join_out(own, received, target, shape, index, group, scale):
    mixed, table = own
    args = [mixed, table, *received]
    in_specs = [whole(a) for a in args]
    aliases = {}
    if target is not None:
        aliases = {len(args): 0}
        args.append(target)
        in_specs.append(pl.BlockSpec(memory_space=pl.ANY))
    return pl.pallas_call(
        functools.partial(join_body, scale=scale, packs=False, waits=len(aliases)),
        out_shape=jax.ShapeDtypeStruct(shape, jnp.bfloat16),
        grid=(1,),
        in_specs=in_specs,
        out_specs=pl.BlockSpec((shape[0], group, shape[2]), lambda i: (0, index, 0)),
        input_output_aliases=aliases,
        compiler_params=pltpu.CompilerParams(vmem_limit_bytes=kernel_bytes),
        name="join_out",
    )(*args)


def visible_counts(table, lengths, owner, steps, slot_count, page_len):
    requests, width = table.shape
    holders = owner ^ (2 * jnp.arange(steps, dtype=jnp.int32))
    chosen = (owner >> 1) ^ (jnp.arange(2, dtype=jnp.int32) * steps)
    column = jnp.arange(width, dtype=jnp.int32)
    count = jnp.clip(lengths[:, None] - column[None, :] * page_len, 0, page_len)
    first = holders[None, :, None, None] * slot_count
    entry = table[None, None]
    held = (entry >= first) & (entry < first + slot_count)
    asked = jnp.arange(requests, dtype=jnp.int32)[None, :] == chosen[:, None]
    picked = held & asked[:, None, :, None]
    return jnp.sum(jnp.where(picked, count[None, None], 0), axis=(2, 3))


def on_device(queries, new_kv, pool, block_table, prefix_len, new_slots):
    owner_count = lax.axis_size("pool")
    owner = lax.axis_index("pool").astype(jnp.int32)
    slot_count, _, kv_heads, page_len, head_dim = pool.shape
    tokens, q_heads, _ = queries.shape
    group = q_heads // kv_heads
    rows = tokens * group
    pairs = owner_count // 2
    near = pairs // 2
    cap = block_table.shape[1] // owner_count
    scale = head_dim**-0.5 * log2_e
    each = range(kv_heads)

    split = [
        queries[:, k * group : (k + 1) * group].reshape(1, rows, head_dim) for k in each
    ]
    far_own = [moved(split[k], pairs) for k in each]
    other = [moved(split[k], 1) for k in each]
    owner_list = jnp.full((1,), owner, jnp.int32)
    lists = [near + k for k in range(1, near)] + list(range(1, near)) + [0, near]
    pages = gather_pages(owner_list, block_table, pool, lists, cap)

    def exchanged(sent):
        return [[moved(sent[i][k], 2 * (i + 1)) for i in range(near - 1)] for k in each]

    got_far = exchanged(pages)
    got_near = exchanged(pages[near - 1 :])
    local, local_far = pages[2 * near - 2 :]
    seen = visible_counts(block_table, prefix_len, owner, near, slot_count, page_len)
    scalars = (owner_list, seen, new_slots)
    new_page = new_kv.transpose(1, 2, 0, 3)

    started = []
    updated = None
    after = []
    for k in each:
        results = attend(
            scalars,
            [(split[k], 0), (other[k], 0)],
            [(local[k], 0)],
            [(0, 0)],
            (False, False),
            scale,
            group,
            1,
            page=(new_page, k),
            pool=pool if k == 0 else None,
            after=after,
        )
        if k == 0:
            updated = results[4]
        started.append(results[:4])
        after = [results[1]]
    far_other = [moved(far_own[k], 1) for k in each]
    far = []
    for k in each:
        results = attend(
            scalars,
            [(far_own[k], 0), (far_other[k], 0)],
            [(local_far[k], 0)] + [(a, 0) for a in got_far[k]],
            [(1, i) for i in range(near)],
            (False, True),
            scale,
            group,
            1,
            after=after,
        )
        far.append((results[:2], moved(results[2], 1)))
        after = [results[1]]
    back = []
    ready = []
    for k in each:
        joined = join_packed(*far[k], scale, after=after)
        back.append(moved(joined, pairs))
        mine, mine_table, theirs, theirs_table = started[k]
        results = attend(
            scalars,
            [(split[k], 0), (other[k], 0)],
            [(a, 0) for a in got_near[k]],
            [(0, i) for i in range(1, near)],
            (False, True),
            scale,
            group,
            1,
            prev=[(mine, mine_table, 0), (theirs, theirs_table, 0)],
            after=[joined],
        )
        ready.append((results[:2], moved(results[2], 1)))
        after = [results[1]]
    attended = None
    for k in each:
        own, received = ready[k]
        attended = join_out(
            own, [received, back[k]], attended, queries.shape, k, group, scale
        )
    return (attended, updated)


def solution(mesh):
    placed = (
        P(("groups", "pool"), "head", None),
        P(("groups", "pool"), None, "head", None),
        P(("groups", "pool"), None, "head", None, None),
        P("groups", None),
        P("groups"),
        P("groups"),
    )

    return jax.shard_map(
        on_device,
        mesh=mesh,
        in_specs=placed,
        out_specs=(
            P(("groups", "pool"), "head", None),
            P(("groups", "pool"), None, "head", None, None),
        ),
        check_vma=False,
    )
```

```python
import functools

import jax
import jax.numpy as jnp
from jax import lax
from jax.experimental import pallas as pl
from jax.experimental.pallas import tpu as pltpu
from jax.sharding import PartitionSpec as P


log2_e = 1.4426950408889634
hidden_score = -2e30
lowest_top = -1e30
lanes = 128
block_rows = 128
kernel_bytes = 24 << 20


def moved(array, apart):
    count = lax.axis_size("pool")
    return lax.ppermute(array, "pool", [(i, i ^ apart) for i in range(count)])


def whole(array):
    return pl.BlockSpec(array.shape, lambda i, *_: (0,) * len(array.shape))


def diagonal():
    shape = (lanes, lanes)
    return lax.broadcasted_iota(jnp.int32, shape, 0) == lax.broadcasted_iota(jnp.int32, shape, 1)


def as_row(column, eye):
    spread = jnp.where(eye, jnp.broadcast_to(column, (lanes, lanes)), 0.0)
    return jnp.sum(spread, axis=0, keepdims=True)


def as_column(row, eye):
    spread = jnp.where(eye, jnp.broadcast_to(row, (lanes, lanes)), 0.0)
    return jnp.sum(spread, axis=1, keepdims=True)


def in_three(values):
    high = values.astype(jnp.bfloat16)
    rest = values - high.astype(jnp.float32)
    middle = rest.astype(jnp.bfloat16)
    low = (rest - middle.astype(jnp.float32)).astype(jnp.bfloat16)
    return (high, middle, low)


def from_three(ref, begin, count):
    parts = [
        ref[0, begin + i * count : begin + (i + 1) * count].astype(jnp.float32) for i in range(3)
    ]
    return parts[0] + parts[1] + parts[2]


def gather_body(owner_ref, table_ref, pool_ref, *refs, lists, kv_heads, cap):
    outs = refs[:-4]
    staged, slots, sem_in, sem_out = refs[-4:]
    owner = owner_ref[0]
    pair = owner >> 1
    slot_count = pool_ref.shape[0]
    base = owner * slot_count
    width = table_ref.shape[1]

    def look(j, found):
        following = []
        for at, which in enumerate(lists):
            slot = table_ref[pair ^ which, j] - base
            slots[at * (cap + 1) + jnp.minimum(found[at], cap)] = slot
            held = (slot >= 0) & (slot < slot_count)
            following.append(found[at] + held.astype(jnp.int32))
        return tuple(following)

    found = lax.fori_loop(0, width, look, (jnp.int32(0),) * len(lists), unroll=4)
    arriving = []
    for at in range(len(lists)):
        for k in range(kv_heads):
            for i in range(cap):
                slot = jnp.where(i < found[at], slots[at * (cap + 1) + i], 0)
                copy = pltpu.make_async_copy(
                    pool_ref.at[slot, :, k], staged.at[at, k, i], sem_in.at[at, k, i]
                )
                copy.start()
                arriving.append(copy)
    leaving = []
    for at in range(len(lists)):
        for k in range(kv_heads):
            for i in range(cap):
                arriving[(at * kv_heads + k) * cap + i].wait()
            copy = pltpu.make_async_copy(
                staged.at[at, k], outs[at * kv_heads + k].at[0], sem_out.at[at, k]
            )
            copy.start()
            leaving.append(copy)
    for copy in leaving:
        copy.wait()


def gather_pages(owner, table, pool, lists, cap):
    _, pair_of, kv_heads, page_len, head_dim = pool.shape
    shape = pltpu.HBM((1, cap, pair_of, page_len, head_dim), pool.dtype)
    count = len(lists) * kv_heads
    outs = pl.pallas_call(
        functools.partial(gather_body, lists=lists, kv_heads=kv_heads, cap=cap),
        out_shape=[shape] * count,
        grid_spec=pltpu.PrefetchScalarGridSpec(
            num_scalar_prefetch=2,
            grid=(1,),
            in_specs=[pl.BlockSpec(memory_space=pltpu.HBM)],
            out_specs=[pl.BlockSpec(memory_space=pltpu.HBM)] * count,
            scratch_shapes=[
                pltpu.VMEM((len(lists), kv_heads, cap, pair_of, page_len, head_dim), pool.dtype),
                pltpu.SMEM((len(lists) * (cap + 1),), jnp.int32),
                pltpu.SemaphoreType.DMA((len(lists), kv_heads, cap)),
                pltpu.SemaphoreType.DMA((len(lists), kv_heads)),
            ],
        ),
        compiler_params=pltpu.CompilerParams(vmem_limit_bytes=kernel_bytes),
        name="gather_pages",
    )(owner, table, pltpu.with_memory_space_constraint(pool, pltpu.HBM))
    return [outs[i * kv_heads : (i + 1) * kv_heads] for i in range(len(lists))]


def attend_body(
    owner_ref,
    seen_ref,
    fresh_ref,
    *refs,
    halves,
    seen_at,
    has_page,
    has_prev,
    packed,
    step_rows,
    tile_rows,
    group,
    scale,
    copies_pool,
    waits,
    page_at,
):
    refs = list(refs)
    q_refs = [refs.pop(0) for _ in range(halves)]
    kv_refs = [refs.pop(0) for _ in seen_at]
    page_ref = refs.pop(0) if has_page else None
    prev_refs = [(refs.pop(0), refs.pop(0)) for _ in range(halves)] if has_prev else None
    pool_ref = refs.pop(0) if copies_pool else None
    del refs[:waits]
    out_refs = []
    for h in range(halves):
        out_refs.append((refs.pop(0),) if packed[h] else (refs.pop(0), refs.pop(0)))
    new_pool = refs.pop(0) if copies_pool else None
    wide_values = refs.pop(0)
    tables = [refs.pop(0) if packed[h] else out_refs[h][1].at[0] for h in range(halves)]
    if copies_pool:
        staged, sem_in, sem_out = refs
    head = pl.program_id(0)
    step = pl.program_id(1)
    heads = pl.num_programs(0)
    steps = pl.num_programs(1)
    owner = owner_ref[0]
    half = 1 - ((owner & 1) ^ ((owner >> 1) & 1))
    page_len = kv_refs[0].shape[3]
    keys = [ref.shape[1] * page_len for ref in kv_refs]

    if copies_pool:

        @pl.when((head == 0) & (step == 0))
        def _():
            pltpu.make_async_copy(pool_ref, staged, sem_in).start()

        @pl.when((head == 0) & (step == jnp.minimum(1, steps - 1)))
        def _():
            pltpu.make_async_copy(pool_ref, staged, sem_in).wait()
            staged[fresh_ref[owner] - owner * staged.shape[0]] = page_ref[...]
            pltpu.make_async_copy(staged, new_pool, sem_out).start()

    @pl.when(step == 0)
    def _():
        ones = jnp.ones((page_len, lanes), jnp.bfloat16)
        begin = 0
        for ref in kv_refs:
            for p in range(ref.shape[1]):
                wide_values[begin : begin + page_len, :lanes] = ref[0, p, 1]
                wide_values[begin : begin + page_len, lanes:] = ones
                begin += page_len
        if has_page:
            wide_values[begin : begin + page_len, :lanes] = page_ref[1, page_at]
            wide_values[begin : begin + page_len, lanes:] = ones

    eye = diagonal()
    limits = []
    for s, at in enumerate(seen_at):
        position = lax.broadcasted_iota(jnp.int32, (1, keys[s]), 1)
        limit = jnp.where(position < seen_ref[at[0], at[1]], jnp.inf, hidden_score)
        limits.append(limit.astype(jnp.float32))

    def score(h, t):
        query = q_refs[h][0, t * tile_rows : (t + 1) * tile_rows]
        scores = []
        for s, ref in enumerate(kv_refs):
            key_rows = ref[0, :, 0].reshape(keys[s], lanes)
            product = lax.dot_general(
                query, key_rows, (((1,), (1,)), ((), ())), preferred_element_type=jnp.float32
            )
            scores.append(jnp.minimum(product, limits[s]))
        if has_page:
            product = lax.dot_general(
                query, page_ref[0, page_at], (((1,), (1,)), ((), ())), preferred_element_type=jnp.float32
            )
            key_at = lax.broadcasted_iota(jnp.int32, product.shape, 1)
            if h == 0:
                row_at = lax.broadcasted_iota(jnp.int32, product.shape, 0)
                token = (step * step_rows + t * tile_rows + row_at) // group
                shown = key_at <= token
            else:
                shown = key_at < jnp.where(half == 0, page_len, 0)
            scores.append(jnp.where(shown, product, hidden_score))
        return scores

    def finish(h, t, scores):
        top = jnp.full((tile_rows, 1), lowest_top, jnp.float32)
        for part in scores:
            top = jnp.maximum(top, jnp.max(part, axis=1, keepdims=True))
        scaled_top = top * scale
        weights = [jnp.exp2(part * scale - scaled_top).astype(jnp.bfloat16) for part in scores]
        mixed = jnp.dot(
            jnp.concatenate(weights, axis=1), wide_values[...], preferred_element_type=jnp.float32
        )
        total = mixed[:, lanes:]
        mixed = mixed[:, :lanes]
        first = step * (step_rows // block_rows) + t * (tile_rows // block_rows)
        count = tables[h].shape[0] // 2
        for u in range(tile_rows // block_rows):
            inner = slice(u * block_rows, (u + 1) * block_rows)
            outer = slice(t * tile_rows + u * block_rows, t * tile_rows + (u + 1) * block_rows)
            part_top, part_total, part_mixed = top[inner], total[inner], mixed[inner]
            row = first + u
            if has_prev:
                prev_mixed, prev_table = prev_refs[h]
                prev_top = as_column(prev_table[0, pl.ds(row, 1)], eye)
                prev_total = as_column(prev_table[0, pl.ds(count + row, 1)], eye)
                joint = jnp.maximum(part_top, prev_top)
                keep = jnp.exp2((part_top - joint) * scale)
                keep_prev = jnp.exp2((prev_top - joint) * scale)
                part_mixed = part_mixed * keep + prev_mixed[0, outer] * keep_prev
                part_total = part_total * keep + prev_total * keep_prev
                part_top = joint
            tables[h][pl.ds(row, 1)] = as_row(part_top, eye)
            tables[h][pl.ds(count + row, 1)] = as_row(part_total, eye)
            if packed[h]:
                at = pl.multiple_of(row * block_rows, block_rows)
                out_refs[h][0][0, pl.ds(at, block_rows)] = part_mixed.astype(jnp.bfloat16)
            else:
                out_refs[h][0][0, outer] = part_mixed

    chains = [(h, t) for t in range(step_rows // tile_rows) for h in range(halves)]
    scores = score(*chains[0])
    for i, chain in enumerate(chains):
        following = score(*chains[i + 1]) if i + 1 < len(chains) else None
        finish(*chain, scores)
        scores = following

    @pl.when(step == steps - 1)
    def _():
        for h in range(halves):
            if packed[h]:
                size = tables[h].shape[0]
                begin = out_refs[h][0].shape[1] - 3 * size
                for i, part in enumerate(in_three(tables[h][...])):
                    out_refs[h][0][0, begin + i * size : begin + (i + 1) * size] = part

    if copies_pool:

        @pl.when((head == heads - 1) & (step == steps - 1))
        def _():
            pltpu.make_async_copy(staged, new_pool, sem_out).wait()


def attend(
    scalars, queries, sources, seen_at, packed, scale, group, heads, page=None, prev=None, pool=None, after=()
):
    halves = len(queries)
    rows = queries[0][0].shape[1]
    size = 2 * (rows // block_rows)
    step_rows = min(rows, 1024 // halves)
    tile_rows = min(step_rows, 256)
    key_count = sum(s.shape[1] * s.shape[3] for s, _ in sources)

    def per_rows(offset):
        return pl.BlockSpec((1, step_rows, lanes), lambda k, i, *_: (k + offset, i, 0))

    def per_head(array, offset):
        tail = array.shape[1:]
        return pl.BlockSpec((1, *tail), lambda k, i, *_: (k + offset,) + (0,) * len(tail))

    anywhere = pl.BlockSpec(memory_space=pl.ANY)
    args = [q for q, _ in queries] + [s for s, _ in sources]
    in_specs = [per_rows(at) for _, at in queries] + [per_head(s, at) for s, at in sources]
    page_at = 0
    if page is not None:
        page, page_at = page
        args.append(page)
        in_specs.append(whole(page))
        key_count += page.shape[2]
    if prev is not None:
        for mixed, table, at in prev:
            args += [mixed, table]
            in_specs += [per_rows(at), per_head(table, at)]
    if pool is not None:
        args.append(pltpu.with_memory_space_constraint(pool, pltpu.HBM))
        in_specs.append(pl.BlockSpec(memory_space=pltpu.HBM))
    args += list(after)
    in_specs += [anywhere] * len(after)
    out_shape = []
    out_specs = []
    scratch = [pltpu.VMEM((key_count, 2 * lanes), jnp.bfloat16)]
    for h in range(halves):
        if packed[h]:
            shape = jax.ShapeDtypeStruct((heads, rows + 3 * size, lanes), jnp.bfloat16)
            out_shape.append(shape)
            out_specs.append(per_head(shape, 0))
            scratch.append(pltpu.VMEM((size, lanes), jnp.float32))
        else:
            table = jax.ShapeDtypeStruct((heads, size, lanes), jnp.float32)
            out_shape += [jax.ShapeDtypeStruct((heads, rows, lanes), jnp.float32), table]
            out_specs += [per_rows(0), per_head(table, 0)]
    if pool is not None:
        out_shape.append(jax.ShapeDtypeStruct(pool.shape, pool.dtype))
        out_specs.append(pl.BlockSpec(memory_space=pltpu.HBM))
        scratch.append(pltpu.VMEM(pool.shape, pool.dtype))
        scratch += [pltpu.SemaphoreType.DMA, pltpu.SemaphoreType.DMA]
    work = halves * heads * rows * key_count
    return pl.pallas_call(
        functools.partial(
            attend_body,
            halves=halves,
            seen_at=seen_at,
            has_page=page is not None,
            has_prev=prev is not None,
            packed=packed,
            step_rows=step_rows,
            tile_rows=tile_rows,
            group=group,
            scale=scale,
            copies_pool=pool is not None,
            waits=len(after),
            page_at=page_at,
        ),
        out_shape=out_shape,
        grid_spec=pltpu.PrefetchScalarGridSpec(
            num_scalar_prefetch=3,
            grid=(heads, rows // step_rows),
            in_specs=in_specs,
            out_specs=out_specs,
            scratch_shapes=scratch,
        ),
        cost_estimate=pl.CostEstimate(
            flops=4 * work * lanes,
            transcendentals=work,
            bytes_accessed=4 * heads * key_count * lanes,
        ),
        compiler_params=pltpu.CompilerParams(vmem_limit_bytes=kernel_bytes),
        name="attend",
    )(*scalars, *args)


def join_body(own_mixed, own_table, *refs, scale, packs, waits):
    refs = list(refs)
    out_ref = refs.pop()
    if waits:
        del refs[-waits:]
    size = own_table.shape[1]
    count = size // 2
    rows = count * block_rows
    eye = diagonal()
    tops = [own_table[0, :count]]
    totals = [own_table[0, count:]]
    for ref in refs:
        table = from_three(ref, rows, size)
        tops.append(table[:count])
        totals.append(table[count:])
    top = functools.reduce(jnp.maximum, tops)
    keeps = [jnp.exp2((t - top) * scale) for t in tops]
    total = sum(t * keep for t, keep in zip(totals, keeps))
    if not packs:
        keeps = [keep / total for keep in keeps]
    for t in range(count):
        at = slice(t * block_rows, (t + 1) * block_rows)
        mixed = own_mixed[0, at] * as_column(keeps[0][t : t + 1], eye)
        for ref, keep in zip(refs, keeps[1:]):
            mixed = mixed + ref[0, at].astype(jnp.float32) * as_column(keep[t : t + 1], eye)
        if packs:
            out_ref[0, at] = mixed.astype(jnp.bfloat16)
        else:
            heads = out_ref.shape[1]
            tokens = block_rows // heads
            shaped = mixed.reshape(tokens, heads, lanes)
            out_ref[t * tokens : (t + 1) * tokens] = shaped.astype(jnp.bfloat16)
    if packs:
        table = jnp.concatenate([top, total], axis=0)
        for i, part in enumerate(in_three(table)):
            out_ref[0, rows + i * size : rows + (i + 1) * size] = part


def join_packed(own, received, scale, after=()):
    mixed, table = own
    args = [mixed, table, received]
    return pl.pallas_call(
        functools.partial(join_body, scale=scale, packs=True, waits=len(after)),
        out_shape=jax.ShapeDtypeStruct(received.shape, received.dtype),
        grid=(1,),
        in_specs=[whole(a) for a in args] + [pl.BlockSpec(memory_space=pl.ANY)] * len(after),
        out_specs=whole(received),
        compiler_params=pltpu.CompilerParams(vmem_limit_bytes=kernel_bytes),
        name="join_packed",
    )(*args, *after)


def join_out(own, received, target, shape, index, group, scale):
    mixed, table = own
    args = [mixed, table, *received]
    in_specs = [whole(a) for a in args]
    aliases = {}
    if target is not None:
        aliases = {len(args): 0}
        args.append(target)
        in_specs.append(pl.BlockSpec(memory_space=pl.ANY))
    return pl.pallas_call(
        functools.partial(join_body, scale=scale, packs=False, waits=len(aliases)),
        out_shape=jax.ShapeDtypeStruct(shape, jnp.bfloat16),
        grid=(1,),
        in_specs=in_specs,
        out_specs=pl.BlockSpec((shape[0], group, shape[2]), lambda i: (0, index, 0)),
        input_output_aliases=aliases,
        compiler_params=pltpu.CompilerParams(vmem_limit_bytes=kernel_bytes),
        name="join_out",
    )(*args)


def visible_counts(table, lengths, owner, steps, slot_count, page_len):
    requests, width = table.shape
    holders = owner ^ (2 * jnp.arange(steps, dtype=jnp.int32))
    chosen = (owner >> 1) ^ (jnp.arange(2, dtype=jnp.int32) * steps)
    column = jnp.arange(width, dtype=jnp.int32)
    count = jnp.clip(lengths[:, None] - column[None, :] * page_len, 0, page_len)
    first = holders[None, :, None, None] * slot_count
    entry = table[None, None]
    held = (entry >= first) & (entry < first + slot_count)
    asked = jnp.arange(requests, dtype=jnp.int32)[None, :] == chosen[:, None]
    picked = held & asked[:, None, :, None]
    return jnp.sum(jnp.where(picked, count[None, None], 0), axis=(2, 3))


def on_device(queries, new_kv, pool, block_table, prefix_len, new_slots):
    owner_count = lax.axis_size("pool")
    owner = lax.axis_index("pool").astype(jnp.int32)
    slot_count, _, kv_heads, page_len, head_dim = pool.shape
    tokens, q_heads, _ = queries.shape
    group = q_heads // kv_heads
    rows = tokens * group
    pairs = owner_count // 2
    near = pairs // 2
    cap = block_table.shape[1] // owner_count
    scale = head_dim**-0.5 * log2_e
    each = range(kv_heads)

    split = [
        queries[:, k * group : (k + 1) * group].reshape(1, rows, head_dim) for k in each
    ]
    far_own = [moved(split[k], pairs) for k in each]
    other = [moved(split[k], 1) for k in each]
    owner_list = jnp.full((1,), owner, jnp.int32)
    far_lists = [near + k for k in range(1, near)]
    sent_far = gather_pages(owner_list, block_table, pool, far_lists, cap)
    rest_lists = list(range(1, near)) + [0, near]
    pages = gather_pages(owner_list, block_table, pool, rest_lists, cap)

    def exchanged(sent):
        return [[moved(sent[i][k], 2 * (i + 1)) for i in range(near - 1)] for k in each]

    got_far = exchanged(sent_far)
    got_near = exchanged(pages)
    local, local_far = pages[near - 1 :]
    seen = visible_counts(block_table, prefix_len, owner, near, slot_count, page_len)
    scalars = (owner_list, seen, new_slots)
    new_page = new_kv.transpose(1, 2, 0, 3)

    started = []
    updated = None
    after = []
    for k in each:
        results = attend(
            scalars,
            [(split[k], 0), (other[k], 0)],
            [(local[k], 0)],
            [(0, 0)],
            (False, False),
            scale,
            group,
            1,
            page=(new_page, k),
            pool=pool if k == 0 else None,
            after=after,
        )
        if k == 0:
            updated = results[4]
        started.append(results[:4])
        after = [results[1]]
    far_other = [moved(far_own[k], 1) for k in each]
    far = []
    for k in each:
        results = attend(
            scalars,
            [(far_own[k], 0), (far_other[k], 0)],
            [(local_far[k], 0)] + [(a, 0) for a in got_far[k]],
            [(1, i) for i in range(near)],
            (False, True),
            scale,
            group,
            1,
            after=after,
        )
        far.append((results[:2], moved(results[2], 1)))
        after = [results[1]]
    back = []
    ready = []
    for k in each:
        joined = join_packed(*far[k], scale, after=after)
        back.append(moved(joined, pairs))
        mine, mine_table, theirs, theirs_table = started[k]
        results = attend(
            scalars,
            [(split[k], 0), (other[k], 0)],
            [(a, 0) for a in got_near[k]],
            [(0, i) for i in range(1, near)],
            (False, True),
            scale,
            group,
            1,
            prev=[(mine, mine_table, 0), (theirs, theirs_table, 0)],
            after=[joined],
        )
        ready.append((results[:2], moved(results[2], 1)))
        after = [results[1]]
    attended = None
    for k in each:
        own, received = ready[k]
        attended = join_out(
            own, [received, back[k]], attended, queries.shape, k, group, scale
        )
    return (attended, updated)


def solution(mesh):
    placed = (
        P(("groups", "pool"), "head", None),
        P(("groups", "pool"), None, "head", None),
        P(("groups", "pool"), None, "head", None, None),
        P("groups", None),
        P("groups"),
        P("groups"),
    )

    return jax.shard_map(
        on_device,
        mesh=mesh,
        in_specs=placed,
        out_specs=(
            P(("groups", "pool"), "head", None),
            P(("groups", "pool"), None, "head", None, None),
        ),
        check_vma=False,
    )
```

```python
import functools

import jax
import jax.numpy as jnp
from jax import lax
from jax.experimental import pallas as pl
from jax.experimental.pallas import tpu as pltpu
from jax.sharding import PartitionSpec as P


log2_e = 1.4426950408889634
hidden_score = -2e30
lowest_top = -1e30
lanes = 128
block_rows = 128
kernel_bytes = 24 << 20


def moved(array, apart):
    count = lax.axis_size("pool")
    return lax.ppermute(array, "pool", [(i, i ^ apart) for i in range(count)])


def whole(array):
    return pl.BlockSpec(array.shape, lambda i, *_: (0,) * len(array.shape))


def diagonal():
    shape = (lanes, lanes)
    return lax.broadcasted_iota(jnp.int32, shape, 0) == lax.broadcasted_iota(jnp.int32, shape, 1)


def as_row(column, eye):
    spread = jnp.where(eye, jnp.broadcast_to(column, (lanes, lanes)), 0.0)
    return jnp.sum(spread, axis=0, keepdims=True)


def as_column(row, eye):
    spread = jnp.where(eye, jnp.broadcast_to(row, (lanes, lanes)), 0.0)
    return jnp.sum(spread, axis=1, keepdims=True)


def in_three(values):
    high = values.astype(jnp.bfloat16)
    rest = values - high.astype(jnp.float32)
    middle = rest.astype(jnp.bfloat16)
    low = (rest - middle.astype(jnp.float32)).astype(jnp.bfloat16)
    return (high, middle, low)


def from_three(ref, begin, count):
    parts = [
        ref[0, begin + i * count : begin + (i + 1) * count].astype(jnp.float32) for i in range(3)
    ]
    return parts[0] + parts[1] + parts[2]


def gather_body(owner_ref, table_ref, pool_ref, *refs, lists, kv_heads, cap):
    outs = refs[:-4]
    staged, slots, sem_in, sem_out = refs[-4:]
    owner = owner_ref[0]
    pair = owner >> 1
    slot_count = pool_ref.shape[0]
    base = owner * slot_count
    width = table_ref.shape[1]

    def look(j, found):
        following = []
        for at, which in enumerate(lists):
            slot = table_ref[pair ^ which, j] - base
            slots[at * (cap + 1) + jnp.minimum(found[at], cap)] = slot
            held = (slot >= 0) & (slot < slot_count)
            following.append(found[at] + held.astype(jnp.int32))
        return tuple(following)

    found = lax.fori_loop(0, width, look, (jnp.int32(0),) * len(lists), unroll=4)
    arriving = []
    for at in range(len(lists)):
        for k in range(kv_heads):
            for i in range(cap):
                slot = jnp.where(i < found[at], slots[at * (cap + 1) + i], 0)
                copy = pltpu.make_async_copy(
                    pool_ref.at[slot, :, k], staged.at[at, k, i], sem_in.at[at, k, i]
                )
                copy.start()
                arriving.append(copy)
    leaving = []
    for at in range(len(lists)):
        for k in range(kv_heads):
            for i in range(cap):
                arriving[(at * kv_heads + k) * cap + i].wait()
            copy = pltpu.make_async_copy(
                staged.at[at, k], outs[at * kv_heads + k].at[0], sem_out.at[at, k]
            )
            copy.start()
            leaving.append(copy)
    for copy in leaving:
        copy.wait()


def gather_pages(owner, table, pool, lists, cap):
    _, pair_of, kv_heads, page_len, head_dim = pool.shape
    shape = pltpu.HBM((1, cap, pair_of, page_len, head_dim), pool.dtype)
    count = len(lists) * kv_heads
    outs = pl.pallas_call(
        functools.partial(gather_body, lists=lists, kv_heads=kv_heads, cap=cap),
        out_shape=[shape] * count,
        grid_spec=pltpu.PrefetchScalarGridSpec(
            num_scalar_prefetch=2,
            grid=(1,),
            in_specs=[pl.BlockSpec(memory_space=pltpu.HBM)],
            out_specs=[pl.BlockSpec(memory_space=pltpu.HBM)] * count,
            scratch_shapes=[
                pltpu.VMEM((len(lists), kv_heads, cap, pair_of, page_len, head_dim), pool.dtype),
                pltpu.SMEM((len(lists) * (cap + 1),), jnp.int32),
                pltpu.SemaphoreType.DMA((len(lists), kv_heads, cap)),
                pltpu.SemaphoreType.DMA((len(lists), kv_heads)),
            ],
        ),
        compiler_params=pltpu.CompilerParams(vmem_limit_bytes=kernel_bytes),
        name="gather_pages",
    )(owner, pltpu.with_memory_space_constraint(table, pltpu.HBM), pltpu.with_memory_space_constraint(pool, pltpu.HBM))
    return [outs[i * kv_heads : (i + 1) * kv_heads] for i in range(len(lists))]


def attend_body(
    owner_ref,
    seen_ref,
    fresh_ref,
    *refs,
    halves,
    seen_at,
    has_page,
    has_prev,
    packed,
    step_rows,
    tile_rows,
    group,
    scale,
    copies_pool,
    waits,
    page_at,
):
    refs = list(refs)
    q_refs = [refs.pop(0) for _ in range(halves)]
    kv_refs = [refs.pop(0) for _ in seen_at]
    page_ref = refs.pop(0) if has_page else None
    prev_refs = [(refs.pop(0), refs.pop(0)) for _ in range(halves)] if has_prev else None
    pool_ref = refs.pop(0) if copies_pool else None
    del refs[:waits]
    out_refs = []
    for h in range(halves):
        out_refs.append((refs.pop(0),) if packed[h] else (refs.pop(0), refs.pop(0)))
    new_pool = refs.pop(0) if copies_pool else None
    wide_values = refs.pop(0)
    tables = [refs.pop(0) if packed[h] else out_refs[h][1].at[0] for h in range(halves)]
    if copies_pool:
        staged, sem_in, sem_out = refs
    head = pl.program_id(0)
    step = pl.program_id(1)
    heads = pl.num_programs(0)
    steps = pl.num_programs(1)
    owner = owner_ref[0]
    half = 1 - ((owner & 1) ^ ((owner >> 1) & 1))
    page_len = kv_refs[0].shape[3]
    keys = [ref.shape[1] * page_len for ref in kv_refs]

    if copies_pool:

        @pl.when((head == 0) & (step == 0))
        def _():
            pltpu.make_async_copy(pool_ref, staged, sem_in).start()

        @pl.when((head == 0) & (step == jnp.minimum(1, steps - 1)))
        def _():
            pltpu.make_async_copy(pool_ref, staged, sem_in).wait()
            staged[fresh_ref[owner] - owner * staged.shape[0]] = page_ref[...]
            pltpu.make_async_copy(staged, new_pool, sem_out).start()

    @pl.when(step == 0)
    def _():
        ones = jnp.ones((page_len, lanes), jnp.bfloat16)
        begin = 0
        for ref in kv_refs:
            for p in range(ref.shape[1]):
                wide_values[begin : begin + page_len, :lanes] = ref[0, p, 1]
                wide_values[begin : begin + page_len, lanes:] = ones
                begin += page_len
        if has_page:
            wide_values[begin : begin + page_len, :lanes] = page_ref[1, page_at]
            wide_values[begin : begin + page_len, lanes:] = ones

    eye = diagonal()
    limits = []
    for s, at in enumerate(seen_at):
        position = lax.broadcasted_iota(jnp.int32, (1, keys[s]), 1)
        limit = jnp.where(position < seen_ref[at[0], at[1]], jnp.inf, hidden_score)
        limits.append(limit.astype(jnp.float32))

    def score(h, t):
        query = q_refs[h][0, t * tile_rows : (t + 1) * tile_rows]
        scores = []
        for s, ref in enumerate(kv_refs):
            key_rows = ref[0, :, 0].reshape(keys[s], lanes)
            product = lax.dot_general(
                query, key_rows, (((1,), (1,)), ((), ())), preferred_element_type=jnp.float32
            )
            scores.append(jnp.minimum(product, limits[s]))
        if has_page:
            product = lax.dot_general(
                query, page_ref[0, page_at], (((1,), (1,)), ((), ())), preferred_element_type=jnp.float32
            )
            key_at = lax.broadcasted_iota(jnp.int32, product.shape, 1)
            if h == 0:
                row_at = lax.broadcasted_iota(jnp.int32, product.shape, 0)
                token = (step * step_rows + t * tile_rows + row_at) // group
                shown = key_at <= token
            else:
                shown = key_at < jnp.where(half == 0, page_len, 0)
            scores.append(jnp.where(shown, product, hidden_score))
        return scores

    def finish(h, t, scores):
        top = jnp.full((tile_rows, 1), lowest_top, jnp.float32)
        for part in scores:
            top = jnp.maximum(top, jnp.max(part, axis=1, keepdims=True))
        scaled_top = top * scale
        weights = [jnp.exp2(part * scale - scaled_top).astype(jnp.bfloat16) for part in scores]
        mixed = jnp.dot(
            jnp.concatenate(weights, axis=1), wide_values[...], preferred_element_type=jnp.float32
        )
        total = mixed[:, lanes:]
        mixed = mixed[:, :lanes]
        first = step * (step_rows // block_rows) + t * (tile_rows // block_rows)
        count = tables[h].shape[0] // 2
        for u in range(tile_rows // block_rows):
            inner = slice(u * block_rows, (u + 1) * block_rows)
            outer = slice(t * tile_rows + u * block_rows, t * tile_rows + (u + 1) * block_rows)
            part_top, part_total, part_mixed = top[inner], total[inner], mixed[inner]
            row = first + u
            if has_prev:
                prev_mixed, prev_table = prev_refs[h]
                prev_top = as_column(prev_table[0, pl.ds(row, 1)], eye)
                prev_total = as_column(prev_table[0, pl.ds(count + row, 1)], eye)
                joint = jnp.maximum(part_top, prev_top)
                keep = jnp.exp2((part_top - joint) * scale)
                keep_prev = jnp.exp2((prev_top - joint) * scale)
                part_mixed = part_mixed * keep + prev_mixed[0, outer] * keep_prev
                part_total = part_total * keep + prev_total * keep_prev
                part_top = joint
            tables[h][pl.ds(row, 1)] = as_row(part_top, eye)
            tables[h][pl.ds(count + row, 1)] = as_row(part_total, eye)
            if packed[h]:
                at = pl.multiple_of(row * block_rows, block_rows)
                out_refs[h][0][0, pl.ds(at, block_rows)] = part_mixed.astype(jnp.bfloat16)
            else:
                out_refs[h][0][0, outer] = part_mixed

    chains = [(h, t) for t in range(step_rows // tile_rows) for h in range(halves)]
    scores = score(*chains[0])
    for i, chain in enumerate(chains):
        following = score(*chains[i + 1]) if i + 1 < len(chains) else None
        finish(*chain, scores)
        scores = following

    @pl.when(step == steps - 1)
    def _():
        for h in range(halves):
            if packed[h]:
                size = tables[h].shape[0]
                begin = out_refs[h][0].shape[1] - 3 * size
                for i, part in enumerate(in_three(tables[h][...])):
                    out_refs[h][0][0, begin + i * size : begin + (i + 1) * size] = part

    if copies_pool:

        @pl.when((head == heads - 1) & (step == steps - 1))
        def _():
            pltpu.make_async_copy(staged, new_pool, sem_out).wait()


def attend(
    scalars, queries, sources, seen_at, packed, scale, group, heads, page=None, prev=None, pool=None, after=()
):
    halves = len(queries)
    rows = queries[0][0].shape[1]
    size = 2 * (rows // block_rows)
    step_rows = min(rows, 1024 // halves)
    tile_rows = min(step_rows, 256)
    key_count = sum(s.shape[1] * s.shape[3] for s, _ in sources)

    def per_rows(offset):
        return pl.BlockSpec((1, step_rows, lanes), lambda k, i, *_: (k + offset, i, 0))

    def per_head(array, offset):
        tail = array.shape[1:]
        return pl.BlockSpec((1, *tail), lambda k, i, *_: (k + offset,) + (0,) * len(tail))

    anywhere = pl.BlockSpec(memory_space=pl.ANY)
    args = [q for q, _ in queries] + [s for s, _ in sources]
    in_specs = [per_rows(at) for _, at in queries] + [per_head(s, at) for s, at in sources]
    page_at = 0
    if page is not None:
        page, page_at = page
        args.append(page)
        in_specs.append(whole(page))
        key_count += page.shape[2]
    if prev is not None:
        for mixed, table, at in prev:
            args += [mixed, table]
            in_specs += [per_rows(at), per_head(table, at)]
    if pool is not None:
        args.append(pltpu.with_memory_space_constraint(pool, pltpu.HBM))
        in_specs.append(pl.BlockSpec(memory_space=pltpu.HBM))
    args += list(after)
    in_specs += [anywhere] * len(after)
    out_shape = []
    out_specs = []
    scratch = [pltpu.VMEM((key_count, 2 * lanes), jnp.bfloat16)]
    for h in range(halves):
        if packed[h]:
            shape = jax.ShapeDtypeStruct((heads, rows + 3 * size, lanes), jnp.bfloat16)
            out_shape.append(shape)
            out_specs.append(per_head(shape, 0))
            scratch.append(pltpu.VMEM((size, lanes), jnp.float32))
        else:
            table = jax.ShapeDtypeStruct((heads, size, lanes), jnp.float32)
            out_shape += [jax.ShapeDtypeStruct((heads, rows, lanes), jnp.float32), table]
            out_specs += [per_rows(0), per_head(table, 0)]
    if pool is not None:
        out_shape.append(jax.ShapeDtypeStruct(pool.shape, pool.dtype))
        out_specs.append(pl.BlockSpec(memory_space=pltpu.HBM))
        scratch.append(pltpu.VMEM(pool.shape, pool.dtype))
        scratch += [pltpu.SemaphoreType.DMA, pltpu.SemaphoreType.DMA]
    work = halves * heads * rows * key_count
    return pl.pallas_call(
        functools.partial(
            attend_body,
            halves=halves,
            seen_at=seen_at,
            has_page=page is not None,
            has_prev=prev is not None,
            packed=packed,
            step_rows=step_rows,
            tile_rows=tile_rows,
            group=group,
            scale=scale,
            copies_pool=pool is not None,
            waits=len(after),
            page_at=page_at,
        ),
        out_shape=out_shape,
        grid_spec=pltpu.PrefetchScalarGridSpec(
            num_scalar_prefetch=3,
            grid=(heads, rows // step_rows),
            in_specs=in_specs,
            out_specs=out_specs,
            scratch_shapes=scratch,
        ),
        cost_estimate=pl.CostEstimate(
            flops=4 * work * lanes,
            transcendentals=work,
            bytes_accessed=4 * heads * key_count * lanes,
        ),
        compiler_params=pltpu.CompilerParams(vmem_limit_bytes=kernel_bytes),
        name="attend",
    )(*scalars, *args)


def join_body(own_mixed, own_table, *refs, scale, packs, waits):
    refs = list(refs)
    out_ref = refs.pop()
    if waits:
        del refs[-waits:]
    size = own_table.shape[1]
    count = size // 2
    rows = count * block_rows
    eye = diagonal()
    tops = [own_table[0, :count]]
    totals = [own_table[0, count:]]
    for ref in refs:
        table = from_three(ref, rows, size)
        tops.append(table[:count])
        totals.append(table[count:])
    top = functools.reduce(jnp.maximum, tops)
    keeps = [jnp.exp2((t - top) * scale) for t in tops]
    total = sum(t * keep for t, keep in zip(totals, keeps))
    if not packs:
        keeps = [keep / total for keep in keeps]
    for t in range(count):
        at = slice(t * block_rows, (t + 1) * block_rows)
        mixed = own_mixed[0, at] * as_column(keeps[0][t : t + 1], eye)
        for ref, keep in zip(refs, keeps[1:]):
            mixed = mixed + ref[0, at].astype(jnp.float32) * as_column(keep[t : t + 1], eye)
        if packs:
            out_ref[0, at] = mixed.astype(jnp.bfloat16)
        else:
            heads = out_ref.shape[1]
            tokens = block_rows // heads
            shaped = mixed.reshape(tokens, heads, lanes)
            out_ref[t * tokens : (t + 1) * tokens] = shaped.astype(jnp.bfloat16)
    if packs:
        table = jnp.concatenate([top, total], axis=0)
        for i, part in enumerate(in_three(table)):
            out_ref[0, rows + i * size : rows + (i + 1) * size] = part


def join_packed(own, received, scale, after=()):
    mixed, table = own
    args = [mixed, table, received]
    return pl.pallas_call(
        functools.partial(join_body, scale=scale, packs=True, waits=len(after)),
        out_shape=jax.ShapeDtypeStruct(received.shape, received.dtype),
        grid=(1,),
        in_specs=[whole(a) for a in args] + [pl.BlockSpec(memory_space=pl.ANY)] * len(after),
        out_specs=whole(received),
        compiler_params=pltpu.CompilerParams(vmem_limit_bytes=kernel_bytes),
        name="join_packed",
    )(*args, *after)


def join_out(own, received, target, shape, index, group, scale):
    mixed, table = own
    args = [mixed, table, *received]
    in_specs = [whole(a) for a in args]
    aliases = {}
    if target is not None:
        aliases = {len(args): 0}
        args.append(target)
        in_specs.append(pl.BlockSpec(memory_space=pl.ANY))
    return pl.pallas_call(
        functools.partial(join_body, scale=scale, packs=False, waits=len(aliases)),
        out_shape=jax.ShapeDtypeStruct(shape, jnp.bfloat16),
        grid=(1,),
        in_specs=in_specs,
        out_specs=pl.BlockSpec((shape[0], group, shape[2]), lambda i: (0, index, 0)),
        input_output_aliases=aliases,
        compiler_params=pltpu.CompilerParams(vmem_limit_bytes=kernel_bytes),
        name="join_out",
    )(*args)


def visible_counts(table, lengths, owner, steps, slot_count, page_len):
    requests, width = table.shape
    holders = owner ^ (2 * jnp.arange(steps, dtype=jnp.int32))
    chosen = (owner >> 1) ^ (jnp.arange(2, dtype=jnp.int32) * steps)
    column = jnp.arange(width, dtype=jnp.int32)
    count = jnp.clip(lengths[:, None] - column[None, :] * page_len, 0, page_len)
    first = holders[None, :, None, None] * slot_count
    entry = table[None, None]
    held = (entry >= first) & (entry < first + slot_count)
    asked = jnp.arange(requests, dtype=jnp.int32)[None, :] == chosen[:, None]
    picked = held & asked[:, None, :, None]
    return jnp.sum(jnp.where(picked, count[None, None], 0), axis=(2, 3))


def on_device(queries, new_kv, pool, block_table, prefix_len, new_slots):
    owner_count = lax.axis_size("pool")
    owner = lax.axis_index("pool").astype(jnp.int32)
    slot_count, _, kv_heads, page_len, head_dim = pool.shape
    tokens, q_heads, _ = queries.shape
    group = q_heads // kv_heads
    rows = tokens * group
    pairs = owner_count // 2
    near = pairs // 2
    cap = block_table.shape[1] // owner_count
    scale = head_dim**-0.5 * log2_e
    each = range(kv_heads)

    split = [
        queries[:, k * group : (k + 1) * group].reshape(1, rows, head_dim) for k in each
    ]
    far_own = [moved(split[k], pairs) for k in each]
    other = [moved(split[k], 1) for k in each]
    owner_list = jnp.full((1,), owner, jnp.int32)
    far_lists = [near + k for k in range(1, near)]
    sent_far = gather_pages(owner_list, block_table, pool, far_lists, cap)
    rest_lists = list(range(1, near)) + [0, near]
    pages = gather_pages(owner_list, block_table, pool, rest_lists, cap)

    def exchanged(sent):
        return [[moved(sent[i][k], 2 * (i + 1)) for i in range(near - 1)] for k in each]

    got_far = exchanged(sent_far)
    got_near = exchanged(pages)
    local, local_far = pages[near - 1 :]
    seen = visible_counts(block_table, prefix_len, owner, near, slot_count, page_len)
    scalars = (owner_list, seen, new_slots)
    new_page = new_kv.transpose(1, 2, 0, 3)

    started = []
    updated = None
    after = []
    for k in each:
        results = attend(
            scalars,
            [(split[k], 0), (other[k], 0)],
            [(local[k], 0)],
            [(0, 0)],
            (False, False),
            scale,
            group,
            1,
            page=(new_page, k),
            pool=pool if k == 0 else None,
            after=after,
        )
        if k == 0:
            updated = results[4]
        started.append(results[:4])
        after = [results[1]]
    far_other = [moved(far_own[k], 1) for k in each]
    far = []
    for k in each:
        results = attend(
            scalars,
            [(far_own[k], 0), (far_other[k], 0)],
            [(local_far[k], 0)] + [(a, 0) for a in got_far[k]],
            [(1, i) for i in range(near)],
            (False, True),
            scale,
            group,
            1,
            after=after,
        )
        far.append((results[:2], moved(results[2], 1)))
        after = [results[1]]
    back = []
    ready = []
    for k in each:
        joined = join_packed(*far[k], scale, after=after)
        back.append(moved(joined, pairs))
        mine, mine_table, theirs, theirs_table = started[k]
        near_keys = [(a, 0) for a in got_near[k]]
        near_at = [(0, i) for i in range(1, near)]
        mine, theirs = (mine, mine_table, 0), (theirs, theirs_table, 0)
        if k + 1 < kv_heads:
            results = attend(
                scalars,
                [(split[k], 0), (other[k], 0)],
                near_keys,
                near_at,
                (False, True),
                scale,
                group,
                1,
                prev=[mine, theirs],
                after=[joined],
            )
            own_part = results[:2]
            other_part = results[2]
        else:
            (other_part,) = attend(
                scalars,
                [(other[k], 0)],
                near_keys,
                near_at,
                (True,),
                scale,
                group,
                1,
                prev=[theirs],
                after=[joined],
            )
            own_part = attend(
                scalars,
                [(split[k], 0)],
                near_keys,
                near_at,
                (False,),
                scale,
                group,
                1,
                prev=[mine],
                after=[other_part],
            )
        ready.append((own_part, moved(other_part, 1)))
        after = [own_part[1]]
    attended = None
    for k in each:
        own, received = ready[k]
        attended = join_out(
            own, [received, back[k]], attended, queries.shape, k, group, scale
        )
    return (attended, updated)


def solution(mesh):
    placed = (
        P(("groups", "pool"), "head", None),
        P(("groups", "pool"), None, "head", None),
        P(("groups", "pool"), None, "head", None, None),
        P("groups", None),
        P("groups"),
        P("groups"),
    )

    return jax.shard_map(
        on_device,
        mesh=mesh,
        in_specs=placed,
        out_specs=(
            P(("groups", "pool"), "head", None),
            P(("groups", "pool"), None, "head", None, None),
        ),
        check_vma=False,
    )
```

```python
import functools

import jax
import jax.numpy as jnp
from jax import lax
from jax.experimental import pallas as pl
from jax.experimental.pallas import tpu as pltpu
from jax.sharding import PartitionSpec as P


log2_e = 1.4426950408889634
hidden_score = -2e30
lowest_top = -1e30
lanes = 128
block_rows = 128
kernel_bytes = 24 << 20


def moved(array, apart):
    count = lax.axis_size("pool")
    return lax.ppermute(array, "pool", [(i, i ^ apart) for i in range(count)])


def whole(array):
    return pl.BlockSpec(array.shape, lambda i, *_: (0,) * len(array.shape))


def diagonal():
    shape = (lanes, lanes)
    return lax.broadcasted_iota(jnp.int32, shape, 0) == lax.broadcasted_iota(jnp.int32, shape, 1)


def as_row(column, eye):
    spread = jnp.where(eye, jnp.broadcast_to(column, (lanes, lanes)), 0.0)
    return jnp.sum(spread, axis=0, keepdims=True)


def as_column(row, eye):
    spread = jnp.where(eye, jnp.broadcast_to(row, (lanes, lanes)), 0.0)
    return jnp.sum(spread, axis=1, keepdims=True)


def in_three(values):
    high = values.astype(jnp.bfloat16)
    rest = values - high.astype(jnp.float32)
    middle = rest.astype(jnp.bfloat16)
    low = (rest - middle.astype(jnp.float32)).astype(jnp.bfloat16)
    return (high, middle, low)


def from_three(ref, begin, count):
    parts = [
        ref[0, begin + i * count : begin + (i + 1) * count].astype(jnp.float32) for i in range(3)
    ]
    return parts[0] + parts[1] + parts[2]


def gather_body(owner_ref, table_ref, pool_ref, *refs, lists, resident, kv_heads, cap):
    outs = refs[: len(lists) * kv_heads]
    staged = refs[len(lists) * kv_heads] if resident < len(lists) else None
    slots, sem, sem_out = refs[-3:]
    owner = owner_ref[0]
    pair = owner >> 1
    slot_count = pool_ref.shape[0]
    base = owner * slot_count
    width = table_ref.shape[1]

    def look(j, found):
        following = []
        for at, which in enumerate(lists):
            slot = table_ref[pair ^ which, j] - base
            slots[at * (cap + 1) + jnp.minimum(found[at], cap)] = slot
            held = (slot >= 0) & (slot < slot_count)
            following.append(found[at] + held.astype(jnp.int32))
        return tuple(following)

    found = lax.fori_loop(0, width, look, (jnp.int32(0),) * len(lists), unroll=16)
    arriving = {}
    for at in reversed(range(len(lists))):
        for k in range(kv_heads):
            out = outs[at * kv_heads + k].at[0] if at < resident else staged.at[at - resident, k]
            arriving[at, k] = []
            for i in range(cap):
                slot = jnp.where(i < found[at], slots[at * (cap + 1) + i], 0)
                copy = pltpu.make_async_copy(
                    pool_ref.at[slot, :, k], out.at[i], sem.at[at, k, i]
                )
                copy.start()
                arriving[at, k].append(copy)
    leaving = []
    for (at, k), copies in arriving.items():
        for copy in copies:
            copy.wait()
        if at >= resident:
            copy = pltpu.make_async_copy(
                staged.at[at - resident, k], outs[at * kv_heads + k].at[0], sem_out.at[at, k]
            )
            copy.start()
            leaving.append(copy)
    for copy in leaving:
        copy.wait()


def gather_pages(owner, table, pool, lists, resident, cap):
    _, pair_of, kv_heads, page_len, head_dim = pool.shape
    outs = []
    specs = []
    for at in range(len(lists)):
        space = pltpu.VMEM if at < resident else pltpu.HBM
        outs += [space((1, cap, pair_of, page_len, head_dim), pool.dtype)] * kv_heads
        specs += [pl.BlockSpec(memory_space=space)] * kv_heads
    scratch = []
    if resident < len(lists):
        size = (len(lists) - resident, kv_heads, cap, pair_of, page_len, head_dim)
        scratch.append(pltpu.VMEM(size, pool.dtype))
    pages = pl.pallas_call(
        functools.partial(
            gather_body, lists=lists, resident=resident, kv_heads=kv_heads, cap=cap
        ),
        out_shape=outs,
        grid_spec=pltpu.PrefetchScalarGridSpec(
            num_scalar_prefetch=2,
            grid=(1,),
            in_specs=[pl.BlockSpec(memory_space=pltpu.HBM)],
            out_specs=specs,
            scratch_shapes=scratch
            + [
                pltpu.SMEM((len(lists) * (cap + 1),), jnp.int32),
                pltpu.SemaphoreType.DMA((len(lists), kv_heads, cap)),
                pltpu.SemaphoreType.DMA((len(lists), kv_heads)),
            ],
        ),
        compiler_params=pltpu.CompilerParams(vmem_limit_bytes=kernel_bytes),
        name="gather_pages",
    )(
        owner,
        pltpu.with_memory_space_constraint(table, pltpu.HBM),
        pltpu.with_memory_space_constraint(pool, pltpu.HBM),
    )
    return [pages[i * kv_heads : (i + 1) * kv_heads] for i in range(len(lists))]


def attend_body(
    owner_ref,
    seen_ref,
    fresh_ref,
    *refs,
    halves,
    seen_at,
    has_page,
    has_prev,
    packed,
    step_rows,
    tile_rows,
    group,
    scale,
    copies_pool,
    waits,
    page_at,
):
    refs = list(refs)
    q_refs = [refs.pop(0) for _ in range(halves)]
    kv_refs = [refs.pop(0) for _ in seen_at]
    page_ref = refs.pop(0) if has_page else None
    prev_refs = [(refs.pop(0), refs.pop(0)) for _ in range(halves)] if has_prev else None
    pool_ref = refs.pop(0) if copies_pool else None
    del refs[:waits]
    out_refs = []
    for h in range(halves):
        out_refs.append((refs.pop(0),) if packed[h] else (refs.pop(0), refs.pop(0)))
    new_pool = refs.pop(0) if copies_pool else None
    wide_values = refs.pop(0)
    tables = [refs.pop(0) if packed[h] else out_refs[h][1].at[0] for h in range(halves)]
    if copies_pool:
        staged, sem_in, sem_out = refs
    head = pl.program_id(0)
    step = pl.program_id(1)
    heads = pl.num_programs(0)
    steps = pl.num_programs(1)
    owner = owner_ref[0]
    half = 1 - ((owner & 1) ^ ((owner >> 1) & 1))
    page_len = kv_refs[0].shape[3]
    keys = [ref.shape[1] * page_len for ref in kv_refs]

    if copies_pool:

        @pl.when((head == 0) & (step == 0))
        def _():
            pltpu.make_async_copy(pool_ref, staged, sem_in).start()

        @pl.when((head == 0) & (step == jnp.minimum(1, steps - 1)))
        def _():
            pltpu.make_async_copy(pool_ref, staged, sem_in).wait()
            staged[fresh_ref[owner] - owner * staged.shape[0]] = page_ref[...]
            pltpu.make_async_copy(staged, new_pool, sem_out).start()

    @pl.when(step == 0)
    def _():
        ones = jnp.ones((page_len, lanes), jnp.bfloat16)
        begin = 0
        for ref in kv_refs:
            for p in range(ref.shape[1]):
                wide_values[begin : begin + page_len, :lanes] = ref[0, p, 1]
                wide_values[begin : begin + page_len, lanes:] = ones
                begin += page_len
        if has_page:
            wide_values[begin : begin + page_len, :lanes] = page_ref[1, page_at]
            wide_values[begin : begin + page_len, lanes:] = ones

    eye = diagonal()
    limits = []
    for s, at in enumerate(seen_at):
        position = lax.broadcasted_iota(jnp.int32, (1, keys[s]), 1)
        limit = jnp.where(position < seen_ref[at[0], at[1]], jnp.inf, hidden_score)
        limits.append(limit.astype(jnp.float32))

    def score(h, t):
        query = q_refs[h][0, t * tile_rows : (t + 1) * tile_rows]
        scores = []
        for s, ref in enumerate(kv_refs):
            key_rows = ref[0, :, 0].reshape(keys[s], lanes)
            product = lax.dot_general(
                query, key_rows, (((1,), (1,)), ((), ())), preferred_element_type=jnp.float32
            )
            scores.append(jnp.minimum(product, limits[s]))
        if has_page:
            product = lax.dot_general(
                query, page_ref[0, page_at], (((1,), (1,)), ((), ())), preferred_element_type=jnp.float32
            )
            key_at = lax.broadcasted_iota(jnp.int32, product.shape, 1)
            if h == 0:
                row_at = lax.broadcasted_iota(jnp.int32, product.shape, 0)
                token = (step * step_rows + t * tile_rows + row_at) // group
                shown = key_at <= token
            else:
                shown = key_at < jnp.where(half == 0, page_len, 0)
            scores.append(jnp.where(shown, product, hidden_score))
        return scores

    def finish(h, t, scores):
        top = jnp.full((tile_rows, 1), lowest_top, jnp.float32)
        for part in scores:
            top = jnp.maximum(top, jnp.max(part, axis=1, keepdims=True))
        scaled_top = top * scale
        weights = [jnp.exp2(part * scale - scaled_top).astype(jnp.bfloat16) for part in scores]
        mixed = jnp.dot(
            jnp.concatenate(weights, axis=1), wide_values[...], preferred_element_type=jnp.float32
        )
        total = mixed[:, lanes:]
        mixed = mixed[:, :lanes]
        first = step * (step_rows // block_rows) + t * (tile_rows // block_rows)
        count = tables[h].shape[0] // 2
        for u in range(tile_rows // block_rows):
            inner = slice(u * block_rows, (u + 1) * block_rows)
            outer = slice(t * tile_rows + u * block_rows, t * tile_rows + (u + 1) * block_rows)
            part_top, part_total, part_mixed = top[inner], total[inner], mixed[inner]
            row = first + u
            if has_prev:
                prev_mixed, prev_table = prev_refs[h]
                prev_top = as_column(prev_table[0, pl.ds(row, 1)], eye)
                prev_total = as_column(prev_table[0, pl.ds(count + row, 1)], eye)
                joint = jnp.maximum(part_top, prev_top)
                keep = jnp.exp2((part_top - joint) * scale)
                keep_prev = jnp.exp2((prev_top - joint) * scale)
                part_mixed = part_mixed * keep + prev_mixed[0, outer] * keep_prev
                part_total = part_total * keep + prev_total * keep_prev
                part_top = joint
            tables[h][pl.ds(row, 1)] = as_row(part_top, eye)
            tables[h][pl.ds(count + row, 1)] = as_row(part_total, eye)
            if packed[h]:
                at = pl.multiple_of(row * block_rows, block_rows)
                out_refs[h][0][0, pl.ds(at, block_rows)] = part_mixed.astype(jnp.bfloat16)
            else:
                out_refs[h][0][0, outer] = part_mixed

    chains = [(h, t) for t in range(step_rows // tile_rows) for h in range(halves)]
    scores = score(*chains[0])
    for i, chain in enumerate(chains):
        following = score(*chains[i + 1]) if i + 1 < len(chains) else None
        finish(*chain, scores)
        scores = following

    @pl.when(step == steps - 1)
    def _():
        for h in range(halves):
            if packed[h]:
                size = tables[h].shape[0]
                begin = out_refs[h][0].shape[1] - 3 * size
                for i, part in enumerate(in_three(tables[h][...])):
                    out_refs[h][0][0, begin + i * size : begin + (i + 1) * size] = part

    if copies_pool:

        @pl.when((head == heads - 1) & (step == steps - 1))
        def _():
            pltpu.make_async_copy(staged, new_pool, sem_out).wait()


def attend(
    scalars, queries, sources, seen_at, packed, scale, group, heads, page=None, prev=None, pool=None, after=()
):
    halves = len(queries)
    rows = queries[0][0].shape[1]
    size = 2 * (rows // block_rows)
    step_rows = min(rows, 1024 // halves)
    tile_rows = min(step_rows, 256)
    key_count = sum(s.shape[1] * s.shape[3] for s, _ in sources)

    def per_rows(offset):
        return pl.BlockSpec((1, step_rows, lanes), lambda k, i, *_: (k + offset, i, 0))

    def per_head(array, offset):
        tail = array.shape[1:]
        return pl.BlockSpec((1, *tail), lambda k, i, *_: (k + offset,) + (0,) * len(tail))

    anywhere = pl.BlockSpec(memory_space=pl.ANY)
    args = [q for q, _ in queries] + [s for s, _ in sources]
    in_specs = [per_rows(at) for _, at in queries] + [per_head(s, at) for s, at in sources]
    page_at = 0
    if page is not None:
        page, page_at = page
        args.append(page)
        in_specs.append(whole(page))
        key_count += page.shape[2]
    if prev is not None:
        for mixed, table, at in prev:
            args += [mixed, table]
            in_specs += [per_rows(at), per_head(table, at)]
    if pool is not None:
        args.append(pltpu.with_memory_space_constraint(pool, pltpu.HBM))
        in_specs.append(pl.BlockSpec(memory_space=pltpu.HBM))
    args += list(after)
    in_specs += [anywhere] * len(after)
    out_shape = []
    out_specs = []
    scratch = [pltpu.VMEM((key_count, 2 * lanes), jnp.bfloat16)]
    for h in range(halves):
        if packed[h]:
            shape = jax.ShapeDtypeStruct((heads, rows + 3 * size, lanes), jnp.bfloat16)
            out_shape.append(shape)
            out_specs.append(per_head(shape, 0))
            scratch.append(pltpu.VMEM((size, lanes), jnp.float32))
        else:
            table = jax.ShapeDtypeStruct((heads, size, lanes), jnp.float32)
            out_shape += [jax.ShapeDtypeStruct((heads, rows, lanes), jnp.float32), table]
            out_specs += [per_rows(0), per_head(table, 0)]
    if pool is not None:
        out_shape.append(jax.ShapeDtypeStruct(pool.shape, pool.dtype))
        out_specs.append(pl.BlockSpec(memory_space=pltpu.HBM))
        scratch.append(pltpu.VMEM(pool.shape, pool.dtype))
        scratch += [pltpu.SemaphoreType.DMA, pltpu.SemaphoreType.DMA]
    work = halves * heads * rows * key_count
    return pl.pallas_call(
        functools.partial(
            attend_body,
            halves=halves,
            seen_at=seen_at,
            has_page=page is not None,
            has_prev=prev is not None,
            packed=packed,
            step_rows=step_rows,
            tile_rows=tile_rows,
            group=group,
            scale=scale,
            copies_pool=pool is not None,
            waits=len(after),
            page_at=page_at,
        ),
        out_shape=out_shape,
        grid_spec=pltpu.PrefetchScalarGridSpec(
            num_scalar_prefetch=3,
            grid=(heads, rows // step_rows),
            in_specs=in_specs,
            out_specs=out_specs,
            scratch_shapes=scratch,
        ),
        cost_estimate=pl.CostEstimate(
            flops=4 * work * lanes,
            transcendentals=work,
            bytes_accessed=4 * heads * key_count * lanes,
        ),
        compiler_params=pltpu.CompilerParams(vmem_limit_bytes=kernel_bytes),
        name="attend",
    )(*scalars, *args)


def join_body(own_mixed, own_table, *refs, scale, packs, waits):
    refs = list(refs)
    out_ref = refs.pop()
    if waits:
        del refs[-waits:]
    size = own_table.shape[1]
    count = size // 2
    rows = count * block_rows
    eye = diagonal()
    tops = [own_table[0, :count]]
    totals = [own_table[0, count:]]
    for ref in refs:
        table = from_three(ref, rows, size)
        tops.append(table[:count])
        totals.append(table[count:])
    top = functools.reduce(jnp.maximum, tops)
    keeps = [jnp.exp2((t - top) * scale) for t in tops]
    total = sum(t * keep for t, keep in zip(totals, keeps))
    if not packs:
        keeps = [keep / total for keep in keeps]
    for t in range(count):
        at = slice(t * block_rows, (t + 1) * block_rows)
        mixed = own_mixed[0, at] * as_column(keeps[0][t : t + 1], eye)
        for ref, keep in zip(refs, keeps[1:]):
            mixed = mixed + ref[0, at].astype(jnp.float32) * as_column(keep[t : t + 1], eye)
        if packs:
            out_ref[0, at] = mixed.astype(jnp.bfloat16)
        else:
            heads = out_ref.shape[1]
            tokens = block_rows // heads
            shaped = mixed.reshape(tokens, heads, lanes)
            out_ref[t * tokens : (t + 1) * tokens] = shaped.astype(jnp.bfloat16)
    if packs:
        table = jnp.concatenate([top, total], axis=0)
        for i, part in enumerate(in_three(table)):
            out_ref[0, rows + i * size : rows + (i + 1) * size] = part


def join_packed(own, received, scale, after=()):
    mixed, table = own
    args = [mixed, table, received]
    return pl.pallas_call(
        functools.partial(join_body, scale=scale, packs=True, waits=len(after)),
        out_shape=jax.ShapeDtypeStruct(received.shape, received.dtype),
        grid=(1,),
        in_specs=[whole(a) for a in args] + [pl.BlockSpec(memory_space=pl.ANY)] * len(after),
        out_specs=whole(received),
        compiler_params=pltpu.CompilerParams(vmem_limit_bytes=kernel_bytes),
        name="join_packed",
    )(*args, *after)


def join_out(own, received, target, shape, index, group, scale):
    mixed, table = own
    args = [mixed, table, *received]
    in_specs = [whole(a) for a in args]
    aliases = {}
    if target is not None:
        aliases = {len(args): 0}
        args.append(target)
        in_specs.append(pl.BlockSpec(memory_space=pl.ANY))
    return pl.pallas_call(
        functools.partial(join_body, scale=scale, packs=False, waits=len(aliases)),
        out_shape=jax.ShapeDtypeStruct(shape, jnp.bfloat16),
        grid=(1,),
        in_specs=in_specs,
        out_specs=pl.BlockSpec((shape[0], group, shape[2]), lambda i: (0, index, 0)),
        input_output_aliases=aliases,
        compiler_params=pltpu.CompilerParams(vmem_limit_bytes=kernel_bytes),
        name="join_out",
    )(*args)


def visible_counts(table, lengths, owner, steps, slot_count, page_len):
    requests, width = table.shape
    holders = owner ^ (2 * jnp.arange(steps, dtype=jnp.int32))
    chosen = (owner >> 1) ^ (jnp.arange(2, dtype=jnp.int32) * steps)
    column = jnp.arange(width, dtype=jnp.int32)
    count = jnp.clip(lengths[:, None] - column[None, :] * page_len, 0, page_len)
    first = holders[None, :, None, None] * slot_count
    entry = table[None, None]
    held = (entry >= first) & (entry < first + slot_count)
    asked = jnp.arange(requests, dtype=jnp.int32)[None, :] == chosen[:, None]
    picked = held & asked[:, None, :, None]
    return jnp.sum(jnp.where(picked, count[None, None], 0), axis=(2, 3))


def on_device(queries, new_kv, pool, block_table, prefix_len, new_slots):
    owner_count = lax.axis_size("pool")
    owner = lax.axis_index("pool").astype(jnp.int32)
    slot_count, _, kv_heads, page_len, head_dim = pool.shape
    tokens, q_heads, _ = queries.shape
    group = q_heads // kv_heads
    rows = tokens * group
    pairs = owner_count // 2
    near = pairs // 2
    cap = block_table.shape[1] // owner_count
    scale = head_dim**-0.5 * log2_e
    each = range(kv_heads)

    split = [
        queries[:, k * group : (k + 1) * group].reshape(1, rows, head_dim) for k in each
    ]
    far_own = [moved(split[k], pairs) for k in each]
    other = [moved(split[k], 1) for k in each]
    owner_list = jnp.full((1,), owner, jnp.int32)
    far_lists = [near + k for k in range(1, near)]
    sent_far = gather_pages(owner_list, block_table, pool, far_lists, near - 1, cap)
    rest_lists = list(range(1, near)) + [0, near]
    pages = gather_pages(owner_list, block_table, pool, rest_lists, near - 1, cap)

    def exchanged(sent):
        return [[moved(sent[i][k], 2 * (i + 1)) for i in range(near - 1)] for k in each]

    got_far = exchanged(sent_far)
    got_near = exchanged(pages)
    local, local_far = pages[near - 1 :]
    seen = visible_counts(block_table, prefix_len, owner, near, slot_count, page_len)
    scalars = (owner_list, seen, new_slots)
    new_page = new_kv.transpose(1, 2, 0, 3)

    started = []
    updated = None
    after = []
    for k in each:
        results = attend(
            scalars,
            [(split[k], 0), (other[k], 0)],
            [(local[k] if k else pltpu.with_memory_space_constraint(local[k], pltpu.HBM), 0)],
            [(0, 0)],
            (False, False),
            scale,
            group,
            1,
            page=(new_page, k),
            pool=pool if k == 0 else None,
            after=after,
        )
        if k == 0:
            updated = results[4]
        started.append(results[:4])
        after = [results[1]]
    far_other = [moved(far_own[k], 1) for k in each]
    far = []
    for k in each:
        results = attend(
            scalars,
            [(far_own[k], 0), (far_other[k], 0)],
            [(local_far[k], 0)] + [(a, 0) for a in got_far[k]],
            [(1, i) for i in range(near)],
            (False, True),
            scale,
            group,
            1,
            after=after,
        )
        far.append((results[:2], moved(results[2], 1)))
        after = [results[1]]
    back = []
    ready = []
    for k in each:
        joined = join_packed(*far[k], scale, after=after)
        back.append(moved(joined, pairs))
        mine, mine_table, theirs, theirs_table = started[k]
        near_keys = [(a, 0) for a in got_near[k]]
        near_at = [(0, i) for i in range(1, near)]
        mine, theirs = (mine, mine_table, 0), (theirs, theirs_table, 0)
        if k + 1 < kv_heads:
            results = attend(
                scalars,
                [(split[k], 0), (other[k], 0)],
                near_keys,
                near_at,
                (False, True),
                scale,
                group,
                1,
                prev=[mine, theirs],
                after=[joined],
            )
            own_part = results[:2]
            other_part = results[2]
        else:
            (other_part,) = attend(
                scalars,
                [(other[k], 0)],
                near_keys,
                near_at,
                (True,),
                scale,
                group,
                1,
                prev=[theirs],
                after=[joined],
            )
            own_part = attend(
                scalars,
                [(split[k], 0)],
                near_keys,
                near_at,
                (False,),
                scale,
                group,
                1,
                prev=[mine],
                after=[other_part],
            )
        ready.append((own_part, moved(other_part, 1)))
        after = [own_part[1]]
    attended = None
    for k in each:
        own, received = ready[k]
        attended = join_out(
            own, [received, back[k]], attended, queries.shape, k, group, scale
        )
    return (attended, updated)


def solution(mesh):
    placed = (
        P(("groups", "pool"), "head", None),
        P(("groups", "pool"), None, "head", None),
        P(("groups", "pool"), None, "head", None, None),
        P("groups", None),
        P("groups"),
        P("groups"),
    )

    return jax.shard_map(
        on_device,
        mesh=mesh,
        in_specs=placed,
        out_specs=(
            P(("groups", "pool"), "head", None),
            P(("groups", "pool"), None, "head", None, None),
        ),
        check_vma=False,
    )
```

```python
import functools

import jax
import jax.numpy as jnp
from jax import lax
from jax.experimental import pallas as pl
from jax.experimental.pallas import tpu as pltpu
from jax.sharding import PartitionSpec as P


log2_e = 1.4426950408889634
hidden_score = -2e30
lowest_top = -1e30
lanes = 128
block_rows = 128
kernel_bytes = 24 << 20


def moved(array, apart):
    count = lax.axis_size("pool")
    return lax.ppermute(array, "pool", [(i, i ^ apart) for i in range(count)])


def whole(array):
    return pl.BlockSpec(array.shape, lambda i, *_: (0,) * len(array.shape))


def diagonal():
    shape = (lanes, lanes)
    return lax.broadcasted_iota(jnp.int32, shape, 0) == lax.broadcasted_iota(jnp.int32, shape, 1)


def as_row(column, eye):
    spread = jnp.where(eye, jnp.broadcast_to(column, (lanes, lanes)), 0.0)
    return jnp.sum(spread, axis=0, keepdims=True)


def as_column(row, eye):
    spread = jnp.where(eye, jnp.broadcast_to(row, (lanes, lanes)), 0.0)
    return jnp.sum(spread, axis=1, keepdims=True)


def in_three(values):
    high = values.astype(jnp.bfloat16)
    rest = values - high.astype(jnp.float32)
    middle = rest.astype(jnp.bfloat16)
    low = (rest - middle.astype(jnp.float32)).astype(jnp.bfloat16)
    return (high, middle, low)


def from_three(ref, begin, count):
    parts = [
        ref[0, begin + i * count : begin + (i + 1) * count].astype(jnp.float32) for i in range(3)
    ]
    return parts[0] + parts[1] + parts[2]


def gather_body(owner_ref, table_ref, length_ref, pool_ref, *refs, lists, near, waits, kv_heads, cap):
    refs = refs[waits:]
    outs = refs[: len(lists) * kv_heads]
    seen_ref = refs[len(lists) * kv_heads] if near else None
    slots, sem = refs[-2:]
    owner = owner_ref[0]
    pair = owner >> 1
    slot_count, _, _, page_len, _ = pool_ref.shape
    width = table_ref.shape[1]

    def held(request, holder, j):
        slot = table_ref[request, j] - holder * slot_count
        return slot, (slot >= 0) & (slot < slot_count)

    def look(j, found):
        following = []
        for at, which in enumerate(lists):
            slot, here = held(pair ^ which, owner, j)
            slots[at * (cap + 1) + jnp.minimum(found[at], cap)] = slot
            following.append(found[at] + here.astype(jnp.int32))
        return tuple(following)

    found = lax.fori_loop(0, width, look, (jnp.int32(0),) * len(lists), unroll=16)
    copies = []
    for at in range(len(lists)):
        for k in range(kv_heads):
            for i in range(cap):
                slot = jnp.where(i < found[at], slots[at * (cap + 1) + i], 0)
                copy = pltpu.make_async_copy(
                    pool_ref.at[slot, :, k], outs[at * kv_heads + k].at[0, i], sem.at[at, k, i]
                )
                copy.start()
                copies.append(copy)
    if near:
        asked = [(t, s) for t in range(2) for s in range(near)]

        def count(j, seen):
            following = []
            for (t, s), so_far in zip(asked, seen):
                request = pair ^ (t * near)
                _, there = held(request, owner ^ (2 * s), j)
                inside = jnp.clip(length_ref[request] - j * page_len, 0, page_len)
                following.append(so_far + jnp.where(there, inside, 0))
            return tuple(following)

        seen = lax.fori_loop(0, width, count, (jnp.int32(0),) * len(asked), unroll=8)
        for (t, s), total in zip(asked, seen):
            seen_ref[t, s] = total
    for copy in copies:
        copy.wait()


def gather_pages(owner, table, lengths, pool, lists, near, cap, after=()):
    _, pair_of, kv_heads, page_len, head_dim = pool.shape
    count = len(lists) * kv_heads
    outs = [pltpu.VMEM((1, cap, pair_of, page_len, head_dim), pool.dtype)] * count
    specs = [pl.BlockSpec(memory_space=pltpu.VMEM)] * count
    if near:
        outs.append(jax.ShapeDtypeStruct((2, near), jnp.int32))
        specs.append(pl.BlockSpec(memory_space=pltpu.SMEM))
    results = pl.pallas_call(
        functools.partial(
            gather_body, lists=lists, near=near, waits=len(after), kv_heads=kv_heads, cap=cap
        ),
        out_shape=outs,
        grid_spec=pltpu.PrefetchScalarGridSpec(
            num_scalar_prefetch=3,
            grid=(1,),
            in_specs=[pl.BlockSpec(memory_space=pltpu.HBM)]
            + [pl.BlockSpec(memory_space=pl.ANY)] * len(after),
            out_specs=specs,
            scratch_shapes=[
                pltpu.SMEM((len(lists) * (cap + 1),), jnp.int32),
                pltpu.SemaphoreType.DMA((len(lists), kv_heads, cap)),
            ],
        ),
        compiler_params=pltpu.CompilerParams(vmem_limit_bytes=kernel_bytes),
        name="gather_pages",
    )(
        owner,
        pltpu.with_memory_space_constraint(table, pltpu.HBM),
        pltpu.with_memory_space_constraint(lengths, pltpu.HBM),
        pltpu.with_memory_space_constraint(pool, pltpu.HBM),
        *after,
    )
    pages = [results[i * kv_heads : (i + 1) * kv_heads] for i in range(len(lists))]
    return pages, results[-1]


def attend_body(
    owner_ref,
    seen_ref,
    fresh_ref,
    *refs,
    halves,
    seen_at,
    has_page,
    has_prev,
    packed,
    step_rows,
    tile_rows,
    group,
    scale,
    copies_pool,
    waits,
    page_at,
):
    refs = list(refs)
    q_refs = [refs.pop(0) for _ in range(halves)]
    kv_refs = [refs.pop(0) for _ in seen_at]
    page_ref = refs.pop(0) if has_page else None
    prev_refs = [(refs.pop(0), refs.pop(0)) for _ in range(halves)] if has_prev else None
    pool_ref = refs.pop(0) if copies_pool else None
    del refs[:waits]
    out_refs = []
    for h in range(halves):
        out_refs.append((refs.pop(0),) if packed[h] else (refs.pop(0), refs.pop(0)))
    new_pool = refs.pop(0) if copies_pool else None
    wide_values = refs.pop(0)
    tables = [refs.pop(0) if packed[h] else out_refs[h][1].at[0] for h in range(halves)]
    if copies_pool:
        staged, sem_in, sem_out = refs
    head = pl.program_id(0)
    step = pl.program_id(1)
    heads = pl.num_programs(0)
    steps = pl.num_programs(1)
    owner = owner_ref[0]
    half = 1 - ((owner & 1) ^ ((owner >> 1) & 1))
    page_len = kv_refs[0].shape[3]
    keys = [ref.shape[1] * page_len for ref in kv_refs]

    if copies_pool:

        @pl.when((head == 0) & (step == 0))
        def _():
            pltpu.make_async_copy(pool_ref, staged, sem_in).start()

        @pl.when((head == 0) & (step == jnp.minimum(1, steps - 1)))
        def _():
            pltpu.make_async_copy(pool_ref, staged, sem_in).wait()
            staged[fresh_ref[owner] - owner * staged.shape[0]] = page_ref[...]
            pltpu.make_async_copy(staged, new_pool, sem_out).start()

    @pl.when(step == 0)
    def _():
        ones = jnp.ones((page_len, lanes), jnp.bfloat16)
        begin = 0
        for ref in kv_refs:
            for p in range(ref.shape[1]):
                wide_values[begin : begin + page_len, :lanes] = ref[0, p, 1]
                wide_values[begin : begin + page_len, lanes:] = ones
                begin += page_len
        if has_page:
            wide_values[begin : begin + page_len, :lanes] = page_ref[1, page_at]
            wide_values[begin : begin + page_len, lanes:] = ones

    eye = diagonal()
    limits = []
    for s, at in enumerate(seen_at):
        position = lax.broadcasted_iota(jnp.int32, (1, keys[s]), 1)
        limit = jnp.where(position < seen_ref[at[0], at[1]], jnp.inf, hidden_score)
        limits.append(limit.astype(jnp.float32))

    def score(h, t):
        query = q_refs[h][0, t * tile_rows : (t + 1) * tile_rows]
        scores = []
        for s, ref in enumerate(kv_refs):
            key_rows = ref[0, :, 0].reshape(keys[s], lanes)
            product = lax.dot_general(
                query, key_rows, (((1,), (1,)), ((), ())), preferred_element_type=jnp.float32
            )
            scores.append(jnp.minimum(product, limits[s]))
        if has_page:
            product = lax.dot_general(
                query, page_ref[0, page_at], (((1,), (1,)), ((), ())), preferred_element_type=jnp.float32
            )
            key_at = lax.broadcasted_iota(jnp.int32, product.shape, 1)
            if h == 0:
                row_at = lax.broadcasted_iota(jnp.int32, product.shape, 0)
                token = (step * step_rows + t * tile_rows + row_at) // group
                shown = key_at <= token
            else:
                shown = key_at < jnp.where(half == 0, page_len, 0)
            scores.append(jnp.where(shown, product, hidden_score))
        return scores

    def finish(h, t, scores):
        top = jnp.full((tile_rows, 1), lowest_top, jnp.float32)
        for part in scores:
            top = jnp.maximum(top, jnp.max(part, axis=1, keepdims=True))
        scaled_top = top * scale
        weights = [jnp.exp2(part * scale - scaled_top).astype(jnp.bfloat16) for part in scores]
        mixed = jnp.dot(
            jnp.concatenate(weights, axis=1), wide_values[...], preferred_element_type=jnp.float32
        )
        total = mixed[:, lanes:]
        mixed = mixed[:, :lanes]
        first = step * (step_rows // block_rows) + t * (tile_rows // block_rows)
        count = tables[h].shape[0] // 2
        for u in range(tile_rows // block_rows):
            inner = slice(u * block_rows, (u + 1) * block_rows)
            outer = slice(t * tile_rows + u * block_rows, t * tile_rows + (u + 1) * block_rows)
            part_top, part_total, part_mixed = top[inner], total[inner], mixed[inner]
            row = first + u
            if has_prev:
                prev_mixed, prev_table = prev_refs[h]
                prev_top = as_column(prev_table[0, pl.ds(row, 1)], eye)
                prev_total = as_column(prev_table[0, pl.ds(count + row, 1)], eye)
                joint = jnp.maximum(part_top, prev_top)
                keep = jnp.exp2((part_top - joint) * scale)
                keep_prev = jnp.exp2((prev_top - joint) * scale)
                part_mixed = part_mixed * keep + prev_mixed[0, outer] * keep_prev
                part_total = part_total * keep + prev_total * keep_prev
                part_top = joint
            tables[h][pl.ds(row, 1)] = as_row(part_top, eye)
            tables[h][pl.ds(count + row, 1)] = as_row(part_total, eye)
            if packed[h]:
                at = pl.multiple_of(row * block_rows, block_rows)
                out_refs[h][0][0, pl.ds(at, block_rows)] = part_mixed.astype(jnp.bfloat16)
            else:
                out_refs[h][0][0, outer] = part_mixed

    chains = [(h, t) for t in range(step_rows // tile_rows) for h in range(halves)]
    scores = score(*chains[0])
    for i, chain in enumerate(chains):
        following = score(*chains[i + 1]) if i + 1 < len(chains) else None
        finish(*chain, scores)
        scores = following

    @pl.when(step == steps - 1)
    def _():
        for h in range(halves):
            if packed[h]:
                size = tables[h].shape[0]
                begin = out_refs[h][0].shape[1] - 3 * size
                for i, part in enumerate(in_three(tables[h][...])):
                    out_refs[h][0][0, begin + i * size : begin + (i + 1) * size] = part

    if copies_pool:

        @pl.when((head == heads - 1) & (step == steps - 1))
        def _():
            pltpu.make_async_copy(staged, new_pool, sem_out).wait()


def attend(
    scalars, queries, sources, seen_at, packed, scale, group, heads, page=None, prev=None, pool=None, after=()
):
    halves = len(queries)
    rows = queries[0][0].shape[1]
    size = 2 * (rows // block_rows)
    step_rows = min(rows, 1024 // halves)
    tile_rows = min(step_rows, 256)
    key_count = sum(s.shape[1] * s.shape[3] for s, _ in sources)

    def per_rows(offset):
        return pl.BlockSpec((1, step_rows, lanes), lambda k, i, *_: (k + offset, i, 0))

    def per_head(array, offset):
        tail = array.shape[1:]
        return pl.BlockSpec((1, *tail), lambda k, i, *_: (k + offset,) + (0,) * len(tail))

    anywhere = pl.BlockSpec(memory_space=pl.ANY)
    args = [q for q, _ in queries] + [s for s, _ in sources]
    in_specs = [per_rows(at) for _, at in queries] + [per_head(s, at) for s, at in sources]
    page_at = 0
    if page is not None:
        page, page_at = page
        args.append(page)
        in_specs.append(whole(page))
        key_count += page.shape[2]
    if prev is not None:
        for mixed, table, at in prev:
            args += [mixed, table]
            in_specs += [per_rows(at), per_head(table, at)]
    if pool is not None:
        args.append(pltpu.with_memory_space_constraint(pool, pltpu.HBM))
        in_specs.append(pl.BlockSpec(memory_space=pltpu.HBM))
    args += list(after)
    in_specs += [anywhere] * len(after)
    out_shape = []
    out_specs = []
    scratch = [pltpu.VMEM((key_count, 2 * lanes), jnp.bfloat16)]
    for h in range(halves):
        if packed[h]:
            shape = jax.ShapeDtypeStruct((heads, rows + 3 * size, lanes), jnp.bfloat16)
            out_shape.append(shape)
            out_specs.append(per_head(shape, 0))
            scratch.append(pltpu.VMEM((size, lanes), jnp.float32))
        else:
            table = jax.ShapeDtypeStruct((heads, size, lanes), jnp.float32)
            out_shape += [jax.ShapeDtypeStruct((heads, rows, lanes), jnp.float32), table]
            out_specs += [per_rows(0), per_head(table, 0)]
    if pool is not None:
        out_shape.append(jax.ShapeDtypeStruct(pool.shape, pool.dtype))
        out_specs.append(pl.BlockSpec(memory_space=pltpu.HBM))
        scratch.append(pltpu.VMEM(pool.shape, pool.dtype))
        scratch += [pltpu.SemaphoreType.DMA, pltpu.SemaphoreType.DMA]
    work = halves * heads * rows * key_count
    return pl.pallas_call(
        functools.partial(
            attend_body,
            halves=halves,
            seen_at=seen_at,
            has_page=page is not None,
            has_prev=prev is not None,
            packed=packed,
            step_rows=step_rows,
            tile_rows=tile_rows,
            group=group,
            scale=scale,
            copies_pool=pool is not None,
            waits=len(after),
            page_at=page_at,
        ),
        out_shape=out_shape,
        grid_spec=pltpu.PrefetchScalarGridSpec(
            num_scalar_prefetch=3,
            grid=(heads, rows // step_rows),
            in_specs=in_specs,
            out_specs=out_specs,
            scratch_shapes=scratch,
        ),
        cost_estimate=pl.CostEstimate(
            flops=4 * work * lanes,
            transcendentals=work,
            bytes_accessed=4 * heads * key_count * lanes,
        ),
        compiler_params=pltpu.CompilerParams(vmem_limit_bytes=kernel_bytes),
        name="attend",
    )(*scalars, *args)


def join_body(own_mixed, own_table, *refs, scale, packs, waits):
    refs = list(refs)
    out_ref = refs.pop()
    if waits:
        del refs[-waits:]
    size = own_table.shape[1]
    count = size // 2
    rows = count * block_rows
    eye = diagonal()
    tops = [own_table[0, :count]]
    totals = [own_table[0, count:]]
    for ref in refs:
        table = from_three(ref, rows, size)
        tops.append(table[:count])
        totals.append(table[count:])
    top = functools.reduce(jnp.maximum, tops)
    keeps = [jnp.exp2((t - top) * scale) for t in tops]
    total = sum(t * keep for t, keep in zip(totals, keeps))
    if not packs:
        keeps = [keep / total for keep in keeps]
    for t in range(count):
        at = slice(t * block_rows, (t + 1) * block_rows)
        mixed = own_mixed[0, at] * as_column(keeps[0][t : t + 1], eye)
        for ref, keep in zip(refs, keeps[1:]):
            mixed = mixed + ref[0, at].astype(jnp.float32) * as_column(keep[t : t + 1], eye)
        if packs:
            out_ref[0, at] = mixed.astype(jnp.bfloat16)
        else:
            heads = out_ref.shape[1]
            tokens = block_rows // heads
            shaped = mixed.reshape(tokens, heads, lanes)
            out_ref[t * tokens : (t + 1) * tokens] = shaped.astype(jnp.bfloat16)
    if packs:
        table = jnp.concatenate([top, total], axis=0)
        for i, part in enumerate(in_three(table)):
            out_ref[0, rows + i * size : rows + (i + 1) * size] = part


def join_packed(own, received, scale, after=()):
    mixed, table = own
    args = [mixed, table, received]
    return pl.pallas_call(
        functools.partial(join_body, scale=scale, packs=True, waits=len(after)),
        out_shape=jax.ShapeDtypeStruct(received.shape, received.dtype),
        grid=(1,),
        in_specs=[whole(a) for a in args] + [pl.BlockSpec(memory_space=pl.ANY)] * len(after),
        out_specs=whole(received),
        compiler_params=pltpu.CompilerParams(vmem_limit_bytes=kernel_bytes),
        name="join_packed",
    )(*args, *after)


def join_out(own, received, target, shape, index, group, scale):
    mixed, table = own
    args = [mixed, table, *received]
    in_specs = [whole(a) for a in args]
    aliases = {}
    if target is not None:
        aliases = {len(args): 0}
        args.append(target)
        in_specs.append(pl.BlockSpec(memory_space=pl.ANY))
    return pl.pallas_call(
        functools.partial(join_body, scale=scale, packs=False, waits=len(aliases)),
        out_shape=jax.ShapeDtypeStruct(shape, jnp.bfloat16),
        grid=(1,),
        in_specs=in_specs,
        out_specs=pl.BlockSpec((shape[0], group, shape[2]), lambda i: (0, index, 0)),
        input_output_aliases=aliases,
        compiler_params=pltpu.CompilerParams(vmem_limit_bytes=kernel_bytes),
        name="join_out",
    )(*args)


def on_device(queries, new_kv, pool, block_table, prefix_len, new_slots):
    owner_count = lax.axis_size("pool")
    owner = lax.axis_index("pool").astype(jnp.int32)
    _, _, kv_heads, _, head_dim = pool.shape
    tokens, q_heads, _ = queries.shape
    group = q_heads // kv_heads
    rows = tokens * group
    pairs = owner_count // 2
    near = pairs // 2
    cap = block_table.shape[1] // owner_count
    scale = head_dim**-0.5 * log2_e
    each = range(kv_heads)

    owner_list = jnp.full((1,), owner, jnp.int32)
    split = [
        queries[:, k * group : (k + 1) * group].reshape(1, rows, head_dim) for k in each
    ]
    new_page = new_kv.transpose(1, 2, 0, 3)
    far_own = [moved(split[k], pairs) for k in each]
    other = [moved(split[k], 1) for k in each]
    lookup = (owner_list, block_table, prefix_len, pool)
    sent_far, _ = gather_pages(*lookup, [near + k for k in range(1, near)], 0, cap)
    rest_lists = list(range(1, near)) + [0, near]
    pages, seen = gather_pages(*lookup, rest_lists, near, cap, after=[new_page])

    def exchanged(sent):
        return [[moved(sent[i][k], 2 * (i + 1)) for i in range(near - 1)] for k in each]

    got_far = exchanged(sent_far)
    got_near = exchanged(pages)
    local, local_far = pages[near - 1 :]
    scalars = (owner_list, seen, new_slots)

    started = []
    updated = None
    after = []
    for k in each:
        results = attend(
            scalars,
            [(split[k], 0), (other[k], 0)],
            [(local[k], 0)],
            [(0, 0)],
            (False, False),
            scale,
            group,
            1,
            page=(new_page, k),
            pool=pool if k == 0 else None,
            after=after,
        )
        if k == 0:
            updated = results[4]
        started.append(results[:4])
        after = [results[1]]
    far_other = [moved(far_own[k], 1) for k in each]
    far = []
    for k in each:
        results = attend(
            scalars,
            [(far_own[k], 0), (far_other[k], 0)],
            [(local_far[k], 0)] + [(a, 0) for a in got_far[k]],
            [(1, i) for i in range(near)],
            (False, True),
            scale,
            group,
            1,
            after=after,
        )
        far.append((results[:2], moved(results[2], 1)))
        after = [results[1]]
    back = []
    ready = []
    for k in each:
        joined = join_packed(*far[k], scale, after=after)
        back.append(moved(joined, pairs))
        mine, mine_table, theirs, theirs_table = started[k]
        near_keys = [(a, 0) for a in got_near[k]]
        near_at = [(0, i) for i in range(1, near)]
        mine, theirs = (mine, mine_table, 0), (theirs, theirs_table, 0)
        if k + 1 < kv_heads:
            results = attend(
                scalars,
                [(split[k], 0), (other[k], 0)],
                near_keys,
                near_at,
                (False, True),
                scale,
                group,
                1,
                prev=[mine, theirs],
                after=[joined],
            )
            own_part = results[:2]
            other_part = results[2]
        else:
            (other_part,) = attend(
                scalars,
                [(other[k], 0)],
                near_keys,
                near_at,
                (True,),
                scale,
                group,
                1,
                prev=[theirs],
                after=[joined],
            )
            own_part = attend(
                scalars,
                [(split[k], 0)],
                near_keys,
                near_at,
                (False,),
                scale,
                group,
                1,
                prev=[mine],
                after=[other_part],
            )
        ready.append((own_part, moved(other_part, 1)))
        after = [own_part[1]]
    attended = None
    for k in each:
        own, received = ready[k]
        attended = join_out(
            own, [received, back[k]], attended, queries.shape, k, group, scale
        )
    return (attended, updated)


def solution(mesh):
    placed = (
        P(("groups", "pool"), "head", None),
        P(("groups", "pool"), None, "head", None),
        P(("groups", "pool"), None, "head", None, None),
        P("groups", None),
        P("groups"),
        P("groups"),
    )

    return jax.shard_map(
        on_device,
        mesh=mesh,
        in_specs=placed,
        out_specs=(
            P(("groups", "pool"), "head", None),
            P(("groups", "pool"), None, "head", None, None),
        ),
        check_vma=False,
    )
```

```python
import functools

import jax
import jax.numpy as jnp
from jax import lax
from jax.experimental import pallas as pl
from jax.experimental.pallas import tpu as pltpu
from jax.sharding import PartitionSpec as P


log2_e = 1.4426950408889634
hidden_score = -2e30
lowest_top = -1e30
lanes = 128
block_rows = 128
kernel_bytes = 24 << 20


def moved(array, apart):
    count = lax.axis_size("pool")
    return lax.ppermute(array, "pool", [(i, i ^ apart) for i in range(count)])


def whole(array):
    return pl.BlockSpec(array.shape, lambda i, *_: (0,) * len(array.shape))


def diagonal():
    shape = (lanes, lanes)
    return lax.broadcasted_iota(jnp.int32, shape, 0) == lax.broadcasted_iota(jnp.int32, shape, 1)


def as_row(column, eye):
    spread = jnp.where(eye, jnp.broadcast_to(column, (lanes, lanes)), 0.0)
    return jnp.sum(spread, axis=0, keepdims=True)


def as_column(row, eye):
    spread = jnp.where(eye, jnp.broadcast_to(row, (lanes, lanes)), 0.0)
    return jnp.sum(spread, axis=1, keepdims=True)


def in_three(values):
    high = values.astype(jnp.bfloat16)
    rest = values - high.astype(jnp.float32)
    middle = rest.astype(jnp.bfloat16)
    low = (rest - middle.astype(jnp.float32)).astype(jnp.bfloat16)
    return (high, middle, low)


def from_three(ref, begin, count):
    parts = [
        ref[0, begin + i * count : begin + (i + 1) * count].astype(jnp.float32) for i in range(3)
    ]
    return parts[0] + parts[1] + parts[2]


def last_pages(cap):
    return max(1, cap // 4)


def gather_body(owner_ref, table_ref, length_ref, pool_ref, *refs, lists, near, waits, ranges, cap):
    refs = refs[waits:]
    outs = refs[: len(ranges)]
    seen_ref = refs[len(ranges)] if near else None
    slots, sem = refs[-2:]
    owner = owner_ref[0]
    pair = owner >> 1
    slot_count, _, _, page_len, _ = pool_ref.shape
    width = table_ref.shape[1]

    def held(request, holder, j):
        slot = table_ref[request, j] - holder * slot_count
        return slot, (slot >= 0) & (slot < slot_count)

    def look(j, found):
        following = []
        for at, which in enumerate(lists):
            slot, here = held(pair ^ which, owner, j)
            slots[at * (cap + 1) + jnp.minimum(found[at], cap)] = slot
            following.append(found[at] + here.astype(jnp.int32))
        return tuple(following)

    found = lax.fori_loop(0, width, look, (jnp.int32(0),) * len(lists), unroll=16)
    copies = []
    for (at, k, begin, end), out in zip(ranges, outs):
        for i in range(begin, end):
            slot = jnp.where(i < found[at], slots[at * (cap + 1) + i], 0)
            copy = pltpu.make_async_copy(
                pool_ref.at[slot, :, k], out.at[0, i - begin], sem.at[at, k, i]
            )
            copy.start()
            copies.append(copy)
    if near:
        asked = [(t, s) for t in range(2) for s in range(near)]

        def count(j, seen):
            following = []
            for (t, s), so_far in zip(asked, seen):
                request = pair ^ (t * near)
                _, there = held(request, owner ^ (2 * s), j)
                inside = jnp.clip(length_ref[request] - j * page_len, 0, page_len)
                following.append(so_far + jnp.where(there, inside, 0))
            return tuple(following)

        seen = lax.fori_loop(0, width, count, (jnp.int32(0),) * len(asked), unroll=8)
        for (t, s), total in zip(asked, seen):
            seen_ref[t, s] = total
    for copy in copies:
        copy.wait()


def gather_pages(owner, table, lengths, pool, lists, near, cap, after=()):
    _, pair_of, kv_heads, page_len, head_dim = pool.shape
    ranges = []
    for at in range(len(lists)):
        for k in range(kv_heads):
            cuts = [0, cap]
            if near and at < near - 1 and k == kv_heads - 1:
                cuts.insert(1, cap - last_pages(cap))
            ranges += [(at, k, begin, end) for begin, end in zip(cuts, cuts[1:])]
    outs = [
        pltpu.VMEM((1, end - begin, pair_of, page_len, head_dim), pool.dtype)
        for _, _, begin, end in ranges
    ]
    specs = [pl.BlockSpec(memory_space=pltpu.VMEM)] * len(outs)
    if near:
        outs.append(jax.ShapeDtypeStruct((2, near), jnp.int32))
        specs.append(pl.BlockSpec(memory_space=pltpu.SMEM))
    results = pl.pallas_call(
        functools.partial(
            gather_body, lists=lists, near=near, waits=len(after), ranges=ranges, cap=cap
        ),
        out_shape=outs,
        grid_spec=pltpu.PrefetchScalarGridSpec(
            num_scalar_prefetch=3,
            grid=(1,),
            in_specs=[pl.BlockSpec(memory_space=pltpu.HBM)]
            + [pl.BlockSpec(memory_space=pl.ANY)] * len(after),
            out_specs=specs,
            scratch_shapes=[
                pltpu.SMEM((len(lists) * (cap + 1),), jnp.int32),
                pltpu.SemaphoreType.DMA((len(lists), kv_heads, cap)),
            ],
        ),
        compiler_params=pltpu.CompilerParams(vmem_limit_bytes=kernel_bytes),
        name="gather_pages",
    )(
        owner,
        pltpu.with_memory_space_constraint(table, pltpu.HBM),
        pltpu.with_memory_space_constraint(lengths, pltpu.HBM),
        pltpu.with_memory_space_constraint(pool, pltpu.HBM),
        *after,
    )
    pages = [[[] for _ in range(kv_heads)] for _ in lists]
    for (at, k, _, _), part in zip(ranges, results):
        pages[at][k].append(part)
    return pages, results[-1]


def attend_body(
    owner_ref,
    seen_ref,
    fresh_ref,
    *refs,
    halves,
    seen_at,
    has_page,
    has_prev,
    packed,
    step_rows,
    tile_rows,
    group,
    scale,
    copies_pool,
    waits,
    page_at,
):
    refs = list(refs)
    q_refs = [refs.pop(0) for _ in range(halves)]
    kv_refs = [refs.pop(0) for _ in seen_at]
    page_ref = refs.pop(0) if has_page else None
    prev_refs = [(refs.pop(0), refs.pop(0)) for _ in range(halves)] if has_prev else None
    pool_ref = refs.pop(0) if copies_pool else None
    del refs[:waits]
    out_refs = []
    for h in range(halves):
        out_refs.append((refs.pop(0),) if packed[h] else (refs.pop(0), refs.pop(0)))
    new_pool = refs.pop(0) if copies_pool else None
    wide_values = refs.pop(0)
    tables = [refs.pop(0) if packed[h] else out_refs[h][1].at[0] for h in range(halves)]
    if copies_pool:
        staged, sem_in, sem_out = refs
    head = pl.program_id(0)
    step = pl.program_id(1)
    heads = pl.num_programs(0)
    steps = pl.num_programs(1)
    owner = owner_ref[0]
    half = 1 - ((owner & 1) ^ ((owner >> 1) & 1))
    page_len = kv_refs[0].shape[3]
    keys = [ref.shape[1] * page_len for ref in kv_refs]

    if copies_pool:

        @pl.when((head == 0) & (step == 0))
        def _():
            pltpu.make_async_copy(pool_ref, staged, sem_in).start()

        @pl.when((head == 0) & (step == jnp.minimum(1, steps - 1)))
        def _():
            pltpu.make_async_copy(pool_ref, staged, sem_in).wait()
            staged[fresh_ref[owner] - owner * staged.shape[0]] = page_ref[...]
            pltpu.make_async_copy(staged, new_pool, sem_out).start()

    @pl.when(step == 0)
    def _():
        ones = jnp.ones((page_len, lanes), jnp.bfloat16)
        begin = 0
        for ref in kv_refs:
            for p in range(ref.shape[1]):
                wide_values[begin : begin + page_len, :lanes] = ref[0, p, 1]
                wide_values[begin : begin + page_len, lanes:] = ones
                begin += page_len
        if has_page:
            wide_values[begin : begin + page_len, :lanes] = page_ref[1, page_at]
            wide_values[begin : begin + page_len, lanes:] = ones

    eye = diagonal()
    limits = []
    for s, at in enumerate(seen_at):
        position = lax.broadcasted_iota(jnp.int32, (1, keys[s]), 1)
        limit = jnp.where(position + at[2] < seen_ref[at[0], at[1]], jnp.inf, hidden_score)
        limits.append(limit.astype(jnp.float32))

    def score(h, t):
        query = q_refs[h][0, t * tile_rows : (t + 1) * tile_rows]
        scores = []
        for s, ref in enumerate(kv_refs):
            key_rows = ref[0, :, 0].reshape(keys[s], lanes)
            product = lax.dot_general(
                query, key_rows, (((1,), (1,)), ((), ())), preferred_element_type=jnp.float32
            )
            scores.append(jnp.minimum(product, limits[s]))
        if has_page:
            product = lax.dot_general(
                query, page_ref[0, page_at], (((1,), (1,)), ((), ())), preferred_element_type=jnp.float32
            )
            key_at = lax.broadcasted_iota(jnp.int32, product.shape, 1)
            if h == 0:
                row_at = lax.broadcasted_iota(jnp.int32, product.shape, 0)
                token = (step * step_rows + t * tile_rows + row_at) // group
                shown = key_at <= token
            else:
                shown = key_at < jnp.where(half == 0, page_len, 0)
            scores.append(jnp.where(shown, product, hidden_score))
        return scores

    def finish(h, t, scores):
        top = jnp.full((tile_rows, 1), lowest_top, jnp.float32)
        for part in scores:
            top = jnp.maximum(top, jnp.max(part, axis=1, keepdims=True))
        scaled_top = top * scale
        weights = [jnp.exp2(part * scale - scaled_top).astype(jnp.bfloat16) for part in scores]
        mixed = jnp.dot(
            jnp.concatenate(weights, axis=1), wide_values[...], preferred_element_type=jnp.float32
        )
        total = mixed[:, lanes:]
        mixed = mixed[:, :lanes]
        first = step * (step_rows // block_rows) + t * (tile_rows // block_rows)
        count = tables[h].shape[0] // 2
        for u in range(tile_rows // block_rows):
            inner = slice(u * block_rows, (u + 1) * block_rows)
            outer = slice(t * tile_rows + u * block_rows, t * tile_rows + (u + 1) * block_rows)
            part_top, part_total, part_mixed = top[inner], total[inner], mixed[inner]
            row = first + u
            if has_prev:
                prev_mixed, prev_table = prev_refs[h]
                prev_top = as_column(prev_table[0, pl.ds(row, 1)], eye)
                prev_total = as_column(prev_table[0, pl.ds(count + row, 1)], eye)
                joint = jnp.maximum(part_top, prev_top)
                keep = jnp.exp2((part_top - joint) * scale)
                keep_prev = jnp.exp2((prev_top - joint) * scale)
                part_mixed = part_mixed * keep + prev_mixed[0, outer] * keep_prev
                part_total = part_total * keep + prev_total * keep_prev
                part_top = joint
            tables[h][pl.ds(row, 1)] = as_row(part_top, eye)
            tables[h][pl.ds(count + row, 1)] = as_row(part_total, eye)
            if packed[h]:
                at = pl.multiple_of(row * block_rows, block_rows)
                out_refs[h][0][0, pl.ds(at, block_rows)] = part_mixed.astype(jnp.bfloat16)
            else:
                out_refs[h][0][0, outer] = part_mixed

    chains = [(h, t) for t in range(step_rows // tile_rows) for h in range(halves)]
    scores = score(*chains[0])
    for i, chain in enumerate(chains):
        following = score(*chains[i + 1]) if i + 1 < len(chains) else None
        finish(*chain, scores)
        scores = following

    @pl.when(step == steps - 1)
    def _():
        for h in range(halves):
            if packed[h]:
                size = tables[h].shape[0]
                begin = out_refs[h][0].shape[1] - 3 * size
                for i, part in enumerate(in_three(tables[h][...])):
                    out_refs[h][0][0, begin + i * size : begin + (i + 1) * size] = part

    if copies_pool:

        @pl.when((head == heads - 1) & (step == steps - 1))
        def _():
            pltpu.make_async_copy(staged, new_pool, sem_out).wait()


def attend(
    scalars, queries, sources, seen_at, packed, scale, group, heads, page=None, prev=None, pool=None, after=()
):
    halves = len(queries)
    rows = queries[0][0].shape[1]
    size = 2 * (rows // block_rows)
    step_rows = min(rows, 1024 // halves)
    tile_rows = min(step_rows, 256)
    key_count = sum(s.shape[1] * s.shape[3] for s, _ in sources)

    def per_rows(offset):
        return pl.BlockSpec((1, step_rows, lanes), lambda k, i, *_: (k + offset, i, 0))

    def per_head(array, offset):
        tail = array.shape[1:]
        return pl.BlockSpec((1, *tail), lambda k, i, *_: (k + offset,) + (0,) * len(tail))

    anywhere = pl.BlockSpec(memory_space=pl.ANY)
    args = [q for q, _ in queries] + [s for s, _ in sources]
    in_specs = [per_rows(at) for _, at in queries] + [per_head(s, at) for s, at in sources]
    page_at = 0
    if page is not None:
        page, page_at = page
        args.append(page)
        in_specs.append(whole(page))
        key_count += page.shape[2]
    if prev is not None:
        for mixed, table, at in prev:
            args += [mixed, table]
            in_specs += [per_rows(at), per_head(table, at)]
    if pool is not None:
        args.append(pltpu.with_memory_space_constraint(pool, pltpu.HBM))
        in_specs.append(pl.BlockSpec(memory_space=pltpu.HBM))
    args += list(after)
    in_specs += [anywhere] * len(after)
    out_shape = []
    out_specs = []
    scratch = [pltpu.VMEM((key_count, 2 * lanes), jnp.bfloat16)]
    for h in range(halves):
        if packed[h]:
            shape = jax.ShapeDtypeStruct((heads, rows + 3 * size, lanes), jnp.bfloat16)
            out_shape.append(shape)
            out_specs.append(per_head(shape, 0))
            scratch.append(pltpu.VMEM((size, lanes), jnp.float32))
        else:
            table = jax.ShapeDtypeStruct((heads, size, lanes), jnp.float32)
            out_shape += [jax.ShapeDtypeStruct((heads, rows, lanes), jnp.float32), table]
            out_specs += [per_rows(0), per_head(table, 0)]
    if pool is not None:
        out_shape.append(jax.ShapeDtypeStruct(pool.shape, pool.dtype))
        out_specs.append(pl.BlockSpec(memory_space=pltpu.HBM))
        scratch.append(pltpu.VMEM(pool.shape, pool.dtype))
        scratch += [pltpu.SemaphoreType.DMA, pltpu.SemaphoreType.DMA]
    work = halves * heads * rows * key_count
    return pl.pallas_call(
        functools.partial(
            attend_body,
            halves=halves,
            seen_at=seen_at,
            has_page=page is not None,
            has_prev=prev is not None,
            packed=packed,
            step_rows=step_rows,
            tile_rows=tile_rows,
            group=group,
            scale=scale,
            copies_pool=pool is not None,
            waits=len(after),
            page_at=page_at,
        ),
        out_shape=out_shape,
        grid_spec=pltpu.PrefetchScalarGridSpec(
            num_scalar_prefetch=3,
            grid=(heads, rows // step_rows),
            in_specs=in_specs,
            out_specs=out_specs,
            scratch_shapes=scratch,
        ),
        cost_estimate=pl.CostEstimate(
            flops=4 * work * lanes,
            transcendentals=work,
            bytes_accessed=4 * heads * key_count * lanes,
        ),
        compiler_params=pltpu.CompilerParams(vmem_limit_bytes=kernel_bytes),
        name="attend",
    )(*scalars, *args)


def join_body(own_mixed, own_table, *refs, scale, packs, waits):
    refs = list(refs)
    out_ref = refs.pop()
    if waits:
        del refs[-waits:]
    size = own_table.shape[1]
    count = size // 2
    rows = count * block_rows
    eye = diagonal()
    tops = [own_table[0, :count]]
    totals = [own_table[0, count:]]
    for ref in refs:
        table = from_three(ref, rows, size)
        tops.append(table[:count])
        totals.append(table[count:])
    top = functools.reduce(jnp.maximum, tops)
    keeps = [jnp.exp2((t - top) * scale) for t in tops]
    total = sum(t * keep for t, keep in zip(totals, keeps))
    if not packs:
        keeps = [keep / total for keep in keeps]
    for t in range(count):
        at = slice(t * block_rows, (t + 1) * block_rows)
        mixed = own_mixed[0, at] * as_column(keeps[0][t : t + 1], eye)
        for ref, keep in zip(refs, keeps[1:]):
            mixed = mixed + ref[0, at].astype(jnp.float32) * as_column(keep[t : t + 1], eye)
        if packs:
            out_ref[0, at] = mixed.astype(jnp.bfloat16)
        else:
            heads = out_ref.shape[1]
            tokens = block_rows // heads
            shaped = mixed.reshape(tokens, heads, lanes)
            out_ref[t * tokens : (t + 1) * tokens] = shaped.astype(jnp.bfloat16)
    if packs:
        table = jnp.concatenate([top, total], axis=0)
        for i, part in enumerate(in_three(table)):
            out_ref[0, rows + i * size : rows + (i + 1) * size] = part


def join_packed(own, received, scale, after=()):
    mixed, table = own
    args = [mixed, table, received]
    return pl.pallas_call(
        functools.partial(join_body, scale=scale, packs=True, waits=len(after)),
        out_shape=jax.ShapeDtypeStruct(received.shape, received.dtype),
        grid=(1,),
        in_specs=[whole(a) for a in args] + [pl.BlockSpec(memory_space=pl.ANY)] * len(after),
        out_specs=whole(received),
        compiler_params=pltpu.CompilerParams(vmem_limit_bytes=kernel_bytes),
        name="join_packed",
    )(*args, *after)


def join_out(own, received, target, shape, index, group, scale):
    mixed, table = own
    args = [mixed, table, *received]
    in_specs = [whole(a) for a in args]
    aliases = {}
    if target is not None:
        aliases = {len(args): 0}
        args.append(target)
        in_specs.append(pl.BlockSpec(memory_space=pl.ANY))
    return pl.pallas_call(
        functools.partial(join_body, scale=scale, packs=False, waits=len(aliases)),
        out_shape=jax.ShapeDtypeStruct(shape, jnp.bfloat16),
        grid=(1,),
        in_specs=in_specs,
        out_specs=pl.BlockSpec((shape[0], group, shape[2]), lambda i: (0, index, 0)),
        input_output_aliases=aliases,
        compiler_params=pltpu.CompilerParams(vmem_limit_bytes=kernel_bytes),
        name="join_out",
    )(*args)


def on_device(queries, new_kv, pool, block_table, prefix_len, new_slots):
    owner_count = lax.axis_size("pool")
    owner = lax.axis_index("pool").astype(jnp.int32)
    _, _, kv_heads, page_len, head_dim = pool.shape
    tokens, q_heads, _ = queries.shape
    group = q_heads // kv_heads
    rows = tokens * group
    pairs = owner_count // 2
    near = pairs // 2
    cap = block_table.shape[1] // owner_count
    scale = head_dim**-0.5 * log2_e
    each = range(kv_heads)

    owner_list = jnp.full((1,), owner, jnp.int32)
    split = [
        queries[:, k * group : (k + 1) * group].reshape(1, rows, head_dim) for k in each
    ]
    new_page = new_kv.transpose(1, 2, 0, 3)
    far_own = [moved(split[k], pairs) for k in each]
    other = [moved(split[k], 1) for k in each]
    lookup = (owner_list, block_table, prefix_len, pool)
    sent_far, _ = gather_pages(*lookup, [near + k for k in range(1, near)], 0, cap)
    rest_lists = list(range(1, near)) + [0, near]
    pages, seen = gather_pages(*lookup, rest_lists, near, cap, after=[new_page])

    def exchanged(sent, k, part):
        return [moved(sent[i][k][part], 2 * (i + 1)) for i in range(near - 1)]

    got_far = [exchanged(sent_far, k, 0) for k in each]
    got_near = [exchanged(pages, k, 0) for k in each]
    got_late = exchanged(pages, kv_heads - 1, 1)
    local, local_far = [[part[0] for part in pages[i]] for i in (near - 1, near)]
    scalars = (owner_list, seen, new_slots)

    started = []
    updated = None
    after = []
    for k in each:
        results = attend(
            scalars,
            [(split[k], 0), (other[k], 0)],
            [(local[k], 0)],
            [(0, 0, 0)],
            (False, False),
            scale,
            group,
            1,
            page=(new_page, k),
            pool=pool if k == 0 else None,
            after=after,
        )
        if k == 0:
            updated = results[4]
        started.append(results[:4])
        after = [results[1]]
    far_other = [moved(far_own[k], 1) for k in each]
    far = []
    for k in each:
        results = attend(
            scalars,
            [(far_own[k], 0), (far_other[k], 0)],
            [(local_far[k], 0)] + [(a, 0) for a in got_far[k]],
            [(1, i, 0) for i in range(near)],
            (False, True),
            scale,
            group,
            1,
            after=after,
        )
        far.append((results[:2], moved(results[2], 1)))
        after = [results[1]]
    back = []
    ready = []
    for k in each:
        joined = join_packed(*far[k], scale, after=after)
        back.append(moved(joined, pairs))
        mine, mine_table, theirs, theirs_table = started[k]
        near_keys = [(a, 0) for a in got_near[k]]
        near_at = [(0, i, 0) for i in range(1, near)]
        mine, theirs = (mine, mine_table, 0), (theirs, theirs_table, 0)
        if k + 1 < kv_heads:
            results = attend(
                scalars,
                [(split[k], 0), (other[k], 0)],
                near_keys,
                near_at,
                (False, True),
                scale,
                group,
                1,
                prev=[mine, theirs],
                after=[joined],
            )
            own_part = results[:2]
            other_part = results[2]
        else:
            late_keys = [(a, 0) for a in got_late]
            skipped = (cap - last_pages(cap)) * page_len
            late_at = [(0, i, skipped) for i in range(1, near)]
            early = attend(
                scalars,
                [(other[k], 0)],
                near_keys,
                near_at,
                (False,),
                scale,
                group,
                1,
                prev=[theirs],
                after=[joined],
            )
            (other_part,) = attend(
                scalars,
                [(other[k], 0)],
                late_keys,
                late_at,
                (True,),
                scale,
                group,
                1,
                prev=[(*early, 0)],
            )
            own_part = attend(
                scalars,
                [(split[k], 0)],
                near_keys + late_keys,
                near_at + late_at,
                (False,),
                scale,
                group,
                1,
                prev=[mine],
                after=[other_part],
            )
        ready.append((own_part, moved(other_part, 1)))
        after = [own_part[1]]
    attended = None
    for k in each:
        own, received = ready[k]
        attended = join_out(
            own, [received, back[k]], attended, queries.shape, k, group, scale
        )
    return (attended, updated)


def solution(mesh):
    placed = (
        P(("groups", "pool"), "head", None),
        P(("groups", "pool"), None, "head", None),
        P(("groups", "pool"), None, "head", None, None),
        P("groups", None),
        P("groups"),
        P("groups"),
    )

    return jax.shard_map(
        on_device,
        mesh=mesh,
        in_specs=placed,
        out_specs=(
            P(("groups", "pool"), "head", None),
            P(("groups", "pool"), None, "head", None, None),
        ),
        check_vma=False,
    )
```

```python
import functools

import jax
import jax.numpy as jnp
from jax import lax
from jax.experimental import pallas as pl
from jax.experimental.pallas import tpu as pltpu
from jax.sharding import PartitionSpec as P


log2_e = 1.4426950408889634
hidden_score = -2e30
lowest_top = -1e30
lanes = 128
block_rows = 128
kernel_bytes = 24 << 20


def moved(array, apart):
    count = lax.axis_size("pool")
    return lax.ppermute(array, "pool", [(i, i ^ apart) for i in range(count)])


def whole(array):
    return pl.BlockSpec(array.shape, lambda i, *_: (0,) * len(array.shape))


def diagonal():
    shape = (lanes, lanes)
    return lax.broadcasted_iota(jnp.int32, shape, 0) == lax.broadcasted_iota(jnp.int32, shape, 1)


def as_row(column, eye):
    spread = jnp.where(eye, jnp.broadcast_to(column, (lanes, lanes)), 0.0)
    return jnp.sum(spread, axis=0, keepdims=True)


def as_column(row, eye):
    spread = jnp.where(eye, jnp.broadcast_to(row, (lanes, lanes)), 0.0)
    return jnp.sum(spread, axis=1, keepdims=True)


def in_three(values):
    high = values.astype(jnp.bfloat16)
    rest = values - high.astype(jnp.float32)
    middle = rest.astype(jnp.bfloat16)
    low = (rest - middle.astype(jnp.float32)).astype(jnp.bfloat16)
    return (high, middle, low)


def from_three(ref, begin, count):
    parts = [
        ref[0, begin + i * count : begin + (i + 1) * count].astype(jnp.float32) for i in range(3)
    ]
    return parts[0] + parts[1] + parts[2]


def last_pages(cap):
    return max(1, cap // 4)


def gather_body(owner_ref, table_ref, length_ref, pool_ref, *refs, near, waits, ranges, cap):
    refs = refs[waits:]
    outs = refs[: len(ranges)]
    seen_ref = refs[len(ranges)] if near else None
    slots, sem = refs[-2:]
    lists = sorted({which for which, _, _, _ in ranges})
    owner = owner_ref[0]
    pair = owner >> 1
    slot_count, _, _, page_len, _ = pool_ref.shape
    width = table_ref.shape[1]

    def held(request, holder, j):
        slot = table_ref[request, j] - holder * slot_count
        return slot, (slot >= 0) & (slot < slot_count)

    def look(j, found):
        following = []
        for at, which in enumerate(lists):
            slot, here = held(pair ^ which, owner, j)
            slots[at * (cap + 1) + jnp.minimum(found[at], cap)] = slot
            following.append(found[at] + here.astype(jnp.int32))
        return tuple(following)

    found = lax.fori_loop(0, width, look, (jnp.int32(0),) * len(lists), unroll=16)
    copies = []
    for (which, k, begin, end), out in zip(ranges, outs):
        at = lists.index(which)
        for i in range(begin, end):
            slot = jnp.where(i < found[at], slots[at * (cap + 1) + i], 0)
            copy = pltpu.make_async_copy(
                pool_ref.at[slot, :, k], out.at[0, i - begin], sem.at[len(copies)]
            )
            copy.start()
            copies.append(copy)
    if near:
        asked = [(t, s) for t in range(2) for s in range(near)]

        def count(j, seen):
            following = []
            for (t, s), so_far in zip(asked, seen):
                request = pair ^ (t * near)
                _, there = held(request, owner ^ (2 * s), j)
                inside = jnp.clip(length_ref[request] - j * page_len, 0, page_len)
                following.append(so_far + jnp.where(there, inside, 0))
            return tuple(following)

        seen = lax.fori_loop(0, width, count, (jnp.int32(0),) * len(asked), unroll=8)
        for (t, s), total in zip(asked, seen):
            seen_ref[t, s] = total
    for copy in copies:
        copy.wait()


def gather_pages(owner, table, lengths, pool, ranges, near, cap, after=()):
    _, pair_of, _, page_len, head_dim = pool.shape
    outs = [
        pltpu.VMEM((1, end - begin, pair_of, page_len, head_dim), pool.dtype)
        for _, _, begin, end in ranges
    ]
    copy_count = sum(end - begin for _, _, begin, end in ranges)
    list_count = len({which for which, _, _, _ in ranges})
    specs = [pl.BlockSpec(memory_space=pltpu.VMEM)] * len(outs)
    if near:
        outs.append(jax.ShapeDtypeStruct((2, near), jnp.int32))
        specs.append(pl.BlockSpec(memory_space=pltpu.SMEM))
    results = pl.pallas_call(
        functools.partial(gather_body, near=near, waits=len(after), ranges=ranges, cap=cap),
        out_shape=outs,
        grid_spec=pltpu.PrefetchScalarGridSpec(
            num_scalar_prefetch=3,
            grid=(1,),
            in_specs=[pl.BlockSpec(memory_space=pltpu.HBM)]
            + [pl.BlockSpec(memory_space=pl.ANY)] * len(after),
            out_specs=specs,
            scratch_shapes=[
                pltpu.SMEM((list_count * (cap + 1),), jnp.int32),
                pltpu.SemaphoreType.DMA((copy_count,)),
            ],
        ),
        compiler_params=pltpu.CompilerParams(vmem_limit_bytes=kernel_bytes),
        name="gather_pages",
    )(
        owner,
        pltpu.with_memory_space_constraint(table, pltpu.HBM),
        pltpu.with_memory_space_constraint(lengths, pltpu.HBM),
        pltpu.with_memory_space_constraint(pool, pltpu.HBM),
        *after,
    )
    pages = {(which, k, begin): part for (which, k, begin, _), part in zip(ranges, results)}
    return pages, results[-1]


def attend_body(
    owner_ref,
    seen_ref,
    fresh_ref,
    *refs,
    halves,
    seen_at,
    has_page,
    has_prev,
    packed,
    step_rows,
    tile_rows,
    group,
    scale,
    copies_pool,
    waits,
    page_at,
    row_count,
):
    refs = list(refs)
    q_refs = [refs.pop(0) for _ in range(halves)]
    kv_refs = [refs.pop(0) for _ in seen_at]
    page_ref = refs.pop(0) if has_page else None
    prev_refs = [[refs.pop(0) for _ in range(has_prev)] for _ in range(halves)]
    pool_ref = refs.pop(0) if copies_pool else None
    del refs[:waits]
    out_refs = []
    for h in range(halves):
        out_refs.append([refs.pop(0) for _ in range({True: 1, False: 2, None: 3}[packed[h]])])
    new_pool = refs.pop(0) if copies_pool else None
    wide_values = refs.pop(0)
    tables = []
    for h in range(halves):
        if packed[h] is None:
            tables.append(None)
        else:
            tables.append(refs.pop(0) if packed[h] else out_refs[h][1].at[0])
    if copies_pool:
        staged, sem_in, sem_out = refs
    head = pl.program_id(0)
    step = pl.program_id(1)
    heads = pl.num_programs(0)
    steps = pl.num_programs(1)
    owner = owner_ref[0]
    half = 1 - ((owner & 1) ^ ((owner >> 1) & 1))
    page_len = kv_refs[0].shape[3]
    keys = [ref.shape[1] * page_len for ref in kv_refs]

    if copies_pool:

        @pl.when((head == 0) & (step == 0))
        def _():
            pltpu.make_async_copy(pool_ref, staged, sem_in).start()

        @pl.when((head == 0) & (step == jnp.minimum(1, steps - 1)))
        def _():
            pltpu.make_async_copy(pool_ref, staged, sem_in).wait()
            staged[fresh_ref[owner] - owner * staged.shape[0]] = page_ref[...]
            pltpu.make_async_copy(staged, new_pool, sem_out).start()

    @pl.when(step == 0)
    def _():
        ones = jnp.ones((page_len, lanes), jnp.bfloat16)
        begin = 0
        for ref in kv_refs:
            for p in range(ref.shape[1]):
                wide_values[begin : begin + page_len, :lanes] = ref[0, p, 1]
                wide_values[begin : begin + page_len, lanes:] = ones
                begin += page_len
        if has_page:
            wide_values[begin : begin + page_len, :lanes] = page_ref[1, page_at]
            wide_values[begin : begin + page_len, lanes:] = ones

    eye = diagonal()
    q_count = row_count // block_rows
    limits = []
    for s, at in enumerate(seen_at):
        position = lax.broadcasted_iota(jnp.int32, (1, keys[s]), 1)
        limit = jnp.where(position + at[2] < seen_ref[at[0], at[1]], jnp.inf, hidden_score)
        limits.append(limit.astype(jnp.float32))

    def score(h, t):
        query = q_refs[h][0, t * tile_rows : (t + 1) * tile_rows]
        scores = []
        for s, ref in enumerate(kv_refs):
            key_rows = ref[0, :, 0].reshape(keys[s], lanes)
            product = lax.dot_general(
                query, key_rows, (((1,), (1,)), ((), ())), preferred_element_type=jnp.float32
            )
            scores.append(jnp.minimum(product, limits[s]))
        if has_page:
            product = lax.dot_general(
                query, page_ref[0, page_at], (((1,), (1,)), ((), ())), preferred_element_type=jnp.float32
            )
            key_at = lax.broadcasted_iota(jnp.int32, product.shape, 1)
            if h == 0:
                row_at = lax.broadcasted_iota(jnp.int32, product.shape, 0)
                token = (step * step_rows + t * tile_rows + row_at) // group
                shown = key_at <= token
            else:
                shown = key_at < jnp.where(half == 0, page_len, 0)
            scores.append(jnp.where(shown, product, hidden_score))
        return scores

    def finish(h, t, scores):
        top = jnp.full((tile_rows, 1), lowest_top, jnp.float32)
        for part in scores:
            top = jnp.maximum(top, jnp.max(part, axis=1, keepdims=True))
        scaled_top = top * scale
        weights = [jnp.exp2(part * scale - scaled_top).astype(jnp.bfloat16) for part in scores]
        mixed = jnp.dot(
            jnp.concatenate(weights, axis=1), wide_values[...], preferred_element_type=jnp.float32
        )
        total = mixed[:, lanes:]
        mixed = mixed[:, :lanes]
        first = step * (step_rows // block_rows) + t * (tile_rows // block_rows)
        count = q_count
        for u in range(tile_rows // block_rows):
            inner = slice(u * block_rows, (u + 1) * block_rows)
            outer = slice(t * tile_rows + u * block_rows, t * tile_rows + (u + 1) * block_rows)
            part_top, part_total, part_mixed = top[inner], total[inner], mixed[inner]
            row = first + u
            if has_prev:
                if has_prev == 3:
                    prev_mixed, prev_tops, prev_totals = prev_refs[h]
                    prev_top = prev_tops[0, outer]
                    prev_total = prev_totals[0, outer]
                else:
                    prev_mixed, prev_table = prev_refs[h]
                    prev_top = as_column(prev_table[0, pl.ds(row, 1)], eye)
                    prev_total = as_column(prev_table[0, pl.ds(count + row, 1)], eye)
                joint = jnp.maximum(part_top, prev_top)
                keep = jnp.exp2((part_top - joint) * scale)
                keep_prev = jnp.exp2((prev_top - joint) * scale)
                part_mixed = part_mixed * keep + prev_mixed[0, outer] * keep_prev
                part_total = part_total * keep + prev_total * keep_prev
                part_top = joint
            if packed[h] is None:
                out_refs[h][1][0, outer] = jnp.broadcast_to(part_top, (block_rows, lanes))
                out_refs[h][2][0, outer] = jnp.broadcast_to(part_total, (block_rows, lanes))
            else:
                tables[h][pl.ds(row, 1)] = as_row(part_top, eye)
                tables[h][pl.ds(count + row, 1)] = as_row(part_total, eye)
            if packed[h]:
                at = pl.multiple_of(row * block_rows, block_rows)
                out_refs[h][0][0, pl.ds(at, block_rows)] = part_mixed.astype(jnp.bfloat16)
            else:
                out_refs[h][0][0, outer] = part_mixed

    chains = [(h, t) for t in range(step_rows // tile_rows) for h in range(halves)]
    scores = score(*chains[0])
    for i, chain in enumerate(chains):
        following = score(*chains[i + 1]) if i + 1 < len(chains) else None
        finish(*chain, scores)
        scores = following

    @pl.when(step == steps - 1)
    def _():
        for h in range(halves):
            if packed[h]:
                size = tables[h].shape[0]
                begin = out_refs[h][0].shape[1] - 3 * size
                for i, part in enumerate(in_three(tables[h][...])):
                    out_refs[h][0][0, begin + i * size : begin + (i + 1) * size] = part

    if copies_pool:

        @pl.when((head == heads - 1) & (step == steps - 1))
        def _():
            pltpu.make_async_copy(staged, new_pool, sem_out).wait()


def attend(
    scalars, queries, sources, seen_at, packed, scale, group, heads, page=None, prev=None, pool=None, after=()
):
    halves = len(queries)
    rows = queries[0][0].shape[1]
    size = 2 * (rows // block_rows)
    step_rows = min(rows, 1024 // halves)
    tile_rows = min(step_rows, 256)
    key_count = sum(s.shape[1] * s.shape[3] for s, _ in sources)

    def per_rows(offset):
        return pl.BlockSpec((1, step_rows, lanes), lambda k, i, *_: (k + offset, i, 0))

    def per_head(array, offset):
        tail = array.shape[1:]
        return pl.BlockSpec((1, *tail), lambda k, i, *_: (k + offset,) + (0,) * len(tail))

    anywhere = pl.BlockSpec(memory_space=pl.ANY)
    args = [q for q, _ in queries] + [s for s, _ in sources]
    in_specs = [per_rows(at) for _, at in queries] + [per_head(s, at) for s, at in sources]
    page_at = 0
    if page is not None:
        page, page_at = page
        args.append(page)
        in_specs.append(whole(page))
        key_count += page.shape[2]
    if prev is not None:
        for *state, at in prev:
            args += state
            if len(state) == 3:
                in_specs += [per_rows(at)] * 3
            else:
                in_specs += [per_rows(at), per_head(state[1], at)]
    if pool is not None:
        args.append(pltpu.with_memory_space_constraint(pool, pltpu.HBM))
        in_specs.append(pl.BlockSpec(memory_space=pltpu.HBM))
    args += list(after)
    in_specs += [anywhere] * len(after)
    out_shape = []
    out_specs = []
    scratch = [pltpu.VMEM((key_count, 2 * lanes), jnp.bfloat16)]
    for h in range(halves):
        if packed[h]:
            shape = jax.ShapeDtypeStruct((heads, rows + 3 * size, lanes), jnp.bfloat16)
            out_shape.append(shape)
            out_specs.append(per_head(shape, 0))
            scratch.append(pltpu.VMEM((size, lanes), jnp.float32))
        elif packed[h] is None:
            out_shape += [jax.ShapeDtypeStruct((heads, rows, lanes), jnp.float32)] * 3
            out_specs += [per_rows(0)] * 3
        else:
            table = jax.ShapeDtypeStruct((heads, size, lanes), jnp.float32)
            out_shape += [jax.ShapeDtypeStruct((heads, rows, lanes), jnp.float32), table]
            out_specs += [per_rows(0), per_head(table, 0)]
    if pool is not None:
        out_shape.append(jax.ShapeDtypeStruct(pool.shape, pool.dtype))
        out_specs.append(pl.BlockSpec(memory_space=pltpu.HBM))
        scratch.append(pltpu.VMEM(pool.shape, pool.dtype))
        scratch += [pltpu.SemaphoreType.DMA, pltpu.SemaphoreType.DMA]
    work = halves * heads * rows * key_count
    return pl.pallas_call(
        functools.partial(
            attend_body,
            halves=halves,
            seen_at=seen_at,
            has_page=page is not None,
            has_prev=len(prev[0]) - 1 if prev else 0,
            packed=packed,
            step_rows=step_rows,
            tile_rows=tile_rows,
            group=group,
            scale=scale,
            copies_pool=pool is not None,
            waits=len(after),
            page_at=page_at,
            row_count=rows,
        ),
        out_shape=out_shape,
        grid_spec=pltpu.PrefetchScalarGridSpec(
            num_scalar_prefetch=3,
            grid=(heads, rows // step_rows),
            in_specs=in_specs,
            out_specs=out_specs,
            scratch_shapes=scratch,
        ),
        cost_estimate=pl.CostEstimate(
            flops=4 * work * lanes,
            transcendentals=work,
            bytes_accessed=4 * heads * key_count * lanes,
        ),
        compiler_params=pltpu.CompilerParams(vmem_limit_bytes=kernel_bytes),
        name="attend",
    )(*scalars, *args)


def join_body(own_mixed, own_table, *refs, scale, packs, waits):
    refs = list(refs)
    shares = refs.pop()
    out_ref = refs.pop()
    if waits:
        del refs[-waits:]
    size = own_table.shape[1]
    count = size // 2
    rows = count * block_rows
    step = pl.program_id(0)
    blocks = own_mixed.shape[1] // block_rows
    eye = diagonal()

    @pl.when(step == 0)
    def _():
        tops = [own_table[0, :count]]
        totals = [own_table[0, count:]]
        for ref in refs:
            table = from_three(ref, rows, size)
            tops.append(table[:count])
            totals.append(table[count:])
        top = functools.reduce(jnp.maximum, tops)
        keeps = [jnp.exp2((t - top) * scale) for t in tops]
        total = sum(t * keep for t, keep in zip(totals, keeps))
        for i, keep in enumerate(keeps):
            shares[i] = keep if packs else keep / total
        if packs:
            table = jnp.concatenate([top, total], axis=0)
            for i, part in enumerate(in_three(table)):
                out_ref[0, rows + i * size : rows + (i + 1) * size] = part

    for t in range(blocks):
        row = step * blocks + t
        at = slice(t * block_rows, (t + 1) * block_rows)
        begin = pl.multiple_of(row * block_rows, block_rows)
        mixed = own_mixed[0, at] * as_column(shares[0, pl.ds(row, 1)], eye)
        for i, ref in enumerate(refs):
            part = ref[0, pl.ds(begin, block_rows)].astype(jnp.float32)
            mixed = mixed + part * as_column(shares[i + 1, pl.ds(row, 1)], eye)
        if packs:
            out_ref[0, at] = mixed.astype(jnp.bfloat16)
        else:
            heads = out_ref.shape[1]
            tokens = block_rows // heads
            shaped = mixed.reshape(tokens, heads, lanes)
            out_ref[t * tokens : (t + 1) * tokens] = shaped.astype(jnp.bfloat16)


def join_packed(own, received, scale, after=()):
    mixed, table = own
    args = [mixed, table, received]
    return pl.pallas_call(
        functools.partial(join_body, scale=scale, packs=True, waits=len(after)),
        out_shape=jax.ShapeDtypeStruct(received.shape, received.dtype),
        grid=(1,),
        in_specs=[whole(a) for a in args] + [pl.BlockSpec(memory_space=pl.ANY)] * len(after),
        out_specs=whole(received),
        scratch_shapes=[pltpu.VMEM((2, table.shape[1] // 2, lanes), jnp.float32)],
        compiler_params=pltpu.CompilerParams(vmem_limit_bytes=kernel_bytes),
        name="join_packed",
    )(*args, *after)


def join_out(own, received, target, shape, index, group, scale):
    mixed, table = own
    args = [mixed, table, *received]
    in_specs = [whole(a) for a in args]
    steps = 2
    rows = mixed.shape[1] // steps
    in_specs[0] = pl.BlockSpec((1, rows, lanes), lambda i: (0, i, 0))
    aliases = {}
    if target is not None:
        aliases = {len(args): 0}
        args.append(target)
        in_specs.append(pl.BlockSpec(memory_space=pl.ANY))
    return pl.pallas_call(
        functools.partial(join_body, scale=scale, packs=False, waits=len(aliases)),
        out_shape=jax.ShapeDtypeStruct(shape, jnp.bfloat16),
        grid=(steps,),
        in_specs=in_specs,
        out_specs=pl.BlockSpec((shape[0] // steps, group, shape[2]), lambda i: (i, index, 0)),
        scratch_shapes=[pltpu.VMEM((len(received) + 1, table.shape[1] // 2, lanes), jnp.float32)],
        input_output_aliases=aliases,
        compiler_params=pltpu.CompilerParams(vmem_limit_bytes=kernel_bytes),
        name="join_out",
    )(*args)


def on_device(queries, new_kv, pool, block_table, prefix_len, new_slots):
    owner_count = lax.axis_size("pool")
    owner = lax.axis_index("pool").astype(jnp.int32)
    _, _, kv_heads, page_len, head_dim = pool.shape
    tokens, q_heads, _ = queries.shape
    group = q_heads // kv_heads
    rows = tokens * group
    pairs = owner_count // 2
    near = pairs // 2
    cap = block_table.shape[1] // owner_count
    scale = head_dim**-0.5 * log2_e
    each = range(kv_heads)

    owner_list = jnp.full((1,), owner, jnp.int32)
    split = [
        queries[:, k * group : (k + 1) * group].reshape(1, rows, head_dim) for k in each
    ]
    new_page = new_kv.transpose(1, 2, 0, 3)
    far_own = [moved(split[k], pairs) for k in each]
    other = [moved(split[k], 1) for k in each]
    lookup = (owner_list, block_table, prefix_len, pool)
    last = kv_heads - 1
    cut = cap - last_pages(cap)
    ring = range(1, near)
    ranges = [(near + i, 0, 0, cap) for i in ring]
    pages, _ = gather_pages(*lookup, ranges, 0, cap)
    ranges = [(near + i, k, 0, cap) for k in each if k for i in ring]
    ranges += [(i, k, 0, cut if k == last else cap) for k in each for i in ring]
    ranges += [(i, last, cut, cap) for i in ring]
    ranges += [(i, k, 0, cap) for i in (0, near) for k in each]
    more, seen = gather_pages(*lookup, ranges, near, cap, after=[new_page])
    pages = {**pages, **more}

    def exchanged(first, k, begin):
        return [moved(pages[first + i, k, begin], 2 * i) for i in ring]

    got_far = [exchanged(near, k, 0) for k in each]
    got_near = [exchanged(0, k, 0) for k in each]
    got_late = exchanged(0, last, cut)
    local, local_far = [[pages[i, k, 0] for k in each] for i in (0, near)]
    scalars = (owner_list, seen, new_slots)

    started = []
    updated = None
    after = []
    for k in each:
        results = attend(
            scalars,
            [(split[k], 0), (other[k], 0)],
            [(local[k], 0)],
            [(0, 0, 0)],
            (False, False),
            scale,
            group,
            1,
            page=(new_page, k),
            pool=pool if k == 0 else None,
            after=after,
        )
        if k == 0:
            updated = results[4]
        started.append(results[:4])
        after = [results[1]]
    far_other = [moved(far_own[k], 1) for k in each]
    far = []
    for k in each:
        results = attend(
            scalars,
            [(far_own[k], 0), (far_other[k], 0)],
            [(local_far[k], 0)] + [(a, 0) for a in got_far[k]],
            [(1, i, 0) for i in range(near)],
            (False, True),
            scale,
            group,
            1,
            after=after,
        )
        far.append((results[:2], moved(results[2], 1)))
        after = [results[1]]
    back = []
    ready = []
    for k in each:
        joined = join_packed(*far[k], scale, after=after)
        back.append(moved(joined, pairs))
        mine, mine_table, theirs, theirs_table = started[k]
        near_keys = [(a, 0) for a in got_near[k]]
        near_at = [(0, i, 0) for i in range(1, near)]
        mine, theirs = (mine, mine_table, 0), (theirs, theirs_table, 0)
        if k + 1 < kv_heads:
            results = attend(
                scalars,
                [(split[k], 0), (other[k], 0)],
                near_keys,
                near_at,
                (False, True),
                scale,
                group,
                1,
                prev=[mine, theirs],
                after=[joined],
            )
            own_part = results[:2]
            other_part = results[2]
        else:
            late_keys = [(a, 0) for a in got_late]
            late_at = [(0, i, cut * page_len) for i in range(1, near)]
            early = attend(
                scalars,
                [(other[k], 0)],
                near_keys,
                near_at,
                (None,),
                scale,
                group,
                1,
                prev=[theirs],
                after=[joined],
            )
            (other_part,) = attend(
                scalars,
                [(other[k], 0)],
                late_keys,
                late_at,
                (True,),
                scale,
                group,
                1,
                prev=[(*early, 0)],
            )
            own_part = attend(
                scalars,
                [(split[k], 0)],
                near_keys + late_keys,
                near_at + late_at,
                (False,),
                scale,
                group,
                1,
                prev=[mine],
                after=[other_part],
            )
        ready.append((own_part, moved(other_part, 1)))
        after = [own_part[1]]
    attended = None
    for k in each:
        own, received = ready[k]
        attended = join_out(
            own, [received, back[k]], attended, queries.shape, k, group, scale
        )
    return (attended, updated)


def solution(mesh):
    placed = (
        P(("groups", "pool"), "head", None),
        P(("groups", "pool"), None, "head", None),
        P(("groups", "pool"), None, "head", None, None),
        P("groups", None),
        P("groups"),
        P("groups"),
    )

    return jax.shard_map(
        on_device,
        mesh=mesh,
        in_specs=placed,
        out_specs=(
            P(("groups", "pool"), "head", None),
            P(("groups", "pool"), None, "head", None, None),
        ),
        check_vma=False,
    )
```

```python
import functools

import jax
import jax.numpy as jnp
from jax import lax
from jax.experimental import pallas as pl
from jax.experimental.pallas import tpu as pltpu
from jax.sharding import PartitionSpec as P


log2_e = 1.4426950408889634
hidden_score = -2e30
lowest_top = -1e30
lanes = 128
block_rows = 128
kernel_bytes = 24 << 20


def moved(array, apart):
    count = lax.axis_size("pool")
    return lax.ppermute(array, "pool", [(i, i ^ apart) for i in range(count)])


def whole(array):
    return pl.BlockSpec(array.shape, lambda i, *_: (0,) * len(array.shape))


def diagonal():
    shape = (lanes, lanes)
    return lax.broadcasted_iota(jnp.int32, shape, 0) == lax.broadcasted_iota(jnp.int32, shape, 1)


def as_row(column, eye):
    spread = jnp.where(eye, jnp.broadcast_to(column, (lanes, lanes)), 0.0)
    return jnp.sum(spread, axis=0, keepdims=True)


def as_column(row, eye):
    spread = jnp.where(eye, jnp.broadcast_to(row, (lanes, lanes)), 0.0)
    return jnp.sum(spread, axis=1, keepdims=True)


def in_three(values):
    high = values.astype(jnp.bfloat16)
    rest = values - high.astype(jnp.float32)
    middle = rest.astype(jnp.bfloat16)
    low = (rest - middle.astype(jnp.float32)).astype(jnp.bfloat16)
    return (high, middle, low)


def from_three(ref, begin, count):
    parts = [
        ref[0, begin + i * count : begin + (i + 1) * count].astype(jnp.float32) for i in range(3)
    ]
    return parts[0] + parts[1] + parts[2]


def last_pages(cap):
    return max(1, cap // 4)


def gather_body(owner_ref, table_ref, length_ref, pool_ref, *refs, near, waits, ranges, cap):
    refs = refs[waits:]
    outs = refs[: len(ranges)]
    seen_ref = refs[len(ranges)] if near else None
    slots, sem = refs[-2:]
    lists = sorted({which for which, _, _, _ in ranges})
    owner = owner_ref[0]
    pair = owner >> 1
    slot_count, _, _, page_len, _ = pool_ref.shape
    width = table_ref.shape[1]

    def held(request, holder, j):
        slot = table_ref[request, j] - holder * slot_count
        return slot, (slot >= 0) & (slot < slot_count)

    def look(j, found):
        following = []
        for at, which in enumerate(lists):
            slot, here = held(pair ^ which, owner, j)
            slots[at * (cap + 1) + jnp.minimum(found[at], cap)] = slot
            following.append(found[at] + here.astype(jnp.int32))
        return tuple(following)

    found = lax.fori_loop(0, width, look, (jnp.int32(0),) * len(lists), unroll=16)
    copies = []
    for (which, k, begin, end), out in zip(ranges, outs):
        at = lists.index(which)
        for i in range(begin, end):
            slot = jnp.where(i < found[at], slots[at * (cap + 1) + i], 0)
            copy = pltpu.make_async_copy(
                pool_ref.at[slot, :, k], out.at[0, i - begin], sem.at[len(copies)]
            )
            copy.start()
            copies.append(copy)
    if near:
        asked = [(t, s) for t in range(3) for s in range(near)]

        def count(j, seen):
            following = []
            for (t, s), so_far in zip(asked, seen):
                request = pair ^ (near if t == 1 else 0)
                _, there = held(request, owner ^ (2 * s + t // 2), j)
                inside = jnp.clip(length_ref[request] - j * page_len, 0, page_len)
                following.append(so_far + jnp.where(there, inside, 0))
            return tuple(following)

        seen = lax.fori_loop(0, width, count, (jnp.int32(0),) * len(asked), unroll=8)
        for (t, s), total in zip(asked, seen):
            seen_ref[t, s] = total
    for copy in copies:
        copy.wait()


def gather_pages(owner, table, lengths, pool, ranges, near, cap, after=()):
    _, pair_of, _, page_len, head_dim = pool.shape
    outs = [
        pltpu.VMEM((1, end - begin, pair_of, page_len, head_dim), pool.dtype)
        for _, _, begin, end in ranges
    ]
    copy_count = sum(end - begin for _, _, begin, end in ranges)
    list_count = len({which for which, _, _, _ in ranges})
    specs = [pl.BlockSpec(memory_space=pltpu.VMEM)] * len(outs)
    if near:
        outs.append(jax.ShapeDtypeStruct((3, near), jnp.int32))
        specs.append(pl.BlockSpec(memory_space=pltpu.SMEM))
    results = pl.pallas_call(
        functools.partial(gather_body, near=near, waits=len(after), ranges=ranges, cap=cap),
        out_shape=outs,
        grid_spec=pltpu.PrefetchScalarGridSpec(
            num_scalar_prefetch=3,
            grid=(1,),
            in_specs=[pl.BlockSpec(memory_space=pltpu.HBM)]
            + [pl.BlockSpec(memory_space=pl.ANY)] * len(after),
            out_specs=specs,
            scratch_shapes=[
                pltpu.SMEM((list_count * (cap + 1),), jnp.int32),
                pltpu.SemaphoreType.DMA((copy_count,)),
            ],
        ),
        compiler_params=pltpu.CompilerParams(vmem_limit_bytes=kernel_bytes),
        name="gather_pages",
    )(
        owner,
        pltpu.with_memory_space_constraint(table, pltpu.HBM),
        pltpu.with_memory_space_constraint(lengths, pltpu.HBM),
        pltpu.with_memory_space_constraint(pool, pltpu.HBM),
        *after,
    )
    pages = {(which, k, begin): part for (which, k, begin, _), part in zip(ranges, results)}
    return pages, results[-1]


def attend_body(
    owner_ref,
    seen_ref,
    fresh_ref,
    *refs,
    halves,
    seen_at,
    has_page,
    has_prev,
    packed,
    step_rows,
    tile_rows,
    group,
    scale,
    copies_pool,
    waits,
    page_at,
):
    refs = list(refs)
    q_refs = [refs.pop(0) for _ in range(halves)]
    kv_refs = [refs.pop(0) for _ in seen_at]
    page_ref = refs.pop(0) if has_page else None
    prev_refs = [(refs.pop(0), refs.pop(0)) for _ in range(halves)] if has_prev else None
    pool_ref = refs.pop(0) if copies_pool else None
    del refs[:waits]
    out_refs = []
    for h in range(halves):
        out_refs.append((refs.pop(0),) if packed[h] else (refs.pop(0), refs.pop(0)))
    new_pool = refs.pop(0) if copies_pool else None
    wide_values = refs.pop(0)
    tables = [refs.pop(0) if packed[h] else out_refs[h][1].at[0] for h in range(halves)]
    if copies_pool:
        staged, sem_in, sem_out = refs
    head = pl.program_id(0)
    step = pl.program_id(1)
    heads = pl.num_programs(0)
    steps = pl.num_programs(1)
    owner = owner_ref[0]
    half = 1 - ((owner & 1) ^ ((owner >> 1) & 1))
    page_len = kv_refs[0].shape[3]
    keys = [ref.shape[1] * page_len for ref in kv_refs]

    if copies_pool:

        @pl.when((head == 0) & (step == 0))
        def _():
            pltpu.make_async_copy(pool_ref, staged, sem_in).start()

        @pl.when((head == 0) & (step == jnp.minimum(1, steps - 1)))
        def _():
            pltpu.make_async_copy(pool_ref, staged, sem_in).wait()
            staged[fresh_ref[owner] - owner * staged.shape[0]] = page_ref[...]
            pltpu.make_async_copy(staged, new_pool, sem_out).start()

    @pl.when(step == 0)
    def _():
        ones = jnp.ones((page_len, lanes), jnp.bfloat16)
        begin = 0
        for ref in kv_refs:
            for p in range(ref.shape[1]):
                wide_values[begin : begin + page_len, :lanes] = ref[0, p, 1]
                wide_values[begin : begin + page_len, lanes:] = ones
                begin += page_len
        if has_page:
            wide_values[begin : begin + page_len, :lanes] = page_ref[1, page_at]
            wide_values[begin : begin + page_len, lanes:] = ones

    eye = diagonal()
    limits = []
    for s, at in enumerate(seen_at):
        position = lax.broadcasted_iota(jnp.int32, (1, keys[s]), 1)
        limit = jnp.where(position + at[2] < seen_ref[at[0], at[1]], jnp.inf, hidden_score)
        limits.append(limit.astype(jnp.float32))

    def score(h, t):
        query = q_refs[h][0, t * tile_rows : (t + 1) * tile_rows]
        scores = []
        for s, ref in enumerate(kv_refs):
            key_rows = ref[0, :, 0].reshape(keys[s], lanes)
            product = lax.dot_general(
                query, key_rows, (((1,), (1,)), ((), ())), preferred_element_type=jnp.float32
            )
            scores.append(jnp.minimum(product, limits[s]))
        if has_page:
            product = lax.dot_general(
                query, page_ref[0, page_at], (((1,), (1,)), ((), ())), preferred_element_type=jnp.float32
            )
            key_at = lax.broadcasted_iota(jnp.int32, product.shape, 1)
            if h == 0:
                row_at = lax.broadcasted_iota(jnp.int32, product.shape, 0)
                token = (step * step_rows + t * tile_rows + row_at) // group
                shown = key_at <= token
            else:
                shown = key_at < jnp.where(half == 0, page_len, 0)
            scores.append(jnp.where(shown, product, hidden_score))
        return scores

    def finish(h, t, scores):
        top = jnp.full((tile_rows, 1), lowest_top, jnp.float32)
        for part in scores:
            top = jnp.maximum(top, jnp.max(part, axis=1, keepdims=True))
        scaled_top = top * scale
        weights = [jnp.exp2(part * scale - scaled_top).astype(jnp.bfloat16) for part in scores]
        mixed = jnp.dot(
            jnp.concatenate(weights, axis=1), wide_values[...], preferred_element_type=jnp.float32
        )
        total = mixed[:, lanes:]
        mixed = mixed[:, :lanes]
        first = step * (step_rows // block_rows) + t * (tile_rows // block_rows)
        count = tables[h].shape[0] // 2
        for u in range(tile_rows // block_rows):
            inner = slice(u * block_rows, (u + 1) * block_rows)
            outer = slice(t * tile_rows + u * block_rows, t * tile_rows + (u + 1) * block_rows)
            part_top, part_total, part_mixed = top[inner], total[inner], mixed[inner]
            row = first + u
            if has_prev:
                prev_mixed, prev_table = prev_refs[h]
                prev_top = as_column(prev_table[0, pl.ds(row, 1)], eye)
                prev_total = as_column(prev_table[0, pl.ds(count + row, 1)], eye)
                joint = jnp.maximum(part_top, prev_top)
                keep = jnp.exp2((part_top - joint) * scale)
                keep_prev = jnp.exp2((prev_top - joint) * scale)
                part_mixed = part_mixed * keep + prev_mixed[0, outer] * keep_prev
                part_total = part_total * keep + prev_total * keep_prev
                part_top = joint
            tables[h][pl.ds(row, 1)] = as_row(part_top, eye)
            tables[h][pl.ds(count + row, 1)] = as_row(part_total, eye)
            if packed[h]:
                at = pl.multiple_of(row * block_rows, block_rows)
                out_refs[h][0][0, pl.ds(at, block_rows)] = part_mixed.astype(jnp.bfloat16)
            else:
                out_refs[h][0][0, outer] = part_mixed

    chains = [(h, t) for t in range(step_rows // tile_rows) for h in range(halves)]
    scores = score(*chains[0])
    for i, chain in enumerate(chains):
        following = score(*chains[i + 1]) if i + 1 < len(chains) else None
        finish(*chain, scores)
        scores = following

    @pl.when(step == steps - 1)
    def _():
        for h in range(halves):
            if packed[h]:
                size = tables[h].shape[0]
                begin = out_refs[h][0].shape[1] - 3 * size
                for i, part in enumerate(in_three(tables[h][...])):
                    out_refs[h][0][0, begin + i * size : begin + (i + 1) * size] = part

    if copies_pool:

        @pl.when((head == heads - 1) & (step == steps - 1))
        def _():
            pltpu.make_async_copy(staged, new_pool, sem_out).wait()


def attend(
    scalars, queries, sources, seen_at, packed, scale, group, heads, page=None, prev=None, pool=None, after=()
):
    halves = len(queries)
    rows = queries[0][0].shape[1]
    size = 2 * (rows // block_rows)
    step_rows = min(rows, 1024 // halves)
    tile_rows = min(step_rows, 256)
    key_count = sum(s.shape[1] * s.shape[3] for s, _ in sources)

    def per_rows(offset):
        return pl.BlockSpec((1, step_rows, lanes), lambda k, i, *_: (k + offset, i, 0))

    def per_head(array, offset):
        tail = array.shape[1:]
        return pl.BlockSpec((1, *tail), lambda k, i, *_: (k + offset,) + (0,) * len(tail))

    anywhere = pl.BlockSpec(memory_space=pl.ANY)
    args = [q for q, _ in queries] + [s for s, _ in sources]
    in_specs = [per_rows(at) for _, at in queries] + [per_head(s, at) for s, at in sources]
    page_at = 0
    if page is not None:
        page, page_at = page
        args.append(page)
        in_specs.append(whole(page))
        key_count += page.shape[2]
    if prev is not None:
        for mixed, table, at in prev:
            args += [mixed, table]
            in_specs += [per_rows(at), per_head(table, at)]
    if pool is not None:
        args.append(pltpu.with_memory_space_constraint(pool, pltpu.HBM))
        in_specs.append(pl.BlockSpec(memory_space=pltpu.HBM))
    args += list(after)
    in_specs += [anywhere] * len(after)
    out_shape = []
    out_specs = []
    scratch = [pltpu.VMEM((key_count, 2 * lanes), jnp.bfloat16)]
    for h in range(halves):
        if packed[h]:
            shape = jax.ShapeDtypeStruct((heads, rows + 3 * size, lanes), jnp.bfloat16)
            out_shape.append(shape)
            out_specs.append(per_head(shape, 0))
            scratch.append(pltpu.VMEM((size, lanes), jnp.float32))
        else:
            table = jax.ShapeDtypeStruct((heads, size, lanes), jnp.float32)
            out_shape += [jax.ShapeDtypeStruct((heads, rows, lanes), jnp.float32), table]
            out_specs += [per_rows(0), per_head(table, 0)]
    if pool is not None:
        out_shape.append(jax.ShapeDtypeStruct(pool.shape, pool.dtype))
        out_specs.append(pl.BlockSpec(memory_space=pltpu.HBM))
        scratch.append(pltpu.VMEM(pool.shape, pool.dtype))
        scratch += [pltpu.SemaphoreType.DMA, pltpu.SemaphoreType.DMA]
    work = halves * heads * rows * key_count
    return pl.pallas_call(
        functools.partial(
            attend_body,
            halves=halves,
            seen_at=seen_at,
            has_page=page is not None,
            has_prev=prev is not None,
            packed=packed,
            step_rows=step_rows,
            tile_rows=tile_rows,
            group=group,
            scale=scale,
            copies_pool=pool is not None,
            waits=len(after),
            page_at=page_at,
        ),
        out_shape=out_shape,
        grid_spec=pltpu.PrefetchScalarGridSpec(
            num_scalar_prefetch=3,
            grid=(heads, rows // step_rows),
            in_specs=in_specs,
            out_specs=out_specs,
            scratch_shapes=scratch,
        ),
        cost_estimate=pl.CostEstimate(
            flops=4 * work * lanes,
            transcendentals=work,
            bytes_accessed=4 * heads * key_count * lanes,
        ),
        compiler_params=pltpu.CompilerParams(vmem_limit_bytes=kernel_bytes),
        name="attend",
    )(*scalars, *args)


def join_body(own_mixed, own_table, *refs, scale, packs, waits):
    refs = list(refs)
    out_ref = refs.pop()
    if waits:
        del refs[-waits:]
    size = own_table.shape[1]
    count = size // 2
    rows = count * block_rows
    eye = diagonal()
    tops = [own_table[0, :count]]
    totals = [own_table[0, count:]]
    for ref in refs:
        table = from_three(ref, rows, size)
        tops.append(table[:count])
        totals.append(table[count:])
    top = functools.reduce(jnp.maximum, tops)
    keeps = [jnp.exp2((t - top) * scale) for t in tops]
    total = sum(t * keep for t, keep in zip(totals, keeps))
    if not packs:
        keeps = [keep / total for keep in keeps]
    for t in range(count):
        at = slice(t * block_rows, (t + 1) * block_rows)
        mixed = own_mixed[0, at] * as_column(keeps[0][t : t + 1], eye)
        for ref, keep in zip(refs, keeps[1:]):
            mixed = mixed + ref[0, at].astype(jnp.float32) * as_column(keep[t : t + 1], eye)
        if packs:
            out_ref[0, at] = mixed.astype(jnp.bfloat16)
        else:
            heads = out_ref.shape[1]
            tokens = block_rows // heads
            shaped = mixed.reshape(tokens, heads, lanes)
            out_ref[t * tokens : (t + 1) * tokens] = shaped.astype(jnp.bfloat16)
    if packs:
        table = jnp.concatenate([top, total], axis=0)
        for i, part in enumerate(in_three(table)):
            out_ref[0, rows + i * size : rows + (i + 1) * size] = part


def join_packed(own, received, scale, after=()):
    mixed, table = own
    args = [mixed, table, received]
    return pl.pallas_call(
        functools.partial(join_body, scale=scale, packs=True, waits=len(after)),
        out_shape=jax.ShapeDtypeStruct(received.shape, received.dtype),
        grid=(1,),
        in_specs=[whole(a) for a in args] + [pl.BlockSpec(memory_space=pl.ANY)] * len(after),
        out_specs=whole(received),
        compiler_params=pltpu.CompilerParams(vmem_limit_bytes=kernel_bytes),
        name="join_packed",
    )(*args, *after)


def join_out(own, received, target, shape, index, group, scale):
    mixed, table = own
    args = [mixed, table, *received]
    in_specs = [whole(a) for a in args]
    aliases = {}
    if target is not None:
        aliases = {len(args): 0}
        args.append(target)
        in_specs.append(pl.BlockSpec(memory_space=pl.ANY))
    return pl.pallas_call(
        functools.partial(join_body, scale=scale, packs=False, waits=len(aliases)),
        out_shape=jax.ShapeDtypeStruct(shape, jnp.bfloat16),
        grid=(1,),
        in_specs=in_specs,
        out_specs=pl.BlockSpec((shape[0], group, shape[2]), lambda i: (0, index, 0)),
        input_output_aliases=aliases,
        compiler_params=pltpu.CompilerParams(vmem_limit_bytes=kernel_bytes),
        name="join_out",
    )(*args)


def on_device(queries, new_kv, pool, block_table, prefix_len, new_slots):
    owner_count = lax.axis_size("pool")
    owner = lax.axis_index("pool").astype(jnp.int32)
    _, _, kv_heads, page_len, head_dim = pool.shape
    tokens, q_heads, _ = queries.shape
    group = q_heads // kv_heads
    rows = tokens * group
    pairs = owner_count // 2
    near = pairs // 2
    cap = block_table.shape[1] // owner_count
    scale = head_dim**-0.5 * log2_e
    each = range(kv_heads)

    owner_list = jnp.full((1,), owner, jnp.int32)
    split = [
        queries[:, k * group : (k + 1) * group].reshape(1, rows, head_dim) for k in each
    ]
    new_page = new_kv.transpose(1, 2, 0, 3)
    far_own = [moved(split[k], pairs) for k in each]
    other = [moved(split[k], 1) for k in each]
    lookup = (owner_list, block_table, prefix_len, pool)
    last = kv_heads - 1
    cut = cap - last_pages(cap)
    ring = range(1, near)
    ranges = [(near + i, 0, 0, cap) for i in ring]
    pages, _ = gather_pages(*lookup, ranges, 0, cap)
    ranges = [(near + i, k, 0, cap) for k in each if k for i in ring]
    ranges += [(i, k, 0, cut if k == last else cap) for k in each for i in ring]
    ranges += [(i, last, cut, cap) for i in ring]
    ranges += [(i, k, 0, cap) for i in (0, near) for k in each]
    more, seen = gather_pages(*lookup, ranges, near, cap, after=[new_page])
    pages = {**pages, **more}

    def exchanged(first, k, begin):
        return [moved(pages[first + i, k, begin], 2 * i) for i in ring]

    got_far = [exchanged(near, k, 0) for k in each]
    got_near = [exchanged(0, k, 0) for k in each]
    got_late = [moved(pages[i, last, cut], 2 * i) for i in ring]
    theirs_late = [moved(pages[i, last, cut], 1) for i in ring]
    got_late += [moved(part, 2 * i) for i, part in zip(ring, theirs_late)]
    local, local_far = [[pages[i, k, 0] for k in each] for i in (0, near)]
    scalars = (owner_list, seen, new_slots)

    started = []
    updated = None
    after = []
    for k in each:
        results = attend(
            scalars,
            [(split[k], 0), (other[k], 0)],
            [(local[k], 0)],
            [(0, 0, 0)],
            (False, False),
            scale,
            group,
            1,
            page=(new_page, k),
            pool=pool if k == 0 else None,
            after=after,
        )
        if k == 0:
            updated = results[4]
        started.append(results[:4])
        after = [results[1]]
    far_other = [moved(far_own[k], 1) for k in each]
    far = []
    for k in each:
        results = attend(
            scalars,
            [(far_own[k], 0), (far_other[k], 0)],
            [(local_far[k], 0)] + [(a, 0) for a in got_far[k]],
            [(1, i, 0) for i in range(near)],
            (False, True),
            scale,
            group,
            1,
            after=after,
        )
        far.append((results[:2], moved(results[2], 1)))
        after = [results[1]]
    back = []
    ready = []
    for k in each:
        joined = join_packed(*far[k], scale, after=after)
        back.append(moved(joined, pairs))
        mine, mine_table, theirs, theirs_table = started[k]
        near_keys = [(a, 0) for a in got_near[k]]
        near_at = [(0, i, 0) for i in range(1, near)]
        mine, theirs = (mine, mine_table, 0), (theirs, theirs_table, 0)
        if k + 1 < kv_heads:
            results = attend(
                scalars,
                [(split[k], 0), (other[k], 0)],
                near_keys,
                near_at,
                (False, True),
                scale,
                group,
                1,
                prev=[mine, theirs],
                after=[joined],
            )
            own_part = results[:2]
            other_part = results[2]
        else:
            late_keys = [(a, 0) for a in got_late]
            late_at = [(t, i, cut * page_len) for t in (0, 2) for i in ring]
            (other_part,) = attend(
                scalars,
                [(other[k], 0)],
                near_keys,
                near_at,
                (True,),
                scale,
                group,
                1,
                prev=[theirs],
                after=[joined],
            )
            early = attend(
                scalars,
                [(split[k], 0)],
                near_keys,
                near_at,
                (False,),
                scale,
                group,
                1,
                prev=[mine],
                after=[other_part],
            )
            own_part = attend(
                scalars,
                [(split[k], 0)],
                late_keys,
                late_at,
                (False,),
                scale,
                group,
                1,
                prev=[(*early, 0)],
            )
        ready.append((own_part, moved(other_part, 1)))
        after = [own_part[1]]
    attended = None
    for k in each:
        own, received = ready[k]
        attended = join_out(
            own, [received, back[k]], attended, queries.shape, k, group, scale
        )
    return (attended, updated)


def solution(mesh):
    placed = (
        P(("groups", "pool"), "head", None),
        P(("groups", "pool"), None, "head", None),
        P(("groups", "pool"), None, "head", None, None),
        P("groups", None),
        P("groups"),
        P("groups"),
    )

    return jax.shard_map(
        on_device,
        mesh=mesh,
        in_specs=placed,
        out_specs=(
            P(("groups", "pool"), "head", None),
            P(("groups", "pool"), None, "head", None, None),
        ),
        check_vma=False,
    )
```

```python
import functools

import jax
import jax.numpy as jnp
from jax import lax
from jax.experimental import pallas as pl
from jax.experimental.pallas import tpu as pltpu
from jax.sharding import PartitionSpec as P


log2_e = 1.4426950408889634
hidden_score = -2e30
lowest_top = -1e30
lanes = 128
block_rows = 128
kernel_bytes = 24 << 20


def moved(array, apart):
    count = lax.axis_size("pool")
    return lax.ppermute(array, "pool", [(i, i ^ apart) for i in range(count)])


def whole(array):
    return pl.BlockSpec(array.shape, lambda i, *_: (0,) * len(array.shape))


def diagonal():
    shape = (lanes, lanes)
    return lax.broadcasted_iota(jnp.int32, shape, 0) == lax.broadcasted_iota(jnp.int32, shape, 1)


def as_row(column, eye):
    spread = jnp.where(eye, jnp.broadcast_to(column, (lanes, lanes)), 0.0)
    return jnp.sum(spread, axis=0, keepdims=True)


def as_column(row, eye):
    spread = jnp.where(eye, jnp.broadcast_to(row, (lanes, lanes)), 0.0)
    return jnp.sum(spread, axis=1, keepdims=True)


def in_three(values):
    high = values.astype(jnp.bfloat16)
    rest = values - high.astype(jnp.float32)
    middle = rest.astype(jnp.bfloat16)
    low = (rest - middle.astype(jnp.float32)).astype(jnp.bfloat16)
    return (high, middle, low)


def from_three(ref, begin, count):
    parts = [
        ref[0, begin + i * count : begin + (i + 1) * count].astype(jnp.float32) for i in range(3)
    ]
    return parts[0] + parts[1] + parts[2]


def last_pages(cap):
    return max(1, 3 * cap // 8)


def gather_body(owner_ref, table_ref, length_ref, pool_ref, *refs, near, waits, ranges, cap):
    refs = refs[waits:]
    outs = refs[: len(ranges)]
    seen_ref = refs[len(ranges)] if near else None
    slots, sem = refs[-2:]
    lists = sorted({which for which, _, _, _ in ranges})
    owner = owner_ref[0]
    pair = owner >> 1
    slot_count, _, _, page_len, _ = pool_ref.shape
    width = table_ref.shape[1]

    def held(request, holder, j):
        slot = table_ref[request, j] - holder * slot_count
        return slot, (slot >= 0) & (slot < slot_count)

    def look(j, found):
        following = []
        for at, which in enumerate(lists):
            slot, here = held(pair ^ which, owner, j)
            slots[at * (cap + 1) + jnp.minimum(found[at], cap)] = slot
            following.append(found[at] + here.astype(jnp.int32))
        return tuple(following)

    found = lax.fori_loop(0, width, look, (jnp.int32(0),) * len(lists), unroll=16)
    copies = []
    for (which, k, begin, end), out in zip(ranges, outs):
        at = lists.index(which)
        for i in range(begin, end):
            slot = jnp.where(i < found[at], slots[at * (cap + 1) + i], 0)
            copy = pltpu.make_async_copy(
                pool_ref.at[slot, :, k], out.at[0, i - begin], sem.at[len(copies)]
            )
            copy.start()
            copies.append(copy)
    if near:
        asked = [(t, s) for t in range(3) for s in range(near)]

        def count(j, seen):
            following = []
            for (t, s), so_far in zip(asked, seen):
                request = pair ^ (near if t == 1 else 0)
                _, there = held(request, owner ^ (2 * s + t // 2), j)
                inside = jnp.clip(length_ref[request] - j * page_len, 0, page_len)
                following.append(so_far + jnp.where(there, inside, 0))
            return tuple(following)

        seen = lax.fori_loop(0, width, count, (jnp.int32(0),) * len(asked), unroll=8)
        for (t, s), total in zip(asked, seen):
            seen_ref[t, s] = total
    for copy in copies:
        copy.wait()


def gather_pages(owner, table, lengths, pool, ranges, near, cap, after=()):
    _, pair_of, _, page_len, head_dim = pool.shape
    outs = [
        pltpu.VMEM((1, end - begin, pair_of, page_len, head_dim), pool.dtype)
        for _, _, begin, end in ranges
    ]
    copy_count = sum(end - begin for _, _, begin, end in ranges)
    list_count = len({which for which, _, _, _ in ranges})
    specs = [pl.BlockSpec(memory_space=pltpu.VMEM)] * len(outs)
    if near:
        outs.append(jax.ShapeDtypeStruct((3, near), jnp.int32))
        specs.append(pl.BlockSpec(memory_space=pltpu.SMEM))
    results = pl.pallas_call(
        functools.partial(gather_body, near=near, waits=len(after), ranges=ranges, cap=cap),
        out_shape=outs,
        grid_spec=pltpu.PrefetchScalarGridSpec(
            num_scalar_prefetch=3,
            grid=(1,),
            in_specs=[pl.BlockSpec(memory_space=pltpu.HBM)]
            + [pl.BlockSpec(memory_space=pl.ANY)] * len(after),
            out_specs=specs,
            scratch_shapes=[
                pltpu.SMEM((list_count * (cap + 1),), jnp.int32),
                pltpu.SemaphoreType.DMA((copy_count,)),
            ],
        ),
        compiler_params=pltpu.CompilerParams(vmem_limit_bytes=kernel_bytes),
        name="gather_pages",
    )(
        owner,
        pltpu.with_memory_space_constraint(table, pltpu.HBM),
        pltpu.with_memory_space_constraint(lengths, pltpu.HBM),
        pltpu.with_memory_space_constraint(pool, pltpu.HBM),
        *after,
    )
    pages = {(which, k, begin): part for (which, k, begin, _), part in zip(ranges, results)}
    return pages, results[-1]


def attend_body(
    owner_ref,
    seen_ref,
    fresh_ref,
    *refs,
    halves,
    seen_at,
    has_page,
    has_prev,
    packed,
    step_rows,
    tile_rows,
    group,
    scale,
    copies_pool,
    waits,
    page_at,
):
    refs = list(refs)
    q_refs = [refs.pop(0) for _ in range(halves)]
    kv_refs = [refs.pop(0) for _ in seen_at]
    page_ref = refs.pop(0) if has_page else None
    prev_refs = [(refs.pop(0), refs.pop(0)) for _ in range(halves)] if has_prev else None
    pool_ref = refs.pop(0) if copies_pool else None
    del refs[:waits]
    out_refs = []
    for h in range(halves):
        out_refs.append((refs.pop(0),) if packed[h] else (refs.pop(0), refs.pop(0)))
    new_pool = refs.pop(0) if copies_pool else None
    wide_values = refs.pop(0)
    tables = [refs.pop(0) if packed[h] else out_refs[h][1].at[0] for h in range(halves)]
    if copies_pool:
        staged, sem_in, sem_out = refs
    head = pl.program_id(0)
    step = pl.program_id(1)
    heads = pl.num_programs(0)
    steps = pl.num_programs(1)
    owner = owner_ref[0]
    half = 1 - ((owner & 1) ^ ((owner >> 1) & 1))
    page_len = kv_refs[0].shape[3]
    keys = [ref.shape[1] * page_len for ref in kv_refs]

    if copies_pool:

        @pl.when((head == 0) & (step == 0))
        def _():
            pltpu.make_async_copy(pool_ref, staged, sem_in).start()

        @pl.when((head == 0) & (step == jnp.minimum(1, steps - 1)))
        def _():
            pltpu.make_async_copy(pool_ref, staged, sem_in).wait()
            staged[fresh_ref[owner] - owner * staged.shape[0]] = page_ref[...]
            pltpu.make_async_copy(staged, new_pool, sem_out).start()

    @pl.when(step == 0)
    def _():
        ones = jnp.ones((page_len, lanes), jnp.bfloat16)
        begin = 0
        for ref in kv_refs:
            for p in range(ref.shape[1]):
                wide_values[begin : begin + page_len, :lanes] = ref[0, p, 1]
                wide_values[begin : begin + page_len, lanes:] = ones
                begin += page_len
        if has_page:
            wide_values[begin : begin + page_len, :lanes] = page_ref[1, page_at]
            wide_values[begin : begin + page_len, lanes:] = ones

    eye = diagonal()
    limits = []
    for s, at in enumerate(seen_at):
        position = lax.broadcasted_iota(jnp.int32, (1, keys[s]), 1)
        limit = jnp.where(position + at[2] < seen_ref[at[0], at[1]], jnp.inf, hidden_score)
        limits.append(limit.astype(jnp.float32))

    def score(h, t):
        query = q_refs[h][0, t * tile_rows : (t + 1) * tile_rows]
        scores = []
        for s, ref in enumerate(kv_refs):
            key_rows = ref[0, :, 0].reshape(keys[s], lanes)
            product = lax.dot_general(
                query, key_rows, (((1,), (1,)), ((), ())), preferred_element_type=jnp.float32
            )
            scores.append(jnp.minimum(product, limits[s]))
        if has_page:
            product = lax.dot_general(
                query, page_ref[0, page_at], (((1,), (1,)), ((), ())), preferred_element_type=jnp.float32
            )
            key_at = lax.broadcasted_iota(jnp.int32, product.shape, 1)
            if h == 0:
                row_at = lax.broadcasted_iota(jnp.int32, product.shape, 0)
                token = (step * step_rows + t * tile_rows + row_at) // group
                shown = key_at <= token
            else:
                shown = key_at < jnp.where(half == 0, page_len, 0)
            scores.append(jnp.where(shown, product, hidden_score))
        return scores

    def finish(h, t, scores):
        top = jnp.full((tile_rows, 1), lowest_top, jnp.float32)
        for part in scores:
            top = jnp.maximum(top, jnp.max(part, axis=1, keepdims=True))
        scaled_top = top * scale
        weights = [jnp.exp2(part * scale - scaled_top).astype(jnp.bfloat16) for part in scores]
        mixed = jnp.dot(
            jnp.concatenate(weights, axis=1), wide_values[...], preferred_element_type=jnp.float32
        )
        total = mixed[:, lanes:]
        mixed = mixed[:, :lanes]
        first = step * (step_rows // block_rows) + t * (tile_rows // block_rows)
        count = tables[h].shape[0] // 2
        for u in range(tile_rows // block_rows):
            inner = slice(u * block_rows, (u + 1) * block_rows)
            outer = slice(t * tile_rows + u * block_rows, t * tile_rows + (u + 1) * block_rows)
            part_top, part_total, part_mixed = top[inner], total[inner], mixed[inner]
            row = first + u
            if has_prev:
                prev_mixed, prev_table = prev_refs[h]
                prev_top = as_column(prev_table[0, pl.ds(row, 1)], eye)
                prev_total = as_column(prev_table[0, pl.ds(count + row, 1)], eye)
                joint = jnp.maximum(part_top, prev_top)
                keep = jnp.exp2((part_top - joint) * scale)
                keep_prev = jnp.exp2((prev_top - joint) * scale)
                part_mixed = part_mixed * keep + prev_mixed[0, outer] * keep_prev
                part_total = part_total * keep + prev_total * keep_prev
                part_top = joint
            tables[h][pl.ds(row, 1)] = as_row(part_top, eye)
            tables[h][pl.ds(count + row, 1)] = as_row(part_total, eye)
            if packed[h]:
                at = pl.multiple_of(row * block_rows, block_rows)
                out_refs[h][0][0, pl.ds(at, block_rows)] = part_mixed.astype(jnp.bfloat16)
            else:
                out_refs[h][0][0, outer] = part_mixed

    chains = [(h, t) for t in range(step_rows // tile_rows) for h in range(halves)]
    scores = score(*chains[0])
    for i, chain in enumerate(chains):
        following = score(*chains[i + 1]) if i + 1 < len(chains) else None
        finish(*chain, scores)
        scores = following

    @pl.when(step == steps - 1)
    def _():
        for h in range(halves):
            if packed[h]:
                size = tables[h].shape[0]
                begin = out_refs[h][0].shape[1] - 3 * size
                for i, part in enumerate(in_three(tables[h][...])):
                    out_refs[h][0][0, begin + i * size : begin + (i + 1) * size] = part

    if copies_pool:

        @pl.when((head == heads - 1) & (step == steps - 1))
        def _():
            pltpu.make_async_copy(staged, new_pool, sem_out).wait()


def attend(
    scalars, queries, sources, seen_at, packed, scale, group, heads, page=None, prev=None, pool=None, after=()
):
    halves = len(queries)
    rows = queries[0][0].shape[1]
    size = 2 * (rows // block_rows)
    step_rows = min(rows, 1024 // halves)
    tile_rows = min(step_rows, 256)
    key_count = sum(s.shape[1] * s.shape[3] for s, _ in sources)

    def per_rows(offset):
        return pl.BlockSpec((1, step_rows, lanes), lambda k, i, *_: (k + offset, i, 0))

    def per_head(array, offset):
        tail = array.shape[1:]
        return pl.BlockSpec((1, *tail), lambda k, i, *_: (k + offset,) + (0,) * len(tail))

    anywhere = pl.BlockSpec(memory_space=pl.ANY)
    args = [q for q, _ in queries] + [s for s, _ in sources]
    in_specs = [per_rows(at) for _, at in queries] + [per_head(s, at) for s, at in sources]
    page_at = 0
    if page is not None:
        page, page_at = page
        args.append(page)
        in_specs.append(whole(page))
        key_count += page.shape[2]
    if prev is not None:
        for mixed, table, at in prev:
            args += [mixed, table]
            in_specs += [per_rows(at), per_head(table, at)]
    if pool is not None:
        args.append(pltpu.with_memory_space_constraint(pool, pltpu.HBM))
        in_specs.append(pl.BlockSpec(memory_space=pltpu.HBM))
    args += list(after)
    in_specs += [anywhere] * len(after)
    out_shape = []
    out_specs = []
    scratch = [pltpu.VMEM((key_count, 2 * lanes), jnp.bfloat16)]
    for h in range(halves):
        if packed[h]:
            shape = jax.ShapeDtypeStruct((heads, rows + 3 * size, lanes), jnp.bfloat16)
            out_shape.append(shape)
            out_specs.append(per_head(shape, 0))
            scratch.append(pltpu.VMEM((size, lanes), jnp.float32))
        else:
            table = jax.ShapeDtypeStruct((heads, size, lanes), jnp.float32)
            out_shape += [jax.ShapeDtypeStruct((heads, rows, lanes), jnp.float32), table]
            out_specs += [per_rows(0), per_head(table, 0)]
    if pool is not None:
        out_shape.append(jax.ShapeDtypeStruct(pool.shape, pool.dtype))
        out_specs.append(pl.BlockSpec(memory_space=pltpu.HBM))
        scratch.append(pltpu.VMEM(pool.shape, pool.dtype))
        scratch += [pltpu.SemaphoreType.DMA, pltpu.SemaphoreType.DMA]
    work = halves * heads * rows * key_count
    return pl.pallas_call(
        functools.partial(
            attend_body,
            halves=halves,
            seen_at=seen_at,
            has_page=page is not None,
            has_prev=prev is not None,
            packed=packed,
            step_rows=step_rows,
            tile_rows=tile_rows,
            group=group,
            scale=scale,
            copies_pool=pool is not None,
            waits=len(after),
            page_at=page_at,
        ),
        out_shape=out_shape,
        grid_spec=pltpu.PrefetchScalarGridSpec(
            num_scalar_prefetch=3,
            grid=(heads, rows // step_rows),
            in_specs=in_specs,
            out_specs=out_specs,
            scratch_shapes=scratch,
        ),
        cost_estimate=pl.CostEstimate(
            flops=4 * work * lanes,
            transcendentals=work,
            bytes_accessed=4 * heads * key_count * lanes,
        ),
        compiler_params=pltpu.CompilerParams(vmem_limit_bytes=kernel_bytes),
        name="attend",
    )(*scalars, *args)


def join_body(own_mixed, own_table, *refs, scale, packs, waits):
    refs = list(refs)
    out_ref = refs.pop()
    if waits:
        del refs[-waits:]
    size = own_table.shape[1]
    count = size // 2
    rows = count * block_rows
    eye = diagonal()
    tops = [own_table[0, :count]]
    totals = [own_table[0, count:]]
    for ref in refs:
        table = from_three(ref, rows, size)
        tops.append(table[:count])
        totals.append(table[count:])
    top = functools.reduce(jnp.maximum, tops)
    keeps = [jnp.exp2((t - top) * scale) for t in tops]
    total = sum(t * keep for t, keep in zip(totals, keeps))
    if not packs:
        keeps = [keep / total for keep in keeps]
    for t in range(count):
        at = slice(t * block_rows, (t + 1) * block_rows)
        mixed = own_mixed[0, at] * as_column(keeps[0][t : t + 1], eye)
        for ref, keep in zip(refs, keeps[1:]):
            mixed = mixed + ref[0, at].astype(jnp.float32) * as_column(keep[t : t + 1], eye)
        if packs:
            out_ref[0, at] = mixed.astype(jnp.bfloat16)
        else:
            heads = out_ref.shape[1]
            tokens = block_rows // heads
            shaped = mixed.reshape(tokens, heads, lanes)
            out_ref[t * tokens : (t + 1) * tokens] = shaped.astype(jnp.bfloat16)
    if packs:
        table = jnp.concatenate([top, total], axis=0)
        for i, part in enumerate(in_three(table)):
            out_ref[0, rows + i * size : rows + (i + 1) * size] = part


def join_packed(own, received, scale, after=()):
    mixed, table = own
    args = [mixed, table, received]
    return pl.pallas_call(
        functools.partial(join_body, scale=scale, packs=True, waits=len(after)),
        out_shape=jax.ShapeDtypeStruct(received.shape, received.dtype),
        grid=(1,),
        in_specs=[whole(a) for a in args] + [pl.BlockSpec(memory_space=pl.ANY)] * len(after),
        out_specs=whole(received),
        compiler_params=pltpu.CompilerParams(vmem_limit_bytes=kernel_bytes),
        name="join_packed",
    )(*args, *after)


def join_out(own, received, target, shape, index, group, scale):
    mixed, table = own
    args = [mixed, table, *received]
    in_specs = [whole(a) for a in args]
    aliases = {}
    if target is not None:
        aliases = {len(args): 0}
        args.append(target)
        in_specs.append(pl.BlockSpec(memory_space=pl.ANY))
    return pl.pallas_call(
        functools.partial(join_body, scale=scale, packs=False, waits=len(aliases)),
        out_shape=jax.ShapeDtypeStruct(shape, jnp.bfloat16),
        grid=(1,),
        in_specs=in_specs,
        out_specs=pl.BlockSpec((shape[0], group, shape[2]), lambda i: (0, index, 0)),
        input_output_aliases=aliases,
        compiler_params=pltpu.CompilerParams(vmem_limit_bytes=kernel_bytes),
        name="join_out",
    )(*args)


def on_device(queries, new_kv, pool, block_table, prefix_len, new_slots):
    owner_count = lax.axis_size("pool")
    owner = lax.axis_index("pool").astype(jnp.int32)
    _, _, kv_heads, page_len, head_dim = pool.shape
    tokens, q_heads, _ = queries.shape
    group = q_heads // kv_heads
    rows = tokens * group
    pairs = owner_count // 2
    near = pairs // 2
    cap = block_table.shape[1] // owner_count
    scale = head_dim**-0.5 * log2_e
    each = range(kv_heads)

    owner_list = jnp.full((1,), owner, jnp.int32)
    split = [
        queries[:, k * group : (k + 1) * group].reshape(1, rows, head_dim) for k in each
    ]
    new_page = new_kv.transpose(1, 2, 0, 3)
    far_own = [moved(split[k], pairs) for k in each]
    other = [moved(split[k], 1) for k in each]
    lookup = (owner_list, block_table, prefix_len, pool)
    last = kv_heads - 1
    cut = cap - last_pages(cap)
    ring = range(1, near)
    ranges = [(near + i, 0, 0, cap) for i in ring]
    pages, _ = gather_pages(*lookup, ranges, 0, cap)
    ranges = [(near + i, k, 0, cap) for k in each if k for i in ring]
    ranges += [(i, k, 0, cut if k == last else cap) for k in each for i in ring]
    ranges += [(i, last, cut, cap) for i in ring]
    ranges += [(i, k, 0, cap) for i in (0, near) for k in each]
    more, seen = gather_pages(*lookup, ranges, near, cap, after=[new_page])
    pages = {**pages, **more}

    def exchanged(first, k, begin):
        return [moved(pages[first + i, k, begin], 2 * i) for i in ring]

    got_far = [exchanged(near, k, 0) for k in each]
    got_near = [exchanged(0, k, 0) for k in each]
    got_late = [moved(pages[i, last, cut], 2 * i) for i in ring]
    theirs_late = [moved(pages[i, last, cut], 1) for i in ring]
    got_late += [moved(part, 2 * i) for i, part in zip(ring, theirs_late)]
    local, local_far = [[pages[i, k, 0] for k in each] for i in (0, near)]
    scalars = (owner_list, seen, new_slots)

    started = []
    updated = None
    after = []
    for k in each:
        results = attend(
            scalars,
            [(split[k], 0), (other[k], 0)],
            [(local[k], 0)],
            [(0, 0, 0)],
            (False, False),
            scale,
            group,
            1,
            page=(new_page, k),
            pool=pool if k == 0 else None,
            after=after,
        )
        if k == 0:
            updated = results[4]
        started.append(results[:4])
        after = [results[1]]
    far_other = [moved(far_own[k], 1) for k in each]
    far = []
    for k in each:
        results = attend(
            scalars,
            [(far_own[k], 0), (far_other[k], 0)],
            [(local_far[k], 0)] + [(a, 0) for a in got_far[k]],
            [(1, i, 0) for i in range(near)],
            (False, True),
            scale,
            group,
            1,
            after=after,
        )
        far.append((results[:2], moved(results[2], 1)))
        after = [results[1]]
    back = []
    ready = []
    for k in each:
        joined = join_packed(*far[k], scale, after=after)
        back.append(moved(joined, pairs))
        after = [joined]
    for k in each:
        mine, mine_table, theirs, theirs_table = started[k]
        near_keys = [(a, 0) for a in got_near[k]]
        near_at = [(0, i, 0) for i in range(1, near)]
        mine, theirs = (mine, mine_table, 0), (theirs, theirs_table, 0)
        if k + 1 < kv_heads:
            results = attend(
                scalars,
                [(split[k], 0), (other[k], 0)],
                near_keys,
                near_at,
                (False, True),
                scale,
                group,
                1,
                prev=[mine, theirs],
                after=after,
            )
            own_part = results[:2]
            other_part = results[2]
        else:
            late_keys = [(a, 0) for a in got_late]
            late_at = [(t, i, cut * page_len) for t in (0, 2) for i in ring]
            (other_part,) = attend(
                scalars,
                [(other[k], 0)],
                near_keys,
                near_at,
                (True,),
                scale,
                group,
                1,
                prev=[theirs],
                after=after,
            )
            early = attend(
                scalars,
                [(split[k], 0)],
                near_keys,
                near_at,
                (False,),
                scale,
                group,
                1,
                prev=[mine],
                after=[other_part],
            )
            own_part = attend(
                scalars,
                [(split[k], 0)],
                late_keys,
                late_at,
                (False,),
                scale,
                group,
                1,
                prev=[(*early, 0)],
            )
        ready.append((own_part, moved(other_part, 1)))
        after = [own_part[1]]
    attended = None
    for k in each:
        own, received = ready[k]
        attended = join_out(
            own, [received, back[k]], attended, queries.shape, k, group, scale
        )
    return (attended, updated)


def solution(mesh):
    placed = (
        P(("groups", "pool"), "head", None),
        P(("groups", "pool"), None, "head", None),
        P(("groups", "pool"), None, "head", None, None),
        P("groups", None),
        P("groups"),
        P("groups"),
    )

    return jax.shard_map(
        on_device,
        mesh=mesh,
        in_specs=placed,
        out_specs=(
            P(("groups", "pool"), "head", None),
            P(("groups", "pool"), None, "head", None, None),
        ),
        check_vma=False,
    )
```

```python
import functools

import jax
import jax.numpy as jnp
from jax import lax
from jax.experimental import pallas as pl
from jax.experimental.pallas import tpu as pltpu
from jax.sharding import PartitionSpec as P


log2_e = 1.4426950408889634
hidden_score = -2e30
lowest_top = -1e30
lanes = 128
block_rows = 128
kernel_bytes = 24 << 20


def moved(array, apart):
    count = lax.axis_size("pool")
    return lax.ppermute(array, "pool", [(i, i ^ apart) for i in range(count)])


def whole(array):
    return pl.BlockSpec(array.shape, lambda i, *_: (0,) * len(array.shape))


def diagonal():
    shape = (lanes, lanes)
    return lax.broadcasted_iota(jnp.int32, shape, 0) == lax.broadcasted_iota(jnp.int32, shape, 1)


def as_row(column, eye):
    spread = jnp.where(eye, jnp.broadcast_to(column, (lanes, lanes)), 0.0)
    return jnp.sum(spread, axis=0, keepdims=True)


def as_column(row, eye):
    spread = jnp.where(eye, jnp.broadcast_to(row, (lanes, lanes)), 0.0)
    return jnp.sum(spread, axis=1, keepdims=True)


def in_three(values):
    high = values.astype(jnp.bfloat16)
    rest = values - high.astype(jnp.float32)
    middle = rest.astype(jnp.bfloat16)
    low = (rest - middle.astype(jnp.float32)).astype(jnp.bfloat16)
    return (high, middle, low)


def from_three(ref, begin, count):
    parts = [
        ref[0, begin + i * count : begin + (i + 1) * count].astype(jnp.float32) for i in range(3)
    ]
    return parts[0] + parts[1] + parts[2]


def last_pages(cap):
    return max(1, cap // 4)


def gather_body(owner_ref, table_ref, length_ref, pool_ref, *refs, near, waits, ranges, cap):
    refs = refs[waits:]
    outs = refs[: len(ranges)]
    seen_ref = refs[len(ranges)] if near else None
    slots, sem = refs[-2:]
    lists = sorted({which for which, _, _, _ in ranges})
    owner = owner_ref[0]
    pair = owner >> 1
    slot_count, _, _, page_len, _ = pool_ref.shape
    width = table_ref.shape[1]

    def held(request, holder, j):
        slot = table_ref[request, j] - holder * slot_count
        return slot, (slot >= 0) & (slot < slot_count)

    def look(j, found):
        following = []
        for at, which in enumerate(lists):
            slot, here = held(pair ^ which, owner, j)
            slots[at * (cap + 1) + jnp.minimum(found[at], cap)] = slot
            following.append(found[at] + here.astype(jnp.int32))
        return tuple(following)

    found = lax.fori_loop(0, width, look, (jnp.int32(0),) * len(lists), unroll=16)
    copies = []
    for (which, k, begin, end), out in zip(ranges, outs):
        at = lists.index(which)
        for i in range(begin, end):
            slot = jnp.where(i < found[at], slots[at * (cap + 1) + i], 0)
            copy = pltpu.make_async_copy(
                pool_ref.at[slot, :, k], out.at[0, i - begin], sem.at[len(copies)]
            )
            copy.start()
            copies.append(copy)
    if near:
        asked = [(t, s) for t in range(2) for s in range(near)]

        def count(j, seen):
            following = []
            for (t, s), so_far in zip(asked, seen):
                request = pair ^ (t * near)
                _, there = held(request, owner ^ (2 * s), j)
                inside = jnp.clip(length_ref[request] - j * page_len, 0, page_len)
                following.append(so_far + jnp.where(there, inside, 0))
            return tuple(following)

        seen = lax.fori_loop(0, width, count, (jnp.int32(0),) * len(asked), unroll=8)
        for (t, s), total in zip(asked, seen):
            seen_ref[t, s] = total
    for copy in copies:
        copy.wait()


def gather_pages(owner, table, lengths, pool, ranges, near, cap, after=()):
    _, pair_of, _, page_len, head_dim = pool.shape
    outs = [
        pltpu.VMEM((1, end - begin, pair_of, page_len, head_dim), pool.dtype)
        for _, _, begin, end in ranges
    ]
    copy_count = sum(end - begin for _, _, begin, end in ranges)
    list_count = len({which for which, _, _, _ in ranges})
    specs = [pl.BlockSpec(memory_space=pltpu.VMEM)] * len(outs)
    if near:
        outs.append(jax.ShapeDtypeStruct((2, near), jnp.int32))
        specs.append(pl.BlockSpec(memory_space=pltpu.SMEM))
    results = pl.pallas_call(
        functools.partial(gather_body, near=near, waits=len(after), ranges=ranges, cap=cap),
        out_shape=outs,
        grid_spec=pltpu.PrefetchScalarGridSpec(
            num_scalar_prefetch=3,
            grid=(1,),
            in_specs=[pl.BlockSpec(memory_space=pltpu.HBM)]
            + [pl.BlockSpec(memory_space=pl.ANY)] * len(after),
            out_specs=specs,
            scratch_shapes=[
                pltpu.SMEM((list_count * (cap + 1),), jnp.int32),
                pltpu.SemaphoreType.DMA((copy_count,)),
            ],
        ),
        compiler_params=pltpu.CompilerParams(vmem_limit_bytes=kernel_bytes),
        name="gather_pages",
    )(
        owner,
        pltpu.with_memory_space_constraint(table, pltpu.HBM),
        pltpu.with_memory_space_constraint(lengths, pltpu.HBM),
        pltpu.with_memory_space_constraint(pool, pltpu.HBM),
        *after,
    )
    pages = {(which, k, begin): part for (which, k, begin, _), part in zip(ranges, results)}
    return pages, results[-1]


def attend_body(
    owner_ref,
    seen_ref,
    fresh_ref,
    *refs,
    halves,
    seen_at,
    has_page,
    has_prev,
    packed,
    step_rows,
    tile_rows,
    group,
    scale,
    copies_pool,
    waits,
    page_at,
):
    refs = list(refs)
    q_refs = [refs.pop(0) for _ in range(halves)]
    kv_refs = [refs.pop(0) for _ in seen_at]
    page_ref = refs.pop(0) if has_page else None
    prev_refs = [(refs.pop(0), refs.pop(0)) for _ in range(halves)] if has_prev else None
    pool_ref = refs.pop(0) if copies_pool else None
    del refs[:waits]
    out_refs = []
    for h in range(halves):
        out_refs.append((refs.pop(0),) if packed[h] else (refs.pop(0), refs.pop(0)))
    new_pool = refs.pop(0) if copies_pool else None
    wide_values = refs.pop(0)
    tables = [refs.pop(0) if packed[h] else out_refs[h][1].at[0] for h in range(halves)]
    if copies_pool:
        staged, sem_in, sem_out = refs
    head = pl.program_id(0)
    step = pl.program_id(1)
    heads = pl.num_programs(0)
    steps = pl.num_programs(1)
    owner = owner_ref[0]
    half = 1 - ((owner & 1) ^ ((owner >> 1) & 1))
    page_len = kv_refs[0].shape[3]
    keys = [ref.shape[1] * page_len for ref in kv_refs]

    if copies_pool:

        @pl.when((head == 0) & (step == 0))
        def _():
            pltpu.make_async_copy(pool_ref, staged, sem_in).start()

        @pl.when((head == 0) & (step == jnp.minimum(1, steps - 1)))
        def _():
            pltpu.make_async_copy(pool_ref, staged, sem_in).wait()
            staged[fresh_ref[owner] - owner * staged.shape[0]] = page_ref[...]
            pltpu.make_async_copy(staged, new_pool, sem_out).start()

    @pl.when(step == 0)
    def _():
        ones = jnp.ones((page_len, lanes), jnp.bfloat16)
        begin = 0
        for ref in kv_refs:
            for p in range(ref.shape[1]):
                wide_values[begin : begin + page_len, :lanes] = ref[0, p, 1]
                wide_values[begin : begin + page_len, lanes:] = ones
                begin += page_len
        if has_page:
            wide_values[begin : begin + page_len, :lanes] = page_ref[1, page_at]
            wide_values[begin : begin + page_len, lanes:] = ones

    eye = diagonal()
    limits = []
    for s, at in enumerate(seen_at):
        position = lax.broadcasted_iota(jnp.int32, (1, keys[s]), 1)
        limit = jnp.where(position + at[2] < seen_ref[at[0], at[1]], jnp.inf, hidden_score)
        limits.append(limit.astype(jnp.float32))

    def score(h, t):
        query = q_refs[h][0, t * tile_rows : (t + 1) * tile_rows]
        scores = []
        for s, ref in enumerate(kv_refs):
            key_rows = ref[0, :, 0].reshape(keys[s], lanes)
            product = lax.dot_general(
                query, key_rows, (((1,), (1,)), ((), ())), preferred_element_type=jnp.float32
            )
            scores.append(jnp.minimum(product, limits[s]))
        if has_page:
            product = lax.dot_general(
                query, page_ref[0, page_at], (((1,), (1,)), ((), ())), preferred_element_type=jnp.float32
            )
            key_at = lax.broadcasted_iota(jnp.int32, product.shape, 1)
            if h == 0:
                row_at = lax.broadcasted_iota(jnp.int32, product.shape, 0)
                token = (step * step_rows + t * tile_rows + row_at) // group
                shown = key_at <= token
            else:
                shown = key_at < jnp.where(half == 0, page_len, 0)
            scores.append(jnp.where(shown, product, hidden_score))
        return scores

    def finish(h, t, scores):
        top = jnp.full((tile_rows, 1), lowest_top, jnp.float32)
        for part in scores:
            top = jnp.maximum(top, jnp.max(part, axis=1, keepdims=True))
        scaled_top = top * scale
        weights = [jnp.exp2(part * scale - scaled_top).astype(jnp.bfloat16) for part in scores]
        mixed = jnp.dot(
            jnp.concatenate(weights, axis=1), wide_values[...], preferred_element_type=jnp.float32
        )
        total = mixed[:, lanes:]
        mixed = mixed[:, :lanes]
        first = step * (step_rows // block_rows) + t * (tile_rows // block_rows)
        count = tables[h].shape[0] // 2
        for u in range(tile_rows // block_rows):
            inner = slice(u * block_rows, (u + 1) * block_rows)
            outer = slice(t * tile_rows + u * block_rows, t * tile_rows + (u + 1) * block_rows)
            part_top, part_total, part_mixed = top[inner], total[inner], mixed[inner]
            row = first + u
            if has_prev:
                prev_mixed, prev_table = prev_refs[h]
                prev_top = as_column(prev_table[0, pl.ds(row, 1)], eye)
                prev_total = as_column(prev_table[0, pl.ds(count + row, 1)], eye)
                joint = jnp.maximum(part_top, prev_top)
                keep = jnp.exp2((part_top - joint) * scale)
                keep_prev = jnp.exp2((prev_top - joint) * scale)
                part_mixed = part_mixed * keep + prev_mixed[0, outer] * keep_prev
                part_total = part_total * keep + prev_total * keep_prev
                part_top = joint
            tables[h][pl.ds(row, 1)] = as_row(part_top, eye)
            tables[h][pl.ds(count + row, 1)] = as_row(part_total, eye)
            if packed[h]:
                at = pl.multiple_of(row * block_rows, block_rows)
                out_refs[h][0][0, pl.ds(at, block_rows)] = part_mixed.astype(jnp.bfloat16)
            else:
                out_refs[h][0][0, outer] = part_mixed

    chains = [(h, t) for t in range(step_rows // tile_rows) for h in range(halves)]
    scores = score(*chains[0])
    for i, chain in enumerate(chains):
        following = score(*chains[i + 1]) if i + 1 < len(chains) else None
        finish(*chain, scores)
        scores = following

    @pl.when(step == steps - 1)
    def _():
        for h in range(halves):
            if packed[h]:
                size = tables[h].shape[0]
                begin = out_refs[h][0].shape[1] - 3 * size
                for i, part in enumerate(in_three(tables[h][...])):
                    out_refs[h][0][0, begin + i * size : begin + (i + 1) * size] = part

    if copies_pool:

        @pl.when((head == heads - 1) & (step == steps - 1))
        def _():
            pltpu.make_async_copy(staged, new_pool, sem_out).wait()


def attend(
    scalars, queries, sources, seen_at, packed, scale, group, heads, page=None, prev=None, pool=None, after=()
):
    halves = len(queries)
    rows = queries[0][0].shape[1]
    size = 2 * (rows // block_rows)
    step_rows = min(rows, 1024 // halves)
    key_count = sum(s.shape[1] * s.shape[3] for s, _ in sources)
    tile_rows = min(step_rows, 512 if key_count <= 2 * block_rows else 256)

    def per_rows(offset):
        return pl.BlockSpec((1, step_rows, lanes), lambda k, i, *_: (k + offset, i, 0))

    def per_head(array, offset):
        tail = array.shape[1:]
        return pl.BlockSpec((1, *tail), lambda k, i, *_: (k + offset,) + (0,) * len(tail))

    anywhere = pl.BlockSpec(memory_space=pl.ANY)
    args = [q for q, _ in queries] + [s for s, _ in sources]
    in_specs = [per_rows(at) for _, at in queries] + [per_head(s, at) for s, at in sources]
    page_at = 0
    if page is not None:
        page, page_at = page
        args.append(page)
        in_specs.append(whole(page))
        key_count += page.shape[2]
    if prev is not None:
        for mixed, table, at in prev:
            args += [mixed, table]
            in_specs += [per_rows(at), per_head(table, at)]
    if pool is not None:
        args.append(pltpu.with_memory_space_constraint(pool, pltpu.HBM))
        in_specs.append(pl.BlockSpec(memory_space=pltpu.HBM))
    args += list(after)
    in_specs += [anywhere] * len(after)
    out_shape = []
    out_specs = []
    scratch = [pltpu.VMEM((key_count, 2 * lanes), jnp.bfloat16)]
    for h in range(halves):
        if packed[h]:
            shape = jax.ShapeDtypeStruct((heads, rows + 3 * size, lanes), jnp.bfloat16)
            out_shape.append(shape)
            out_specs.append(per_head(shape, 0))
            scratch.append(pltpu.VMEM((size, lanes), jnp.float32))
        else:
            table = jax.ShapeDtypeStruct((heads, size, lanes), jnp.float32)
            out_shape += [jax.ShapeDtypeStruct((heads, rows, lanes), jnp.float32), table]
            out_specs += [per_rows(0), per_head(table, 0)]
    if pool is not None:
        out_shape.append(jax.ShapeDtypeStruct(pool.shape, pool.dtype))
        out_specs.append(pl.BlockSpec(memory_space=pltpu.HBM))
        scratch.append(pltpu.VMEM(pool.shape, pool.dtype))
        scratch += [pltpu.SemaphoreType.DMA, pltpu.SemaphoreType.DMA]
    work = halves * heads * rows * key_count
    return pl.pallas_call(
        functools.partial(
            attend_body,
            halves=halves,
            seen_at=seen_at,
            has_page=page is not None,
            has_prev=prev is not None,
            packed=packed,
            step_rows=step_rows,
            tile_rows=tile_rows,
            group=group,
            scale=scale,
            copies_pool=pool is not None,
            waits=len(after),
            page_at=page_at,
        ),
        out_shape=out_shape,
        grid_spec=pltpu.PrefetchScalarGridSpec(
            num_scalar_prefetch=3,
            grid=(heads, rows // step_rows),
            in_specs=in_specs,
            out_specs=out_specs,
            scratch_shapes=scratch,
        ),
        cost_estimate=pl.CostEstimate(
            flops=4 * work * lanes,
            transcendentals=work,
            bytes_accessed=4 * heads * key_count * lanes,
        ),
        compiler_params=pltpu.CompilerParams(vmem_limit_bytes=kernel_bytes),
        name="attend",
    )(*scalars, *args)


def join_body(own_mixed, own_table, *refs, scale, packs, waits):
    refs = list(refs)
    out_ref = refs.pop()
    if waits:
        del refs[-waits:]
    size = own_table.shape[1]
    count = size // 2
    rows = count * block_rows
    eye = diagonal()
    tops = [own_table[0, :count]]
    totals = [own_table[0, count:]]
    for ref in refs:
        table = from_three(ref, rows, size)
        tops.append(table[:count])
        totals.append(table[count:])
    top = functools.reduce(jnp.maximum, tops)
    keeps = [jnp.exp2((t - top) * scale) for t in tops]
    total = sum(t * keep for t, keep in zip(totals, keeps))
    if not packs:
        keeps = [keep / total for keep in keeps]
    for t in range(count):
        at = slice(t * block_rows, (t + 1) * block_rows)
        mixed = own_mixed[0, at] * as_column(keeps[0][t : t + 1], eye)
        for ref, keep in zip(refs, keeps[1:]):
            mixed = mixed + ref[0, at].astype(jnp.float32) * as_column(keep[t : t + 1], eye)
        if packs:
            out_ref[0, at] = mixed.astype(jnp.bfloat16)
        else:
            heads = out_ref.shape[1]
            tokens = block_rows // heads
            shaped = mixed.reshape(tokens, heads, lanes)
            out_ref[t * tokens : (t + 1) * tokens] = shaped.astype(jnp.bfloat16)
    if packs:
        table = jnp.concatenate([top, total], axis=0)
        for i, part in enumerate(in_three(table)):
            out_ref[0, rows + i * size : rows + (i + 1) * size] = part


def join_packed(own, received, scale, after=()):
    mixed, table = own
    args = [mixed, table, received]
    return pl.pallas_call(
        functools.partial(join_body, scale=scale, packs=True, waits=len(after)),
        out_shape=jax.ShapeDtypeStruct(received.shape, received.dtype),
        grid=(1,),
        in_specs=[whole(a) for a in args] + [pl.BlockSpec(memory_space=pl.ANY)] * len(after),
        out_specs=whole(received),
        compiler_params=pltpu.CompilerParams(vmem_limit_bytes=kernel_bytes),
        name="join_packed",
    )(*args, *after)


def join_out(own, received, target, shape, index, group, scale):
    mixed, table = own
    args = [mixed, table, *received]
    in_specs = [whole(a) for a in args]
    aliases = {}
    if target is not None:
        aliases = {len(args): 0}
        args.append(target)
        in_specs.append(pl.BlockSpec(memory_space=pl.ANY))
    return pl.pallas_call(
        functools.partial(join_body, scale=scale, packs=False, waits=len(aliases)),
        out_shape=jax.ShapeDtypeStruct(shape, jnp.bfloat16),
        grid=(1,),
        in_specs=in_specs,
        out_specs=pl.BlockSpec((shape[0], group, shape[2]), lambda i: (0, index, 0)),
        input_output_aliases=aliases,
        compiler_params=pltpu.CompilerParams(vmem_limit_bytes=kernel_bytes),
        name="join_out",
    )(*args)


def on_device(queries, new_kv, pool, block_table, prefix_len, new_slots):
    owner_count = lax.axis_size("pool")
    owner = lax.axis_index("pool").astype(jnp.int32)
    _, _, kv_heads, page_len, head_dim = pool.shape
    tokens, q_heads, _ = queries.shape
    group = q_heads // kv_heads
    rows = tokens * group
    pairs = owner_count // 2
    near = pairs // 2
    cap = block_table.shape[1] // owner_count
    scale = head_dim**-0.5 * log2_e
    each = range(kv_heads)

    owner_list = jnp.full((1,), owner, jnp.int32)
    split = [
        queries[:, k * group : (k + 1) * group].reshape(1, rows, head_dim) for k in each
    ]
    new_page = new_kv.transpose(1, 2, 0, 3)
    far_own = [moved(split[k], pairs) for k in each]
    other = [moved(split[k], 1) for k in each]
    lookup = (owner_list, block_table, prefix_len, pool)
    last = kv_heads - 1
    cut = cap - last_pages(cap)
    ring = range(1, near)
    ranges = [(near + i, 0, 0, cap) for i in ring]
    pages, _ = gather_pages(*lookup, ranges, 0, cap)
    ranges = [(near + i, k, 0, cap) for k in each if k for i in ring]
    ranges += [(i, k, 0, cut if k == last else cap) for k in each for i in ring]
    ranges += [(i, last, cut, cap) for i in ring]
    ranges += [(i, k, 0, cap) for i in (0, near) for k in each]
    more, seen = gather_pages(*lookup, ranges, near, cap, after=[new_page])
    pages = {**pages, **more}

    def exchanged(first, k, begin):
        return [moved(pages[first + i, k, begin], 2 * i) for i in ring]

    got_far = [exchanged(near, k, 0) for k in each]
    got_near = [exchanged(0, k, 0) for k in each]
    got_late = exchanged(0, last, cut)
    local, local_far = [[pages[i, k, 0] for k in each] for i in (0, near)]
    scalars = (owner_list, seen, new_slots)

    started = []
    updated = None
    after = []
    for k in each:
        results = attend(
            scalars,
            [(split[k], 0), (other[k], 0)],
            [(local[k], 0)],
            [(0, 0, 0)],
            (False, False),
            scale,
            group,
            1,
            page=(new_page, k),
            pool=pool if k == 0 else None,
            after=after,
        )
        if k == 0:
            updated = results[4]
        started.append(results[:4])
        after = [results[1]]
    far_other = [moved(far_own[k], 1) for k in each]
    far = []
    for k in each:
        results = attend(
            scalars,
            [(far_own[k], 0), (far_other[k], 0)],
            [(local_far[k], 0)] + [(a, 0) for a in got_far[k]],
            [(1, i, 0) for i in range(near)],
            (False, True),
            scale,
            group,
            1,
            after=after,
        )
        far.append((results[:2], moved(results[2], 1)))
        after = [results[1]]
    back = []
    ready = []
    for k in each:
        joined = join_packed(*far[k], scale, after=after)
        back.append(moved(joined, pairs))
        mine, mine_table, theirs, theirs_table = started[k]
        near_keys = [(a, 0) for a in got_near[k]]
        near_at = [(0, i, 0) for i in range(1, near)]
        mine, theirs = (mine, mine_table, 0), (theirs, theirs_table, 0)
        if k + 1 < kv_heads:
            results = attend(
                scalars,
                [(split[k], 0), (other[k], 0)],
                near_keys,
                near_at,
                (False, True),
                scale,
                group,
                1,
                prev=[mine, theirs],
                after=[joined],
            )
            own_part = results[:2]
            other_part = results[2]
        else:
            late_keys = [(a, 0) for a in got_late]
            late_at = [(0, i, cut * page_len) for i in range(1, near)]
            early = attend(
                scalars,
                [(other[k], 0)],
                near_keys,
                near_at,
                (False,),
                scale,
                group,
                1,
                prev=[theirs],
                after=[joined],
            )
            (other_part,) = attend(
                scalars,
                [(other[k], 0)],
                late_keys,
                late_at,
                (True,),
                scale,
                group,
                1,
                prev=[(*early, 0)],
            )
            own_part = attend(
                scalars,
                [(split[k], 0)],
                near_keys + late_keys,
                near_at + late_at,
                (False,),
                scale,
                group,
                1,
                prev=[mine],
                after=[other_part],
            )
        ready.append((own_part, moved(other_part, 1)))
        after = [own_part[1]]
    attended = None
    for k in each:
        own, received = ready[k]
        attended = join_out(
            own, [received, back[k]], attended, queries.shape, k, group, scale
        )
    return (attended, updated)


def solution(mesh):
    placed = (
        P(("groups", "pool"), "head", None),
        P(("groups", "pool"), None, "head", None),
        P(("groups", "pool"), None, "head", None, None),
        P("groups", None),
        P("groups"),
        P("groups"),
    )

    return jax.shard_map(
        on_device,
        mesh=mesh,
        in_specs=placed,
        out_specs=(
            P(("groups", "pool"), "head", None),
            P(("groups", "pool"), None, "head", None, None),
        ),
        check_vma=False,
    )
```
